256 devices in a mesh: clip: 128 (over z, y, x), mp: 2 (over core).
Axes of the slice: x: 4, y: 4, z: 8, core: 2. Of those that a mesh axis runs over, the one named last changes fastest.
Arguments:
- tokens: bfloat16 [384, 128, 1024], P('clip', None, 'mp'), may hold values from -6 to 6
- bottleneck: bfloat16 [128, 4, 1024], P('clip', None, 'mp'), may hold values from -6 to 6
- clip_lengths: int32 [128], replicated, may hold values from 2 to 4, as said below
- video_blocks: int32 [128], replicated, may hold values from 1 to 3, as said below
- store_map: int32 [128, 3], replicated, may hold values from -1 to 511, as said below
- norm1_gain: float32 [1024], replicated, may hold values from 0.4 to 1.6
- w_qkv: bfloat16 [3, 1024, 1024], P(None, None, 'mp'), may hold values from -0.625 to 0.625
- w_out: bfloat16 [1024, 1024], P('mp'), may hold values from -0.1875 to 0.1875
- norm2_gain: float32 [1024], replicated, may hold values from 0.4 to 1.6
- w_up: bfloat16 [1024, 4096], P(None, 'mp'), may hold values from -0.1875 to 0.1875
- w_down: bfloat16 [4096, 1024], P('mp'), may hold values from -0.09375 to 0.09375
Outputs:
- mixed_tokens: bfloat16 [384, 128, 1024], P('clip', None, 'mp')
- merged_bottleneck: bfloat16 [128, 4, 1024], P('clip', None, 'mp')
The draws below stay inside these ranges and needn't reach their ends.
Inputs may be any that keep to these rules, and one draw needn't show every extreme that they name: clip_lengths[c] counts the blocks of the clip owned by index c of clip. The first video_blocks[c] blocks of clip c are video, the others up to clip_lengths[c] audio; video_blocks[c] <= clip_lengths[c] - 1. store_map[d, s] = c * 4 + b when slot s of device d along clip holds block b of clip c, and -1 when the slot is empty; each block b < clip_lengths[c] of each clip sits in exactly one slot, on a device of the same aligned group of 4 devices along clip as c; no device holds two blocks of one clip.
All inputs are finite; a program needn't handle non-finite values.
Results may differ from the reference program's by a relative error of at most 0.006.
Values may be sent and summed in bfloat16 or wider, within the bound.
No kernel may reach another device: no remote copies, remote signals or barrier semaphores. Data moves between devices by JAX's collectives and lax.ppermute only.
A program may use at most 128 MiB of HBM per device.

```python
import jax
import jax.numpy as jnp
from jax import lax

D = 1024
HEADS = 16
FF = 4096
HEAD_DIM = 64
BLK = 128
NB = 4
SLOT_DEV = 4
STORE_DEV = 3
GROUP = 4
CLIPS = 128


def layout(key):
    groups = CLIPS // GROUP
    base = jax.random.fold_in(key, 11)
    keys = [jax.random.fold_in(base, index) for index in range(5)]
    spots = jnp.arange(GROUP, dtype=jnp.int32)
    first = jax.random.randint(keys[0], (groups, GROUP), 0, 1 << 20) * GROUP + spots
    order = jnp.argsort(first, axis=1).astype(jnp.int32)
    ranking = jnp.argsort(order, axis=1).astype(jnp.int32)
    longer = jax.random.randint(keys[1], (groups, GROUP), SLOT_DEV // 2 + 1, SLOT_DEV + 1)
    shorter = jax.random.randint(keys[2], (groups, GROUP), 2, SLOT_DEV // 2 + 1)
    lengths = jnp.where(ranking % 2 == 0, longer, shorter)
    lengths = jnp.where(ranking == 0, SLOT_DEV, lengths).astype(jnp.int32)
    video = (1 + jax.random.randint(keys[3], (groups, GROUP), 0, 1 << 20) % (lengths - 1)).astype(jnp.int32)
    by_rank = jnp.take_along_axis(lengths, order, axis=1)
    ends = jnp.cumsum(by_rank, axis=1).astype(jnp.int32)
    starts = ends - by_rank
    second = jax.random.randint(keys[4], (groups, GROUP), 0, 1 << 20) * GROUP + spots
    residue = jnp.argsort(jnp.argsort(second, axis=1), axis=1).astype(jnp.int32)
    slots = jnp.arange(STORE_DEV, dtype=jnp.int32)
    position = residue[:, :, None] + GROUP * slots[None, None, :]
    owner_rank = jnp.sum((ends[:, None, None, :] <= position[:, :, :, None]).astype(jnp.int32), axis=-1)
    live = owner_rank < GROUP
    safe = jnp.minimum(owner_rank, GROUP - 1).reshape(groups, GROUP * STORE_DEV)
    start_of = jnp.take_along_axis(starts, safe, axis=1).reshape(groups, GROUP, STORE_DEV)
    owner_spot = jnp.take_along_axis(order, safe, axis=1).reshape(groups, GROUP, STORE_DEV)
    owner = owner_spot + GROUP * jnp.arange(groups, dtype=jnp.int32)[:, None, None]
    entry = jnp.where(live, owner * SLOT_DEV + position - start_of, -1).astype(jnp.int32)
    return (lengths.reshape(CLIPS), video.reshape(CLIPS), entry.reshape(CLIPS, STORE_DEV))


def draw_clip_lengths(key, part):
    return layout(key)[0]


def draw_video_blocks(key, part):
    return layout(key)[1]


def draw_store_map(key, part):
    return layout(key)[2]


def draw_w_qkv(key, part):
    raw = jnp.clip(jax.random.normal(jax.random.fold_in(key, 3), (3, D, D), jnp.float32), -4.0, 4.0) * D ** (-0.5)
    return raw.astype(jnp.bfloat16)


def level_of(own_key, extent, cuts, low, high):
    level, own = 1.0, jax.random.fold_in(own_key, 6)
    for dim, shards_of in cuts:
        draws = jnp.exp(jax.random.uniform(jax.random.fold_in(own, dim), (shards_of,), jnp.float32, low / len(cuts), high / len(cuts)))
        level = level * jnp.repeat(draws, extent[dim] // shards_of).reshape([-1 if axis == dim else 1 for axis in range(len(extent))])
    return level


def gaussian(key, shape, deviation, most, shards=(), kind=jnp.bfloat16):
    drawn = deviation * jax.random.normal(key, shape, jnp.float32)
    if shards:
        drawn = drawn * level_of(key, shape, shards, -0.22, 0.18)
    return jnp.clip(drawn, -most, most).astype(kind)


def setup_inputs(seed: int = 0) -> dict:
    seeds = jax.random.split(jax.random.key(seed), 12)
    tokens = gaussian(seeds[0], (CLIPS * STORE_DEV, BLK, D), 1.0, 6.0, ((0, 128), (2, 2)))
    bottleneck = gaussian(seeds[1], (CLIPS, NB, D), 1.0, 6.0, ((0, 128), (2, 2)))
    clip_lengths = draw_clip_lengths(jax.random.fold_in(seeds[11], 71), 0)
    video_blocks = draw_video_blocks(jax.random.fold_in(seeds[11], 71), 0)
    store_map = draw_store_map(jax.random.fold_in(seeds[11], 71), 0)
    norm1_gain = jnp.clip(1.0 + 0.12 * jax.random.normal(seeds[5], (D,), jnp.float32), 0.4, 1.6)
    w_qkv = draw_w_qkv(jax.random.fold_in(seeds[11], 71), 0)
    w_out = gaussian(seeds[7], (D, D), D ** -0.5, 0.1875, ((0, 2),))
    norm2_gain = jnp.clip(1.0 + 0.12 * jax.random.normal(seeds[8], (D,), jnp.float32), 0.4, 1.6)
    w_up = gaussian(seeds[9], (D, FF), D ** -0.5, 0.1875, ((1, 2),))
    w_down = gaussian(seeds[10], (FF, D), FF ** -0.5, 0.09375, ((0, 2),))
    return {"tokens": tokens, "bottleneck": bottleneck, "clip_lengths": clip_lengths, "video_blocks": video_blocks, "store_map": store_map, "norm1_gain": norm1_gain, "w_qkv": w_qkv, "w_out": w_out, "norm2_gain": norm2_gain, "w_up": w_up, "w_down": w_down}


def layer_norm(rows, gain):
    mean = lax.optimization_barrier(jnp.mean(rows, axis=-1, keepdims=True))
    centred = rows - mean
    moment = lax.optimization_barrier(jnp.mean(centred * centred, axis=-1, keepdims=True))
    return centred * lax.rsqrt(moment + 1e-05) * gain.astype(jnp.float32)

def attend(scores, allowed, values):
    masked = jnp.where(allowed, scores, -1e+30)
    top = lax.optimization_barrier(jnp.max(masked, axis=-1, keepdims=True))
    weights = jnp.where(allowed, jnp.exp(masked - top), 0.0)
    weights = (weights / lax.optimization_barrier(jnp.sum(weights, axis=-1, keepdims=True))).astype(jnp.bfloat16)
    return jnp.dot(weights, values, preferred_element_type=jnp.float32)

def reference(tokens, bottleneck, clip_lengths, video_blocks, store_map, norm1_gain, w_qkv, w_out, norm2_gain, w_up, w_down):
    total_rows = SLOT_DEV * BLK
    flat_map = store_map.reshape(-1).astype(jnp.int32)
    target = jnp.where(flat_map >= 0, flat_map, CLIPS * SLOT_DEV).astype(jnp.int32)
    placed = jnp.zeros((CLIPS * SLOT_DEV, BLK, D), tokens.dtype).at[target].set(tokens, mode='drop')
    placed = placed.reshape(CLIPS, total_rows, D)

    def one_clip(items):
        clip_rows, extra, length, video = items
        rows = jnp.concatenate([clip_rows, extra], axis=0)
        normed = layer_norm(rows.astype(jnp.float32), norm1_gain).astype(jnp.bfloat16)
        query = jnp.dot(normed, w_qkv[0], preferred_element_type=jnp.float32).astype(jnp.bfloat16)
        keys = jnp.dot(normed, w_qkv[1], preferred_element_type=jnp.float32).astype(jnp.bfloat16)
        values = jnp.dot(normed, w_qkv[2], preferred_element_type=jnp.float32).astype(jnp.bfloat16)
        block_of = jnp.arange(total_rows, dtype=jnp.int32) // BLK
        token_mode = jnp.where(block_of < video, 0, jnp.where(block_of < length, 1, -1)).astype(jnp.int32)
        key_mode = jnp.concatenate([token_mode, jnp.full((NB,), 2, jnp.int32)])
        token_allow = (key_mode[None, :] == token_mode[:, None]) | (key_mode[None, :] == 2)
        video_allow = jnp.broadcast_to((key_mode == 0) | (key_mode == 2), (NB, total_rows + NB))
        audio_allow = jnp.broadcast_to((key_mode == 1) | (key_mode == 2), (NB, total_rows + NB))
        pieces = []
        for head in range(HEADS):
            cols = slice(head * HEAD_DIM, (head + 1) * HEAD_DIM)
            scores = lax.dot_general(query[:, cols], keys[:, cols], (((1,), (1,)), ((), ())), preferred_element_type=jnp.float32)
            scores = scores * HEAD_DIM ** (-0.5)
            own = attend(scores[:total_rows], token_allow, values[:, cols])
            seen_video = attend(scores[total_rows:], video_allow, values[:, cols])
            seen_audio = attend(scores[total_rows:], audio_allow, values[:, cols])
            pieces.append(jnp.concatenate([own, 0.5 * (seen_video + seen_audio)], axis=0))
        context = jnp.concatenate(pieces, axis=1).astype(jnp.bfloat16)
        after = (rows.astype(jnp.float32) + jnp.dot(context, w_out, preferred_element_type=jnp.float32)).astype(jnp.bfloat16)
        normed2 = layer_norm(after.astype(jnp.float32), norm2_gain).astype(jnp.bfloat16)
        active = jax.nn.gelu(jnp.dot(normed2, w_up, preferred_element_type=jnp.float32), approximate=True).astype(jnp.bfloat16)
        merged = (after.astype(jnp.float32) + jnp.dot(active, w_down, preferred_element_type=jnp.float32)).astype(jnp.bfloat16)
        return (merged[:total_rows], merged[total_rows:])
    merged_rows, merged_extra = lax.map(one_clip, (placed, bottleneck, clip_lengths, video_blocks))
    merged_rows = merged_rows.reshape(CLIPS * SLOT_DEV, BLK, D)
    picked = merged_rows[jnp.maximum(flat_map, 0)]
    mixed_tokens = jnp.where(flat_map[:, None, None] >= 0, picked, jnp.zeros_like(picked))
    return (mixed_tokens, merged_extra)
```

```python
import functools

import jax
import jax.numpy as jnp
from jax import lax
from jax.experimental import pallas as pl
from jax.experimental.pallas import tpu as pltpu
from jax.sharding import PartitionSpec as P

HEAD_DIM = 64
BLK = 128
NB = 4
SLOT_DEV = 4
STORE_DEV = 3
GROUP = 4
PAD = 16
STORED = STORE_DEV * BLK
ROWS = STORED + PAD
CLIP_ROWS = SLOT_DEV * BLK
BF16 = jnp.bfloat16
F32 = jnp.float32

VMEM = pl.BlockSpec(memory_space=pltpu.VMEM)
SMEM = pl.BlockSpec(memory_space=pltpu.SMEM)


def spec(shape, dtype=BF16):
    return jax.ShapeDtypeStruct(shape, dtype)


def partner(x, step):
    return lax.ppermute(x, "clip", [(i, i ^ step) for i in range(lax.axis_size("clip"))])


def slot_for(store_map, device, owner):
    slot = jnp.int32(-1)
    block = jnp.int32(-1)
    for s in range(STORE_DEV):
        entry = store_map[device, s]
        hit = (entry >= 0) & (entry // SLOT_DEV == owner)
        slot = jnp.where(hit, s, slot)
        block = jnp.where(hit, entry % SLOT_DEV, block)
    return slot, block


def norm_into(x0, x1, gain, out, at, rows):
    half = x0.shape[1]
    x0 = x0.astype(F32)
    x1 = x1.astype(F32)
    scale = 1.0 / (2 * half)
    mean = (jnp.sum(x0, axis=-1, keepdims=True) + jnp.sum(x1, axis=-1, keepdims=True)) * scale
    x0 = x0 - mean
    x1 = x1 - mean
    moment = (
        jnp.sum(x0 * x0, axis=-1, keepdims=True) + jnp.sum(x1 * x1, axis=-1, keepdims=True)
    ) * scale
    inv = lax.rsqrt(moment + 1e-05)
    out[pl.ds(at, rows), :half] = (x0 * inv * gain[:, :half]).astype(BF16)
    out[pl.ds(at, rows), half:] = (x1 * inv * gain[:, half:]).astype(BF16)


def pack_kernel(store_map, tokens, extra, near, across, far, stored):
    member = lax.axis_index("clip")
    for step, out in ((1, near), (3, across), (2, far)):
        slot, _ = slot_for(store_map, member, member ^ step)

        @pl.when(slot >= 0)
        def _():
            out[...] = tokens[jnp.maximum(slot, 0)]

        @pl.when(slot < 0)
        def _():
            out[...] = jnp.zeros_like(out)

    for s in range(STORE_DEV):
        stored[s * BLK : (s + 1) * BLK, :] = tokens[s]
    width = stored.shape[1]
    stored[STORED:, :] = jnp.concatenate(
        [extra[0].astype(F32), jnp.zeros((PAD - NB, width), F32)], axis=0
    ).astype(BF16)


def attend_kernel(
    store_map,
    lengths,
    videos,
    stored,
    arrived,
    gain,
    w_qkv,
    near,
    across,
    far,
    own,
    normed,
    query,
    keys,
    values,
    context,
):
    member = lax.axis_index("clip")
    length = lengths[member]
    video = videos[member]
    width = query.shape[1]
    gains = gain[...]
    sources = []
    for step in range(GROUP):
        sources.append(slot_for(store_map, member ^ step, member))
    source_of = []
    for b in range(SLOT_DEV):
        source = jnp.int32(-1)
        for step in range(GROUP):
            source = jnp.where(sources[step][1] == b, step, source)
        source_of.append(source)
    own_slot = sources[0][0]
    place = {1: 0, 3: 1, 2: 2}

    for b in range(SLOT_DEV):
        source = source_of[b]
        at = jnp.where(source == 1, place[1], jnp.where(source == 3, place[3], place[2]))
        at = pl.multiple_of(at * BLK, BLK)
        here = pl.multiple_of(jnp.maximum(own_slot, 0) * BLK, BLK)

        @pl.when(source == 0)
        def _():
            norm_into(
                stored[0, pl.ds(here, BLK), :], stored[1, pl.ds(here, BLK), :], gains, normed, b * BLK, BLK
            )

        @pl.when(source > 0)
        def _():
            norm_into(
                arrived[0, pl.ds(at, BLK), :], arrived[1, pl.ds(at, BLK), :], gains, normed, b * BLK, BLK
            )

        @pl.when(source < 0)
        def _():
            normed[b * BLK : (b + 1) * BLK, :] = jnp.zeros((BLK, normed.shape[1]), BF16)

    norm_into(stored[0, STORED:, :], stored[1, STORED:, :], gains, normed, CLIP_ROWS, PAD)

    tile = 256
    for which, out in ((0, query), (1, keys), (2, values)):
        for j in range(0, width, tile):
            got = jnp.dot(normed[...], w_qkv[which, :, j : j + tile], preferred_element_type=F32)
            if which == 0:
                got = got * HEAD_DIM ** (-0.5)
            out[: CLIP_ROWS + PAD, j : j + tile] = got.astype(BF16)
    for out in (keys, values):
        out[CLIP_ROWS + PAD :, :] = jnp.zeros((BLK - PAD, width), BF16)
    context[...] = jnp.zeros_like(context)

    lane = lax.broadcasted_iota(jnp.int32, (BLK, BLK), 1)
    low = lane < HEAD_DIM
    lane2 = lax.broadcasted_iota(jnp.int32, (2 * BLK, BLK), 1)
    nt = (((1,), (1,)), ((), ()))

    def token_block(b, first, count, source):
        start = pl.multiple_of(first * BLK, BLK)
        at = pl.multiple_of(b * BLK, BLK)
        for p in range(width // BLK):
            cols = slice(p * BLK, (p + 1) * BLK)
            q = query[pl.ds(at, BLK), cols]
            both = jnp.concatenate(
                [jnp.where(low, q, jnp.zeros_like(q)), jnp.where(low, jnp.zeros_like(q), q)], axis=0
            )
            seen = keys[pl.ds(start, count * BLK), cols]
            s = lax.dot_general(both, seen, nt, preferred_element_type=F32)
            se = lax.dot_general(both, keys[CLIP_ROWS:, cols], nt, preferred_element_type=F32)
            se = jnp.where(lane2 < NB, se, -1e30)
            top = se
            for k in range(count):
                top = jnp.maximum(top, s[:, k * BLK : (k + 1) * BLK])
            top = jnp.max(top, axis=-1, keepdims=True)
            e = jnp.exp(s - top).astype(BF16)
            ee = jnp.exp(se - top).astype(BF16)
            v = values[pl.ds(start, count * BLK), cols]
            v = jnp.concatenate([v, jnp.ones_like(v)], axis=1)
            ve = values[CLIP_ROWS:, cols]
            ve = jnp.concatenate([ve, jnp.ones_like(ve)], axis=1)
            o = jnp.dot(e, v, preferred_element_type=F32) + jnp.dot(ee, ve, preferred_element_type=F32)
            top_part = jnp.where(low, o[:BLK, :BLK], o[BLK:, :BLK])
            total = jnp.where(low, o[:BLK, BLK:], o[BLK:, BLK:])
            context[source, :, cols] = (top_part / total).astype(BF16)

    for b in range(SLOT_DEV):
        is_video = b < video
        first = jnp.where(is_video, 0, video)
        seen = jnp.where(is_video, video, length - video)
        for count in range(1, SLOT_DEV):

            @pl.when((b < length) & (seen == count))
            def _():
                token_block(b, first, count, jnp.maximum(source_of[b], 0))

    heads = width // HEAD_DIM
    sub = 8
    qe = query[CLIP_ROWS : CLIP_ROWS + PAD, :].astype(F32)[:sub]
    qe = jnp.concatenate([qe] * heads, axis=0)
    row_head = lax.broadcasted_iota(jnp.int32, (heads * sub, width), 0) // sub
    col_head = lax.broadcasted_iota(jnp.int32, (heads * sub, width), 1) // HEAD_DIM
    mine = row_head == col_head
    qe = jnp.where(mine, qe, 0.0).astype(BF16)
    s = lax.dot_general(qe, keys[...], nt, preferred_element_type=F32)
    col = lax.broadcasted_iota(jnp.int32, s.shape, 1)
    bottle = (col >= CLIP_ROWS) & (col < CLIP_ROWS + NB)
    parts = []
    for allowed in (
        bottle | (col < video * BLK),
        bottle | ((col >= video * BLK) & (col < length * BLK)),
    ):
        masked = jnp.where(allowed, s, -1e30)
        e = jnp.exp(masked - jnp.max(masked, axis=-1, keepdims=True))
        parts.append((e / jnp.sum(e, axis=-1, keepdims=True)).astype(BF16))
    o = jnp.dot(jnp.concatenate(parts, axis=0), values[...], preferred_element_type=F32)
    o = 0.5 * (o[: heads * sub] + o[heads * sub :])
    o = jnp.where(mine, o, 0.0)
    total = o[:sub]
    for h in range(1, heads):
        total = total + o[h * sub : (h + 1) * sub]
    own[BLK:, :] = jnp.concatenate([total, jnp.zeros_like(total)], axis=0).astype(BF16)
    own[:BLK, :] = context[0]
    near[...] = context[1]
    far[...] = context[2]
    across[...] = context[3]


def feed_kernel(
    store_map,
    stored,
    own,
    arrived,
    w_out,
    gain,
    w_up,
    w_down,
    base,
    send,
    context,
    after,
    normed,
    active,
):
    member = lax.axis_index("clip")
    core = lax.axis_index("mp")
    half = base.shape[1]
    for s in range(STORE_DEV):
        entry = store_map[member, s]
        step = jnp.where(entry >= 0, (entry // SLOT_DEV) ^ member, -1)
        at = jnp.where(step == 1, 0, jnp.where(step == 3, 1, 2))
        at = pl.multiple_of(at * BLK, BLK)
        rows = slice(s * BLK, (s + 1) * BLK)

        @pl.when(step == 0)
        def _():
            context[rows, :half] = own[0, :BLK, :]
            context[rows, half:] = own[1, :BLK, :]

        @pl.when(step > 0)
        def _():
            context[rows, :half] = arrived[0, pl.ds(at, BLK), :]
            context[rows, half:] = arrived[1, pl.ds(at, BLK), :]

        @pl.when(step < 0)
        def _():
            context[rows, :] = jnp.zeros((BLK, 2 * half), BF16)

    context[STORED:, :half] = own[0, BLK:, :]
    context[STORED:, half:] = own[1, BLK:, :]

    tile = 256
    for j in range(0, 2 * half, tile):
        got = jnp.dot(context[:, :half], w_out[0, :, j : j + tile], preferred_element_type=F32)
        got = got + jnp.dot(context[:, half:], w_out[1, :, j : j + tile], preferred_element_type=F32)
        side, off = divmod(j, half)
        got = got + stored[side, :, off : off + tile].astype(F32)
        after[:, j : j + tile] = got.astype(BF16)
    gains = gain[...]
    for r in range(0, ROWS, 80):
        norm_into(after[r : r + 80, :half], after[r : r + 80, half:], gains, normed, r, 80)
    hidden = w_up.shape[1]
    for j in range(0, hidden, tile):
        got = jnp.dot(normed[...], w_up[:, j : j + tile], preferred_element_type=F32)
        active[:, j : j + tile] = jax.nn.gelu(got, approximate=True).astype(BF16)
    for j in range(0, half, tile):
        mine = pl.multiple_of(core * half + j, tile)
        other = pl.multiple_of((1 - core) * half + j, tile)
        got = jnp.dot(active[...], w_down[:, pl.ds(other, tile)], preferred_element_type=F32)
        send[:, j : j + tile] = got.astype(BF16)
        got = jnp.dot(active[...], w_down[:, pl.ds(mine, tile)], preferred_element_type=F32)
        base[:, j : j + tile] = got + after[:, pl.ds(mine, tile)].astype(F32)


def finish_kernel(store_map, base, sums, mixed, merged):
    member = lax.axis_index("clip")
    core = lax.axis_index("mp")
    other = 1 - core
    for s in range(STORE_DEV):
        rows = slice(s * BLK, (s + 1) * BLK)
        got = base[rows, :] + sums[other, rows, :].astype(F32)
        keep = store_map[member, s] >= 0
        mixed[s] = jnp.where(keep, got, 0.0).astype(BF16)
    got = base[STORED:, :] + sums[other, STORED:, :].astype(F32)
    merged[0] = got[:NB].astype(BF16)


def body(
    tokens,
    bottleneck,
    clip_lengths,
    video_blocks,
    store_map,
    norm1_gain,
    w_qkv,
    w_out,
    norm2_gain,
    w_up,
    w_down,
):
    width = tokens.shape[2]
    model = 2 * width
    heads_width = w_qkv.shape[2]
    hidden = w_up.shape[1]
    gain1 = norm1_gain.reshape(1, model)
    gain2 = norm2_gain.reshape(1, model)
    block = spec((BLK, width))
    w_out_all = lax.all_gather(w_out, "mp", axis=0)

    near, across, far, stored = pl.pallas_call(
        pack_kernel,
        name="pack",
        out_shape=(block, block, block, spec((ROWS, width))),
        in_specs=[SMEM, VMEM, VMEM],
        out_specs=(VMEM,) * 4,
    )(store_map, tokens, bottleneck)
    across = partner(across, 3)
    near = partner(near, 1)
    far = partner(far, 2)
    stored_all = lax.all_gather(stored, "mp", axis=0)
    arrived = lax.all_gather(jnp.concatenate([near, across, far], axis=0), "mp", axis=0)

    near, across, far, own = pl.pallas_call(
        attend_kernel,
        name="attend",
        out_shape=(block, block, block, spec((BLK + PAD, width))),
        in_specs=[SMEM, SMEM, SMEM, VMEM, VMEM, VMEM, VMEM],
        out_specs=(VMEM,) * 4,
        scratch_shapes=[
            pltpu.VMEM((CLIP_ROWS + PAD, model), BF16),
            pltpu.VMEM((CLIP_ROWS + BLK, heads_width), BF16),
            pltpu.VMEM((CLIP_ROWS + BLK, heads_width), BF16),
            pltpu.VMEM((CLIP_ROWS + BLK, heads_width), BF16),
            pltpu.VMEM((GROUP, BLK, heads_width), BF16),
        ],
        compiler_params=pltpu.CompilerParams(vmem_limit_bytes=24 << 20),
        cost_estimate=pl.CostEstimate(flops=2500000000, bytes_accessed=6000000, transcendentals=3000000),
    )(store_map, clip_lengths, video_blocks, stored_all, arrived, gain1, w_qkv)
    across = partner(across, 3)
    near = partner(near, 1)
    far = partner(far, 2)
    own_all = lax.all_gather(own, "mp", axis=0)
    arrived = lax.all_gather(jnp.concatenate([near, across, far], axis=0), "mp", axis=0)

    base, send = pl.pallas_call(
        feed_kernel,
        name="feed",
        out_shape=(spec((ROWS, width), F32), spec((ROWS, width))),
        in_specs=[SMEM] + [VMEM] * 7,
        out_specs=(VMEM,) * 2,
        scratch_shapes=[
            pltpu.VMEM((ROWS, model), BF16),
            pltpu.VMEM((ROWS, model), BF16),
            pltpu.VMEM((ROWS, model), BF16),
            pltpu.VMEM((ROWS, hidden), BF16),
        ],
        compiler_params=pltpu.CompilerParams(vmem_limit_bytes=32 << 20),
        cost_estimate=pl.CostEstimate(flops=4100000000, bytes_accessed=14000000, transcendentals=820000),
    )(store_map, stored_all, own_all, arrived, w_out_all, gain2, w_up, w_down)
    sums = lax.all_gather(send, "mp", axis=0)

    mixed, merged = pl.pallas_call(
        finish_kernel,
        name="finish",
        out_shape=(spec(tokens.shape), spec(bottleneck.shape)),
        in_specs=[SMEM, VMEM, VMEM],
        out_specs=(VMEM,) * 2,
    )(store_map, base, sums)
    return mixed, merged


def solution(mesh):
    placed = (
        P("clip", None, "mp"),
        P("clip", None, "mp"),
        P(),
        P(),
        P(),
        P(),
        P(None, None, "mp"),
        P("mp", None),
        P(),
        P(None, "mp"),
        P("mp", None),
    )
    return jax.shard_map(
        body,
        mesh=mesh,
        in_specs=placed,
        out_specs=(P("clip", None, "mp"), P("clip", None, "mp")),
        check_vma=False,
    )
```

```python
import jax
import jax.numpy as jnp
from jax import lax
from jax.experimental import pallas as pl
from jax.experimental.pallas import tpu as pltpu
from jax.sharding import PartitionSpec as P

HEAD_DIM = 64
BLK = 128
NB = 4
SLOT_DEV = 4
STORE_DEV = 3
GROUP = 4
PAD = 16
STORED = STORE_DEV * BLK
ROWS = STORED + PAD
CLIP_ROWS = SLOT_DEV * BLK
BF16 = jnp.bfloat16
F32 = jnp.float32

VMEM = pl.BlockSpec(memory_space=pltpu.VMEM)
HBM = pl.BlockSpec(memory_space=pltpu.HBM)
DMA = pltpu.SemaphoreType.DMA
SMEM = pl.BlockSpec(memory_space=pltpu.SMEM)


def spec(shape, dtype=BF16):
    return jax.ShapeDtypeStruct(shape, dtype)


def partner(x, step):
    return lax.ppermute(x, "clip", [(i, i ^ step) for i in range(lax.axis_size("clip"))])


def slot_for(store_map, device, owner):
    slot = jnp.int32(-1)
    block = jnp.int32(-1)
    for s in range(STORE_DEV):
        entry = store_map[s, device]
        hit = (entry >= 0) & (entry // SLOT_DEV == owner)
        slot = jnp.where(hit, s, slot)
        block = jnp.where(hit, entry % SLOT_DEV, block)
    return slot, block


def norm_into(x0, x1, gain, out, at, rows):
    half = x0.shape[1]
    x0 = x0.astype(F32)
    x1 = x1.astype(F32)
    scale = 1.0 / (2 * half)
    mean = (jnp.sum(x0, axis=-1, keepdims=True) + jnp.sum(x1, axis=-1, keepdims=True)) * scale
    x0 = x0 - mean
    x1 = x1 - mean
    moment = (
        jnp.sum(x0 * x0, axis=-1, keepdims=True) + jnp.sum(x1 * x1, axis=-1, keepdims=True)
    ) * scale
    inv = lax.rsqrt(moment + 1e-05)
    out[pl.ds(at, rows), :half] = (x0 * inv * gain[:, :half]).astype(BF16)
    out[pl.ds(at, rows), half:] = (x1 * inv * gain[:, half:]).astype(BF16)


def pack_kernel(slots, tokens, extra, near, across, far, stored, store_map, few, tail, sems):
    member = lax.axis_index("clip")
    load_map = pltpu.make_async_copy(slots, store_map, sems.at[0])
    load_few = pltpu.make_async_copy(extra, few, sems.at[1])
    load_map.start()
    load_few.start()
    copies = [
        pltpu.make_async_copy(tokens.at[s], stored.at[pl.ds(s * BLK, BLK), :], sems.at[2 + s])
        for s in range(STORE_DEV)
    ]
    load_map.wait()
    for k, (step, out) in enumerate(((1, near), (3, across), (2, far))):
        slot, _ = slot_for(store_map, member, member ^ step)
        copies.append(
            pltpu.make_async_copy(tokens.at[jnp.maximum(slot, 0)], out, sems.at[2 + STORE_DEV + k])
        )
    for copy in copies:
        copy.start()
    load_few.wait()
    width = stored.shape[1]
    tail[...] = jnp.concatenate(
        [few[0].astype(F32), jnp.zeros((PAD - NB, width), F32)], axis=0
    ).astype(BF16)
    last = pltpu.make_async_copy(tail, stored.at[pl.ds(STORED, PAD), :], sems.at[2 + 2 * STORE_DEV])
    last.start()
    for copy in copies + [last]:
        copy.wait()


def attend_kernel(
    slots,
    all_lengths,
    all_videos,
    stored,
    arrived,
    gain_in,
    w_qkv,
    near,
    across,
    far,
    own,
    normed,
    query,
    keys,
    values,
    context,
    weights,
    gain,
    store_map,
    lengths,
    videos,
    sems,
):
    member = lax.axis_index("clip")
    small = [
        pltpu.make_async_copy(x, y, sems.at[i])
        for i, (x, y) in enumerate(
            ((gain_in, gain), (slots, store_map), (all_lengths, lengths), (all_videos, videos))
        )
    ]
    loads = [pltpu.make_async_copy(w_qkv.at[i], weights.at[i], sems.at[4 + i]) for i in range(3)]
    for load in small + loads:
        load.start()
    width = query.shape[1]
    for load in small:
        load.wait()
    gains = gain[...]
    for k in range(GROUP - 1):
        rows = slice(k * BLK, (k + 1) * BLK)
        norm_into(arrived[0, rows, :], arrived[1, rows, :], gains, normed, k * BLK, BLK)
    norm_into(stored[0, STORED:, :], stored[1, STORED:, :], gains, normed, CLIP_ROWS, PAD)

    length = lengths[member]
    video = videos[member]
    own_slot, own_block = slot_for(store_map, member, member)
    here = pl.multiple_of(jnp.maximum(own_slot, 0) * BLK, BLK)
    norm_into(
        stored[0, pl.ds(here, BLK), :],
        stored[1, pl.ds(here, BLK), :],
        gains,
        normed,
        (GROUP - 1) * BLK,
        BLK,
    )
    block_at = [slot_for(store_map, member ^ step, member)[1] for step in (1, 3, 2)] + [own_block]
    source_of = []
    for b in range(SLOT_DEV):
        source = jnp.int32(0)
        for place, block in enumerate(block_at):
            source = jnp.where(block == b, place, source)
        source_of.append(source)
    row_at = [
        pl.multiple_of(jnp.where(block < 0, SLOT_DEV + 1, block) * BLK, BLK) for block in block_at
    ]

    tile = 256
    for which, out in ((0, query), (1, keys), (2, values)):
        loads[which].wait()
        for j in range(0, width, tile):
            got = jnp.dot(normed[...], weights[which, :, j : j + tile], preferred_element_type=F32)
            if which == 0:
                got = got * HEAD_DIM ** (-0.5)
            got = got.astype(BF16)
            for place in range(GROUP):
                out[pl.ds(row_at[place], BLK), j : j + tile] = got[place * BLK : (place + 1) * BLK]
            out[CLIP_ROWS : CLIP_ROWS + PAD, j : j + tile] = got[CLIP_ROWS:]
    for out in (keys, values):
        out[CLIP_ROWS + PAD : CLIP_ROWS + BLK, :] = jnp.zeros((BLK - PAD, width), BF16)
    for b in range(2, SLOT_DEV):

        @pl.when(b >= length)
        def _():
            values[b * BLK : (b + 1) * BLK, :] = jnp.zeros((BLK, width), BF16)

    context[...] = jnp.zeros_like(context)

    lane = lax.broadcasted_iota(jnp.int32, (BLK, BLK), 1)
    low = lane < HEAD_DIM
    lane2 = lax.broadcasted_iota(jnp.int32, (2 * BLK, BLK), 1)
    nt = (((1,), (1,)), ((), ()))

    def token_block(b, first, count, source):
        start = pl.multiple_of(first * BLK, BLK)
        at = pl.multiple_of(b * BLK, BLK)
        for p in range(width // BLK):
            cols = slice(p * BLK, (p + 1) * BLK)
            q = query[pl.ds(at, BLK), cols]
            both = jnp.concatenate(
                [jnp.where(low, q, jnp.zeros_like(q)), jnp.where(low, jnp.zeros_like(q), q)], axis=0
            )
            seen = keys[pl.ds(start, count * BLK), cols]
            s = lax.dot_general(both, seen, nt, preferred_element_type=F32)
            se = lax.dot_general(both, keys[CLIP_ROWS : CLIP_ROWS + BLK, cols], nt, preferred_element_type=F32)
            se = jnp.where(lane2 < NB, se, -1e30)
            top = se
            for k in range(count):
                top = jnp.maximum(top, s[:, k * BLK : (k + 1) * BLK])
            top = jnp.max(top, axis=-1, keepdims=True)
            e = jnp.exp(s - top).astype(BF16)
            ee = jnp.exp(se - top).astype(BF16)
            v = values[pl.ds(start, count * BLK), cols]
            v = jnp.concatenate([v, jnp.ones_like(v)], axis=1)
            ve = values[CLIP_ROWS : CLIP_ROWS + BLK, cols]
            ve = jnp.concatenate([ve, jnp.ones_like(ve)], axis=1)
            o = jnp.dot(e, v, preferred_element_type=F32) + jnp.dot(ee, ve, preferred_element_type=F32)
            top_part = jnp.where(low, o[:BLK, :BLK], o[BLK:, :BLK])
            total = jnp.where(low, o[:BLK, BLK:], o[BLK:, BLK:])
            context[source, :, cols] = (top_part / total).astype(BF16)

    for b in range(SLOT_DEV):
        is_video = b < video
        first = jnp.where(is_video, 0, video)
        seen = jnp.where(is_video, video, length - video)
        for count in range(1, SLOT_DEV):

            @pl.when((b < length) & (seen == count))
            def _():
                token_block(b, first, count, source_of[b])

    heads = width // HEAD_DIM
    sub = 8
    qe = query[CLIP_ROWS : CLIP_ROWS + PAD, :].astype(F32)[:sub]
    qe = jnp.concatenate([qe] * heads, axis=0)
    row_head = lax.broadcasted_iota(jnp.int32, (heads * sub, width), 0) // sub
    col_head = lax.broadcasted_iota(jnp.int32, (heads * sub, width), 1) // HEAD_DIM
    mine = row_head == col_head
    qe = jnp.where(mine, qe, 0.0).astype(BF16)
    s = lax.dot_general(qe, keys[: CLIP_ROWS + BLK, :], nt, preferred_element_type=F32)
    col = lax.broadcasted_iota(jnp.int32, s.shape, 1)
    bottle = (col >= CLIP_ROWS) & (col < CLIP_ROWS + NB)
    parts = []
    for allowed in (
        bottle | (col < video * BLK),
        bottle | ((col >= video * BLK) & (col < length * BLK)),
    ):
        masked = jnp.where(allowed, s, -1e30)
        e = jnp.exp(masked - jnp.max(masked, axis=-1, keepdims=True))
        parts.append((e / jnp.sum(e, axis=-1, keepdims=True)).astype(BF16))
    o = jnp.dot(jnp.concatenate(parts, axis=0), values[: CLIP_ROWS + BLK, :], preferred_element_type=F32)
    o = 0.5 * (o[: heads * sub] + o[heads * sub :])
    o = jnp.where(mine, o, 0.0)
    total = o[:sub]
    for h in range(1, heads):
        total = total + o[h * sub : (h + 1) * sub]
    own[BLK:, :] = jnp.concatenate([total, jnp.zeros_like(total)], axis=0).astype(BF16)
    near[...] = context[0]
    across[...] = context[1]
    far[...] = context[2]
    own[:BLK, :] = context[3]


def feed_kernel(
    store_map,
    stored,
    own,
    arrived,
    w_out,
    w_out_other,
    gain,
    w_up,
    w_down,
    base,
    send,
    context,
    after,
    normed,
    active,
    outs,
    ups,
    downs,
    sems,
):
    member = lax.axis_index("clip")
    core = lax.axis_index("mp")
    half = base.shape[1]
    hidden = w_up.shape[1]
    loads_out = [
        pltpu.make_async_copy(w_out, outs.at[0], sems.at[0]),
        pltpu.make_async_copy(w_out_other, outs.at[1], sems.at[1]),
    ]
    part = 512
    loads_up = [
        pltpu.make_async_copy(
            w_up.at[:, pl.ds(k * part, part)], ups.at[:, pl.ds(k * part, part)], sems.at[2 + k]
        )
        for k in range(hidden // part)
    ]
    loads_down = []
    for k, side in enumerate((1 - core, core)):
        loads_down.append(
            pltpu.make_async_copy(
                w_down.at[:, pl.ds(pl.multiple_of(side * half, half), half)],
                downs.at[k],
                sems.at[2 + hidden // part + k],
            )
        )
    for load in loads_out + loads_up + loads_down:
        load.start()
    sides = (core, 1 - core)
    for s in range(STORE_DEV):
        entry = store_map[s, member]
        step = jnp.where(entry >= 0, (entry // SLOT_DEV) ^ member, -1)
        at = jnp.where(step == 1, 0, jnp.where(step == 3, 1, 2))
        at = pl.multiple_of(at * BLK, BLK)
        rows = slice(s * BLK, (s + 1) * BLK)

        @pl.when(step == 0)
        def _():
            for k in range(2):
                context[k, rows, :] = own[sides[k], :BLK, :]

        @pl.when(step > 0)
        def _():
            for k in range(2):
                context[k, rows, :] = arrived[sides[k], pl.ds(at, BLK), :]

        @pl.when(step < 0)
        def _():
            for k in range(2):
                context[k, rows, :] = jnp.zeros((BLK, half), BF16)

    for k in range(2):
        context[k, STORED:, :] = own[sides[k], BLK:, :]

    tile = 256
    for load in loads_out:
        load.wait()
    for j in range(0, 2 * half, tile):
        got = jnp.dot(context[0], outs[0, :, j : j + tile], preferred_element_type=F32)
        got = got + jnp.dot(context[1], outs[1, :, j : j + tile], preferred_element_type=F32)
        side, off = divmod(j, half)
        got = got + stored[side, :, off : off + tile].astype(F32)
        after[:, j : j + tile] = got.astype(BF16)
    gains = gain[...]
    for r in range(0, ROWS, 80):
        norm_into(after[r : r + 80, :half], after[r : r + 80, half:], gains, normed, r, 80)
    for k, load in enumerate(loads_up):
        load.wait()
        for j in range(k * part, (k + 1) * part, tile):
            got = jnp.dot(normed[...], ups[:, j : j + tile], preferred_element_type=F32)
            active[:, j : j + tile] = jax.nn.gelu(got, approximate=True).astype(BF16)
    loads_down[0].wait()
    for j in range(0, half, tile):
        got = jnp.dot(active[...], downs[0, :, j : j + tile], preferred_element_type=F32)
        send[:, j : j + tile] = got.astype(BF16)
    loads_down[1].wait()
    for j in range(0, half, tile):
        mine = pl.multiple_of(core * half + j, tile)
        got = jnp.dot(active[...], downs[1, :, j : j + tile], preferred_element_type=F32)
        base[:, j : j + tile] = got + after[:, pl.ds(mine, tile)].astype(F32)


def finish_kernel(store_map, base, sums, mixed, merged):
    member = lax.axis_index("clip")
    core = lax.axis_index("mp")
    other = 1 - core
    for s in range(STORE_DEV):
        rows = slice(s * BLK, (s + 1) * BLK)
        got = base[rows, :] + sums[other, rows, :].astype(F32)
        keep = store_map[s, member] >= 0
        mixed[s] = jnp.where(keep, got, 0.0).astype(BF16)
    got = base[STORED:, :] + sums[other, STORED:, :].astype(F32)
    merged[0] = got[:NB].astype(BF16)


def body(
    tokens,
    bottleneck,
    clip_lengths,
    video_blocks,
    store_map,
    norm1_gain,
    w_qkv,
    w_out,
    norm2_gain,
    w_up,
    w_down,
):
    width = tokens.shape[2]
    model = 2 * width
    heads_width = w_qkv.shape[2]
    hidden = w_up.shape[1]
    gain1 = norm1_gain.reshape(1, model)
    gain2 = norm2_gain.reshape(1, model)
    block = spec((BLK, width))
    w_out_other = lax.ppermute(w_out, "mp", [(0, 1), (1, 0)])
    slots = store_map.T
    stay = lambda x: pltpu.with_memory_space_constraint(x, pltpu.HBM)

    near, across, far, stored = pl.pallas_call(
        pack_kernel,
        name="pack",
        out_shape=(block, block, block, spec((ROWS, width))),
        in_specs=[HBM, HBM, HBM],
        out_specs=(HBM,) * 4,
        scratch_shapes=[
            pltpu.SMEM(slots.shape, jnp.int32),
            pltpu.VMEM(bottleneck.shape, BF16),
            pltpu.VMEM((PAD, width), BF16),
            DMA((2 * STORE_DEV + 3,)),
        ],
        compiler_params=pltpu.CompilerParams(vmem_limit_bytes=4 << 20),
    )(stay(slots), stay(tokens), stay(bottleneck))
    across = partner(across, 3)
    near = partner(near, 1)
    far = partner(far, 2)
    stored_all = lax.all_gather(stored, "mp", axis=0)
    arrived = lax.all_gather(jnp.concatenate([near, across, far], axis=0), "mp", axis=0)

    near, across, far, own = pl.pallas_call(
        attend_kernel,
        name="attend",
        out_shape=(block, block, block, spec((BLK + PAD, width))),
        in_specs=[HBM, HBM, HBM, VMEM, VMEM, HBM, HBM],
        out_specs=(VMEM,) * 4,
        scratch_shapes=[
            pltpu.VMEM((CLIP_ROWS + PAD, model), BF16),
            pltpu.VMEM((CLIP_ROWS + 2 * BLK, heads_width), BF16),
            pltpu.VMEM((CLIP_ROWS + 2 * BLK, heads_width), BF16),
            pltpu.VMEM((CLIP_ROWS + 2 * BLK, heads_width), BF16),
            pltpu.VMEM((GROUP, BLK, heads_width), BF16),
            pltpu.VMEM(w_qkv.shape, BF16),
            pltpu.VMEM((1, model), F32),
            pltpu.SMEM(slots.shape, jnp.int32),
            pltpu.SMEM(clip_lengths.shape, jnp.int32),
            pltpu.SMEM(video_blocks.shape, jnp.int32),
            DMA((7,)),
        ],
        compiler_params=pltpu.CompilerParams(vmem_limit_bytes=24 << 20),
        cost_estimate=pl.CostEstimate(flops=2500000000, bytes_accessed=6000000, transcendentals=3000000),
    )(
        stay(slots),
        stay(clip_lengths),
        stay(video_blocks),
        stored_all,
        arrived,
        stay(gain1),
        stay(w_qkv),
    )
    across = partner(across, 3)
    near = partner(near, 1)
    far = partner(far, 2)
    own_all = lax.all_gather(own, "mp", axis=0)
    arrived = lax.all_gather(jnp.concatenate([near, across, far], axis=0), "mp", axis=0)

    base, send = pl.pallas_call(
        feed_kernel,
        name="feed",
        out_shape=(spec((ROWS, width), F32), spec((ROWS, width))),
        in_specs=[SMEM, VMEM, VMEM, VMEM, HBM, HBM, VMEM, HBM, HBM],
        out_specs=(VMEM,) * 2,
        scratch_shapes=[
            pltpu.VMEM((2, ROWS, width), BF16),
            pltpu.VMEM((ROWS, model), BF16),
            pltpu.VMEM((ROWS, model), BF16),
            pltpu.VMEM((ROWS, hidden), BF16),
            pltpu.VMEM((2, *w_out.shape), BF16),
            pltpu.VMEM(w_up.shape, BF16),
            pltpu.VMEM((2, hidden, width), BF16),
            DMA((2 + hidden // 512 + 2,)),
        ],
        compiler_params=pltpu.CompilerParams(vmem_limit_bytes=32 << 20),
        cost_estimate=pl.CostEstimate(flops=4100000000, bytes_accessed=14000000, transcendentals=820000),
    )(slots, stored_all, own_all, arrived, w_out, w_out_other, gain2, w_up, w_down)
    sums = lax.all_gather(send, "mp", axis=0)

    mixed, merged = pl.pallas_call(
        finish_kernel,
        name="finish",
        out_shape=(spec(tokens.shape), spec(bottleneck.shape)),
        in_specs=[SMEM, VMEM, VMEM],
        out_specs=(VMEM,) * 2,
        compiler_params=pltpu.CompilerParams(vmem_limit_bytes=8 << 20),
    )(slots, base, sums)
    return mixed, merged


def solution(mesh):
    placed = (
        P("clip", None, "mp"),
        P("clip", None, "mp"),
        P(),
        P(),
        P(),
        P(),
        P(None, None, "mp"),
        P("mp", None),
        P(),
        P(None, "mp"),
        P("mp", None),
    )
    return jax.shard_map(
        body,
        mesh=mesh,
        in_specs=placed,
        out_specs=(P("clip", None, "mp"), P("clip", None, "mp")),
        check_vma=False,
    )
```

```python
import jax
import jax.numpy as jnp
from jax import lax
from jax.experimental import pallas as pl
from jax.experimental.pallas import tpu as pltpu
from jax.sharding import PartitionSpec as P

HEAD_DIM = 64
BLK = 128
NB = 4
SLOT_DEV = 4
STORE_DEV = 3
GROUP = 4
PAD = 16
STORED = STORE_DEV * BLK
ROWS = STORED + PAD
CLIP_ROWS = SLOT_DEV * BLK
BF16 = jnp.bfloat16
F32 = jnp.float32

VMEM = pl.BlockSpec(memory_space=pltpu.VMEM)
HBM = pl.BlockSpec(memory_space=pltpu.HBM)
DMA = pltpu.SemaphoreType.DMA
SMEM = pl.BlockSpec(memory_space=pltpu.SMEM)


def spec(shape, dtype=BF16):
    return jax.ShapeDtypeStruct(shape, dtype)


def partner(x, step):
    return lax.ppermute(x, "clip", [(i, i ^ step) for i in range(lax.axis_size("clip"))])


def slot_for(store_map, device, owner):
    slot = jnp.int32(-1)
    block = jnp.int32(-1)
    for s in range(STORE_DEV):
        entry = store_map[s, device]
        hit = (entry >= 0) & (entry // SLOT_DEV == owner)
        slot = jnp.where(hit, s, slot)
        block = jnp.where(hit, entry % SLOT_DEV, block)
    return slot, block


def norm_into(x0, x1, gain, out, at, rows):
    half = x0.shape[1]
    x0 = x0.astype(F32)
    x1 = x1.astype(F32)
    scale = 1.0 / (2 * half)
    mean = (jnp.sum(x0, axis=-1, keepdims=True) + jnp.sum(x1, axis=-1, keepdims=True)) * scale
    x0 = x0 - mean
    x1 = x1 - mean
    moment = (
        jnp.sum(x0 * x0, axis=-1, keepdims=True) + jnp.sum(x1 * x1, axis=-1, keepdims=True)
    ) * scale
    inv = lax.rsqrt(moment + 1e-05)
    out[pl.ds(at, rows), :half] = (x0 * inv * gain[:, :half]).astype(BF16)
    out[pl.ds(at, rows), half:] = (x1 * inv * gain[:, half:]).astype(BF16)


def pack_kernel(slots, tokens, extra, near, across, far, stored, store_map, few, tail, sems):
    member = lax.axis_index("clip")
    load_map = pltpu.make_async_copy(slots, store_map, sems.at[0])
    load_few = pltpu.make_async_copy(extra, few, sems.at[1])
    load_map.start()
    load_few.start()
    copies = [
        pltpu.make_async_copy(tokens.at[s], stored.at[pl.ds(s * BLK, BLK), :], sems.at[2 + s])
        for s in range(STORE_DEV)
    ]
    load_map.wait()
    for k, (step, out) in enumerate(((1, near), (3, across), (2, far))):
        slot, _ = slot_for(store_map, member, member ^ step)
        copies.append(
            pltpu.make_async_copy(tokens.at[jnp.maximum(slot, 0)], out, sems.at[2 + STORE_DEV + k])
        )
    for copy in copies:
        copy.start()
    load_few.wait()
    width = stored.shape[1]
    tail[...] = jnp.concatenate(
        [few[0].astype(F32), jnp.zeros((PAD - NB, width), F32)], axis=0
    ).astype(BF16)
    last = pltpu.make_async_copy(tail, stored.at[pl.ds(STORED, PAD), :], sems.at[2 + 2 * STORE_DEV])
    last.start()
    for copy in copies + [last]:
        copy.wait()


def attend_kernel(
    slots,
    all_lengths,
    all_videos,
    stored,
    arrived,
    gain_in,
    w_qkv,
    near,
    across,
    far,
    own,
    normed,
    query,
    keys,
    values,
    context,
    weights,
    info,
    gain,
    store_map,
    lengths,
    videos,
    sems,
):
    member = lax.axis_index("clip")
    small = [
        pltpu.make_async_copy(x, y, sems.at[i])
        for i, (x, y) in enumerate(
            ((gain_in, gain), (slots, store_map), (all_lengths, lengths), (all_videos, videos))
        )
    ]
    loads = [pltpu.make_async_copy(w_qkv.at[i], weights.at[i], sems.at[4 + i]) for i in range(3)]
    for load in small + loads:
        load.start()
    width = query.shape[1]
    for load in small:
        load.wait()
    gains = gain[...]
    for k in range(GROUP - 1):
        rows = slice(k * BLK, (k + 1) * BLK)
        norm_into(arrived[0, rows, :], arrived[1, rows, :], gains, normed, k * BLK, BLK)
    norm_into(stored[0, STORED:, :], stored[1, STORED:, :], gains, normed, CLIP_ROWS, PAD)

    length = lengths[member]
    video = videos[member]
    own_slot, own_block = slot_for(store_map, member, member)
    here = pl.multiple_of(jnp.maximum(own_slot, 0) * BLK, BLK)
    norm_into(
        stored[0, pl.ds(here, BLK), :],
        stored[1, pl.ds(here, BLK), :],
        gains,
        normed,
        (GROUP - 1) * BLK,
        BLK,
    )
    block_at = [slot_for(store_map, member ^ step, member)[1] for step in (1, 3, 2)] + [own_block]
    row_at = [
        pl.multiple_of(jnp.where(block < 0, SLOT_DEV + 1, block) * BLK, BLK) for block in block_at
    ]

    for place in range(GROUP):
        info[place] = block_at[place]

    tile = 256
    pairs = width // BLK
    end = CLIP_ROWS + PAD
    for which, out in ((0, query), (1, keys)):
        loads[which].wait()
        for j in range(0, width, tile):
            got = jnp.dot(normed[...], weights[which, :, j : j + tile], preferred_element_type=F32)
            if which == 0:
                got = got * HEAD_DIM ** (-0.5)
            got = got.astype(BF16)
            for place in range(GROUP):
                out[pl.ds(row_at[place], BLK), j : j + tile] = got[place * BLK : (place + 1) * BLK]
            out[CLIP_ROWS:end, j : j + tile] = got[CLIP_ROWS:]
    loads[2].wait()
    for p in range(pairs):
        if p % 2 == 0:
            j = p * BLK
            wide = jnp.dot(normed[...], weights[2, :, j : j + tile], preferred_element_type=F32)
        got = wide[:, p % 2 * BLK : (p % 2 + 1) * BLK]
        for place in range(GROUP):
            turned = got[place * BLK : (place + 1) * BLK].T
            values[p, :BLK, pl.ds(row_at[place], BLK)] = turned.astype(BF16)
        values[p, :BLK, CLIP_ROWS:end] = got[CLIP_ROWS:].T.astype(BF16)
        values[p, BLK:, :end] = jnp.ones((PAD, end), BF16)
    for b in range(2, SLOT_DEV):

        @pl.when(b >= length)
        def _():
            values[:, :BLK, b * BLK : (b + 1) * BLK] = jnp.zeros((pairs, BLK, BLK), BF16)

    context[...] = jnp.zeros_like(context)
    low = lax.broadcasted_iota(jnp.int32, (BLK, BLK), 1) < HEAD_DIM
    real = lax.broadcasted_iota(jnp.int32, (PAD, 2 * BLK), 0) < NB
    nt = (((1,), (1,)), ((), ()))

    def token_block(place, block, first, count):
        start = pl.multiple_of(first * BLK, BLK)
        at = pl.multiple_of(block * BLK, BLK)
        seen = count * BLK
        cols = [slice(p * BLK, (p + 1) * BLK) for p in range(pairs)]
        scores = []
        for p in range(pairs):
            q = query[pl.ds(at, BLK), cols[p]]
            none = jnp.zeros_like(q)
            both = jnp.concatenate([jnp.where(low, q, none), jnp.where(low, none, q)], axis=0)
            k = jnp.concatenate([keys[pl.ds(start, seen), cols[p]], keys[CLIP_ROWS:end, cols[p]]], axis=0)
            s = lax.dot_general(k, both, nt, preferred_element_type=F32)
            scores.append((s[:seen], jnp.where(real, s[seen:], -1e30)))
        tops = [
            jnp.maximum(jnp.max(s, axis=0, keepdims=True), jnp.max(se, axis=0, keepdims=True))
            for s, se in scores
        ]
        parts = [
            jnp.concatenate([jnp.exp(s - top).astype(BF16), jnp.exp(se - top).astype(BF16)], axis=0)
            for (s, se), top in zip(scores, tops)
        ]
        sums = []
        for p in range(pairs):
            v = jnp.concatenate([values[p, :, pl.ds(start, seen)], values[p, :, CLIP_ROWS:end]], axis=1)
            sums.append(jnp.dot(v, parts[p], preferred_element_type=F32))
        for p in range(pairs):
            o = sums[p]
            total = o[BLK : BLK + 1]
            o = jnp.concatenate(
                [o[:HEAD_DIM, :BLK] / total[:, :BLK], o[HEAD_DIM:BLK, BLK:] / total[:, BLK:]], axis=0
            )
            context[place, :, cols[p]] = o.T.astype(BF16)

    def visit(place, carry):
        block = info[place]
        is_video = block < video
        first = jnp.where(is_video, 0, video)
        seen = jnp.where(is_video, video, length - video)
        for count in range(1, SLOT_DEV):

            @pl.when((block >= 0) & (seen == count))
            def _():
                token_block(place, block, first, count)

        return carry

    lax.fori_loop(0, GROUP, visit, 0)

    heads = width // HEAD_DIM
    sub = 8
    qe = query[CLIP_ROWS:end, :].astype(F32)[:sub]
    qe = jnp.concatenate([qe] * heads, axis=0)
    row_head = lax.broadcasted_iota(jnp.int32, (heads * sub, width), 0) // sub
    col_head = lax.broadcasted_iota(jnp.int32, (heads * sub, width), 1) // HEAD_DIM
    qe = jnp.where(row_head == col_head, qe, 0.0).astype(BF16)
    s = lax.dot_general(qe, keys[:end, :], nt, preferred_element_type=F32)
    col = lax.broadcasted_iota(jnp.int32, s.shape, 1)
    bottle = (col >= CLIP_ROWS) & (col < CLIP_ROWS + NB)
    parts = []
    for allowed in (
        bottle | (col < video * BLK),
        bottle | ((col >= video * BLK) & (col < length * BLK)),
    ):
        masked = jnp.where(allowed, s, -1e30)
        e = jnp.exp(masked - jnp.max(masked, axis=-1, keepdims=True))
        parts.append((e / jnp.sum(e, axis=-1, keepdims=True)).astype(BF16))
    first_head = lax.broadcasted_iota(jnp.int32, (sub, BLK), 1) < HEAD_DIM
    for p in range(pairs):
        rows = slice(2 * p * sub, (2 * p + 2) * sub)
        both = jnp.concatenate([parts[0][rows], parts[1][rows]], axis=0)
        o = lax.dot_general(both, values[p, :BLK, :end], nt, preferred_element_type=F32)
        o = 0.5 * (o[: 2 * sub] + o[2 * sub :])
        o = jnp.where(first_head, o[:sub], o[sub:])
        own[BLK:, p * BLK : (p + 1) * BLK] = jnp.concatenate([o, jnp.zeros_like(o)], axis=0).astype(BF16)
    near[...] = context[0]
    across[...] = context[1]
    far[...] = context[2]
    own[:BLK, :] = context[3]


def feed_kernel(
    store_map,
    stored,
    own,
    arrived,
    w_out,
    w_out_other,
    gain,
    w_up,
    w_down,
    base,
    send,
    context,
    after,
    normed,
    active,
):
    member = lax.axis_index("clip")
    core = lax.axis_index("mp")
    half = base.shape[1]
    hidden = w_up.shape[1]
    sides = (core, 1 - core)
    for s in range(STORE_DEV):
        entry = store_map[s, member]
        step = jnp.where(entry >= 0, (entry // SLOT_DEV) ^ member, -1)
        at = jnp.where(step == 1, 0, jnp.where(step == 3, 1, 2))
        at = pl.multiple_of(at * BLK, BLK)
        rows = slice(s * BLK, (s + 1) * BLK)

        @pl.when(step == 0)
        def _():
            for k in range(2):
                context[k, rows, :] = own[sides[k], :BLK, :]

        @pl.when(step > 0)
        def _():
            for k in range(2):
                context[k, rows, :] = arrived[sides[k], pl.ds(at, BLK), :]

        @pl.when(step < 0)
        def _():
            for k in range(2):
                context[k, rows, :] = jnp.zeros((BLK, half), BF16)

    for k in range(2):
        context[k, STORED:, :] = own[sides[k], BLK:, :]

    tile = 256
    for j in range(0, 2 * half, tile):
        got = jnp.dot(context[0], w_out[:, j : j + tile], preferred_element_type=F32)
        got = got + jnp.dot(context[1], w_out_other[:, j : j + tile], preferred_element_type=F32)
        side, off = divmod(j, half)
        got = got + stored[side, :, off : off + tile].astype(F32)
        after[:, j : j + tile] = got.astype(BF16)
    gains = gain[...]
    for r in range(0, ROWS, 80):
        norm_into(after[r : r + 80, :half], after[r : r + 80, half:], gains, normed, r, 80)
    for j in range(0, hidden, tile):
        got = jnp.dot(normed[...], w_up[:, j : j + tile], preferred_element_type=F32)
        active[:, j : j + tile] = jax.nn.gelu(got, approximate=True).astype(BF16)
    for j in range(0, half, tile):
        other = pl.multiple_of((1 - core) * half + j, tile)
        got = jnp.dot(active[...], w_down[:, pl.ds(other, tile)], preferred_element_type=F32)
        send[:, j : j + tile] = got.astype(BF16)
        mine = pl.multiple_of(core * half + j, tile)
        got = jnp.dot(active[...], w_down[:, pl.ds(mine, tile)], preferred_element_type=F32)
        base[:, j : j + tile] = got + after[:, pl.ds(mine, tile)].astype(F32)


def finish_kernel(store_map, base, sums, mixed, merged):
    member = lax.axis_index("clip")
    core = lax.axis_index("mp")
    other = 1 - core
    for s in range(STORE_DEV):
        rows = slice(s * BLK, (s + 1) * BLK)
        got = base[rows, :] + sums[other, rows, :].astype(F32)
        keep = store_map[s, member] >= 0
        mixed[s] = jnp.where(keep, got, 0.0).astype(BF16)
    got = base[STORED:, :] + sums[other, STORED:, :].astype(F32)
    merged[0] = got[:NB].astype(BF16)


def stay(x):
    return pltpu.with_memory_space_constraint(x, pltpu.HBM)


def attend(slots, clip_lengths, video_blocks, stored_all, arrived, gain1, w_qkv):
    width = stored_all.shape[2]
    model = 2 * width
    heads_width = w_qkv.shape[2]
    block = spec((BLK, width))
    return pl.pallas_call(
        attend_kernel,
        name="attend",
        out_shape=(block, block, block, spec((BLK + PAD, width))),
        in_specs=[HBM, HBM, HBM, VMEM, VMEM, HBM, HBM],
        out_specs=(VMEM,) * 4,
        scratch_shapes=[
            pltpu.VMEM((CLIP_ROWS + PAD, model), BF16),
            pltpu.VMEM((CLIP_ROWS + 2 * BLK, heads_width), BF16),
            pltpu.VMEM((CLIP_ROWS + 2 * BLK, heads_width), BF16),
            pltpu.VMEM((heads_width // BLK, BLK + PAD, CLIP_ROWS + 2 * BLK), BF16),
            pltpu.VMEM((GROUP, BLK, heads_width), BF16),
            pltpu.VMEM(w_qkv.shape, BF16),
            pltpu.SMEM((GROUP,), jnp.int32),
            pltpu.VMEM((1, model), F32),
            pltpu.SMEM(slots.shape, jnp.int32),
            pltpu.SMEM(clip_lengths.shape, jnp.int32),
            pltpu.SMEM(video_blocks.shape, jnp.int32),
            DMA((7,)),
        ],
        compiler_params=pltpu.CompilerParams(vmem_limit_bytes=24 << 20),
        cost_estimate=pl.CostEstimate(flops=2500000000, bytes_accessed=6000000, transcendentals=3000000),
    )(
        stay(slots),
        stay(clip_lengths),
        stay(video_blocks),
        stored_all,
        arrived,
        stay(gain1),
        stay(w_qkv),
    )


def feed(slots, stored_all, own_all, arrived, w_out, w_out_other, gain2, w_up, w_down):
    width = stored_all.shape[2]
    model = 2 * width
    hidden = w_up.shape[1]
    return pl.pallas_call(
        feed_kernel,
        name="feed",
        out_shape=(spec((ROWS, width), F32), spec((ROWS, width))),
        in_specs=[SMEM] + [VMEM] * 8,
        out_specs=(VMEM,) * 2,
        scratch_shapes=[
            pltpu.VMEM((2, ROWS, width), BF16),
            pltpu.VMEM((ROWS, model), BF16),
            pltpu.VMEM((ROWS, model), BF16),
            pltpu.VMEM((ROWS, hidden), BF16),
        ],
        compiler_params=pltpu.CompilerParams(vmem_limit_bytes=16 << 20),
        cost_estimate=pl.CostEstimate(flops=4100000000, bytes_accessed=14000000, transcendentals=820000),
    )(slots, stored_all, own_all, arrived, w_out, w_out_other, gain2, w_up, w_down)


def body(
    tokens,
    bottleneck,
    clip_lengths,
    video_blocks,
    store_map,
    norm1_gain,
    w_qkv,
    w_out,
    norm2_gain,
    w_up,
    w_down,
):
    width = tokens.shape[2]
    model = 2 * width
    gain1 = norm1_gain.reshape(1, model)
    gain2 = norm2_gain.reshape(1, model)
    block = spec((BLK, width))
    w_out_other = lax.ppermute(w_out, "mp", [(0, 1), (1, 0)])
    slots = store_map.T

    near, across, far, stored = pl.pallas_call(
        pack_kernel,
        name="pack",
        out_shape=(block, block, block, spec((ROWS, width))),
        in_specs=[HBM, HBM, HBM],
        out_specs=(HBM,) * 4,
        scratch_shapes=[
            pltpu.SMEM(slots.shape, jnp.int32),
            pltpu.VMEM(bottleneck.shape, BF16),
            pltpu.VMEM((PAD, width), BF16),
            DMA((2 * STORE_DEV + 3,)),
        ],
        compiler_params=pltpu.CompilerParams(vmem_limit_bytes=4 << 20),
    )(stay(slots), stay(tokens), stay(bottleneck))
    across = partner(across, 3)
    near = partner(near, 1)
    far = partner(far, 2)
    stored_all = lax.all_gather(stored, "mp", axis=0)
    arrived = lax.all_gather(jnp.concatenate([near, across, far], axis=0), "mp", axis=0)

    near, across, far, own = attend(
        slots, clip_lengths, video_blocks, stored_all, arrived, gain1, w_qkv
    )
    across = partner(across, 3)
    near = partner(near, 1)
    far = partner(far, 2)
    own_all = lax.all_gather(own, "mp", axis=0)
    arrived = lax.all_gather(jnp.concatenate([near, across, far], axis=0), "mp", axis=0)

    base, send = feed(
        slots, stored_all, own_all, arrived, w_out, w_out_other, gain2, w_up, w_down
    )
    sums = lax.all_gather(send, "mp", axis=0)

    mixed, merged = pl.pallas_call(
        finish_kernel,
        name="finish",
        out_shape=(spec(tokens.shape), spec(bottleneck.shape)),
        in_specs=[SMEM, VMEM, VMEM],
        out_specs=(VMEM,) * 2,
        compiler_params=pltpu.CompilerParams(vmem_limit_bytes=8 << 20),
    )(slots, base, sums)
    return mixed, merged


def solution(mesh):
    placed = (
        P("clip", None, "mp"),
        P("clip", None, "mp"),
        P(),
        P(),
        P(),
        P(),
        P(None, None, "mp"),
        P("mp", None),
        P(),
        P(None, "mp"),
        P("mp", None),
    )
    return jax.shard_map(
        body,
        mesh=mesh,
        in_specs=placed,
        out_specs=(P("clip", None, "mp"), P("clip", None, "mp")),
        check_vma=False,
    )
```

```python
import jax
import jax.numpy as jnp
from jax import lax
from jax.experimental import pallas as pl
from jax.experimental.pallas import tpu as pltpu
from jax.sharding import PartitionSpec as P

HEAD_DIM = 64
BLK = 128
NB = 4
SLOT_DEV = 4
STORE_DEV = 3
GROUP = 4
PAD = 16
STORED = STORE_DEV * BLK
ROWS = STORED + PAD
CLIP_ROWS = SLOT_DEV * BLK
BF16 = jnp.bfloat16
F32 = jnp.float32

VMEM = pl.BlockSpec(memory_space=pltpu.VMEM)
HBM = pl.BlockSpec(memory_space=pltpu.HBM)
DMA = pltpu.SemaphoreType.DMA
SMEM = pl.BlockSpec(memory_space=pltpu.SMEM)


def spec(shape, dtype=BF16):
    return jax.ShapeDtypeStruct(shape, dtype)


def partner(x, step):
    return lax.ppermute(x, "clip", [(i, i ^ step) for i in range(lax.axis_size("clip"))])


def slot_for(store_map, device, owner):
    slot = jnp.int32(-1)
    block = jnp.int32(-1)
    for s in range(STORE_DEV):
        entry = store_map[s, device]
        hit = (entry >= 0) & (entry // SLOT_DEV == owner)
        slot = jnp.where(hit, s, slot)
        block = jnp.where(hit, entry % SLOT_DEV, block)
    return slot, block


def norm_into(x0, x1, gain, out, at, rows):
    half = x0.shape[1]
    x0 = x0.astype(F32)
    x1 = x1.astype(F32)
    scale = 1.0 / (2 * half)
    mean = (jnp.sum(x0, axis=-1, keepdims=True) + jnp.sum(x1, axis=-1, keepdims=True)) * scale
    x0 = x0 - mean
    x1 = x1 - mean
    moment = (
        jnp.sum(x0 * x0, axis=-1, keepdims=True) + jnp.sum(x1 * x1, axis=-1, keepdims=True)
    ) * scale
    inv = lax.rsqrt(moment + 1e-05)
    out[pl.ds(at, rows), :half] = (x0 * inv * gain[:, :half]).astype(BF16)
    out[pl.ds(at, rows), half:] = (x1 * inv * gain[:, half:]).astype(BF16)


def pack_kernel(slots, tokens, extra, near, across, far, stored, store_map, few, tail, sems):
    member = lax.axis_index("clip")
    load_map = pltpu.make_async_copy(slots, store_map, sems.at[0])
    load_few = pltpu.make_async_copy(extra, few, sems.at[1])
    load_map.start()
    load_few.start()
    copies = [
        pltpu.make_async_copy(tokens.at[s], stored.at[pl.ds(s * BLK, BLK), :], sems.at[2 + s])
        for s in range(STORE_DEV)
    ]
    load_map.wait()
    for k, (step, out) in enumerate(((1, near), (3, across), (2, far))):
        slot, _ = slot_for(store_map, member, member ^ step)
        copies.append(
            pltpu.make_async_copy(tokens.at[jnp.maximum(slot, 0)], out, sems.at[2 + STORE_DEV + k])
        )
    for copy in copies:
        copy.start()
    load_few.wait()
    width = stored.shape[1]
    tail[...] = jnp.concatenate(
        [few[0].astype(F32), jnp.zeros((PAD - NB, width), F32)], axis=0
    ).astype(BF16)
    last = pltpu.make_async_copy(tail, stored.at[pl.ds(STORED, PAD), :], sems.at[2 + 2 * STORE_DEV])
    last.start()
    for copy in copies + [last]:
        copy.wait()


def ready_kernel(slots, gain_in, w_qkv, stored, weights, query, keys, values, normed, gain, store_map, sems):
    member = lax.axis_index("clip")
    small = [
        pltpu.make_async_copy(x, y, sems.at[i])
        for i, (x, y) in enumerate(((gain_in, gain), (slots, store_map)))
    ]
    loads = [pltpu.make_async_copy(w_qkv.at[i], weights.at[i], sems.at[2 + i]) for i in range(3)]
    for load in small + loads:
        load.start()
    small[0].wait()
    gains = gain[...]
    norm_into(stored[0, STORED:, :], stored[1, STORED:, :], gains, normed, BLK, PAD)
    small[1].wait()
    slot, _ = slot_for(store_map, member, member)
    here = pl.multiple_of(jnp.maximum(slot, 0) * BLK, BLK)
    norm_into(
        stored[0, pl.ds(here, BLK), :], stored[1, pl.ds(here, BLK), :], gains, normed, 0, BLK
    )
    width = query.shape[1]
    tile = 256
    for which, out in ((0, query), (1, keys)):
        loads[which].wait()
        for j in range(0, width, tile):
            got = jnp.dot(normed[...], weights[which, :, j : j + tile], preferred_element_type=F32)
            if which == 0:
                got = got * HEAD_DIM ** (-0.5)
            out[:, j : j + tile] = got.astype(BF16)
    loads[2].wait()
    for j in range(0, width, tile):
        got = jnp.dot(normed[...], weights[2, :, j : j + tile], preferred_element_type=F32)
        for k in range(tile // BLK):
            p = j // BLK + k
            cols = slice(k * BLK, (k + 1) * BLK)
            values[p, :, :BLK] = got[:BLK, cols].T.astype(BF16)
            values[p, :, BLK:] = got[BLK:, cols].T.astype(BF16)


NT = (((1,), (1,)), ((), ()))
END = CLIP_ROWS + PAD


def token_block(query, keys, values, context, place, block, first, count):
    pairs = values.shape[0]
    low = lax.broadcasted_iota(jnp.int32, (BLK, BLK), 1) < HEAD_DIM
    real = lax.broadcasted_iota(jnp.int32, (PAD, 2 * BLK), 0) < NB
    start = pl.multiple_of(first * BLK, BLK)
    at = pl.multiple_of(block * BLK, BLK)
    seen = count * BLK
    cols = [slice(p * BLK, (p + 1) * BLK) for p in range(pairs)]
    scores = []
    for p in range(pairs):
        q = query[pl.ds(at, BLK), cols[p]]
        none = jnp.zeros_like(q)
        both = jnp.concatenate([jnp.where(low, q, none), jnp.where(low, none, q)], axis=0)
        k = jnp.concatenate([keys[pl.ds(start, seen), cols[p]], keys[CLIP_ROWS:END, cols[p]]], axis=0)
        s = lax.dot_general(k, both, NT, preferred_element_type=F32)
        scores.append((s[:seen], jnp.where(real, s[seen:], -1e30)))
    tops = [
        jnp.maximum(jnp.max(s, axis=0, keepdims=True), jnp.max(se, axis=0, keepdims=True))
        for s, se in scores
    ]
    parts = [
        jnp.concatenate([jnp.exp(s - top).astype(BF16), jnp.exp(se - top).astype(BF16)], axis=0)
        for (s, se), top in zip(scores, tops)
    ]
    sums = []
    for p in range(pairs):
        v = jnp.concatenate([values[p, :, pl.ds(start, seen)], values[p, :, CLIP_ROWS:END]], axis=1)
        sums.append(jnp.dot(v, parts[p], preferred_element_type=F32))
    for p in range(pairs):
        o = sums[p]
        total = o[BLK : BLK + 1]
        o = jnp.concatenate(
            [o[:HEAD_DIM, :BLK] / total[:, :BLK], o[HEAD_DIM:BLK, BLK:] / total[:, BLK:]], axis=0
        )
        context[place, :, cols[p]] = o.T.astype(BF16)


def visit_blocks(info, places, query, keys, values, context):
    def visit(i, carry):
        place = places[0] + i * (places[1] - places[0])
        block = info[0, place]
        length = info[0, GROUP]
        video = info[0, GROUP + 1]
        is_video = block < video
        first = jnp.where(is_video, 0, video)
        seen = jnp.where(is_video, video, length - video)
        for count in range(1, SLOT_DEV):

            @pl.when((block >= 0) & (seen == count))
            def _():
                token_block(query, keys, values, context, i, block, first, count)

        return carry

    lax.fori_loop(0, 2, visit, 0)


def attend_kernel(
    slots,
    all_lengths,
    all_videos,
    gain_in,
    arrived,
    weights,
    own_query,
    own_keys,
    own_values,
    across,
    far,
    query,
    keys,
    values,
    facts,
    normed,
    context,
    info,
    gain,
    store_map,
    lengths,
    videos,
    sems,
):
    member = lax.axis_index("clip")
    small = [
        pltpu.make_async_copy(x, y, sems.at[i])
        for i, (x, y) in enumerate(
            ((gain_in, gain), (slots, store_map), (all_lengths, lengths), (all_videos, videos))
        )
    ]
    for load in small:
        load.start()
    width = query.shape[1]
    pairs = width // BLK
    context[...] = jnp.zeros_like(context)
    small[0].wait()
    gains = gain[...]
    for k in range(GROUP - 1):
        rows = slice(k * BLK, (k + 1) * BLK)
        norm_into(arrived[0, rows, :], arrived[1, rows, :], gains, normed, k * BLK, BLK)
    for load in small[1:]:
        load.wait()
    length = lengths[member]
    video = videos[member]
    block_at = [slot_for(store_map, member ^ step, member)[1] for step in (1, 3, 2, 0)]
    row_at = [
        pl.multiple_of(jnp.where(block < 0, SLOT_DEV + 1, block) * BLK, BLK) for block in block_at
    ]
    for place in range(GROUP):
        info[0, place] = block_at[place]
    info[0, GROUP] = length
    info[0, GROUP + 1] = video
    keep = pltpu.make_async_copy(info, facts, sems.at[4])
    keep.start()

    last = GROUP - 1
    for own, out in ((own_query, query), (own_keys, keys)):
        out[pl.ds(row_at[last], BLK), :] = own[:BLK, :]
        out[CLIP_ROWS:END, :] = own[BLK:, :]
    for p in range(pairs):
        values[p, :BLK, pl.ds(row_at[last], BLK)] = own_values[p, :, :BLK]
        values[p, :BLK, CLIP_ROWS:END] = own_values[p, :, BLK:]
        values[p, BLK:, :END] = jnp.ones((PAD, END), BF16)
    tile = 256
    for which, out in ((0, query), (1, keys)):
        for j in range(0, width, tile):
            got = jnp.dot(normed[...], weights[which, :, j : j + tile], preferred_element_type=F32)
            if which == 0:
                got = got * HEAD_DIM ** (-0.5)
            got = got.astype(BF16)
            for place in range(last):
                out[pl.ds(row_at[place], BLK), j : j + tile] = got[place * BLK : (place + 1) * BLK]
    for j in range(0, width, tile):
        got = jnp.dot(normed[...], weights[2, :, j : j + tile], preferred_element_type=F32)
        for k in range(tile // BLK):
            p = j // BLK + k
            cols = slice(k * BLK, (k + 1) * BLK)
            for place in range(last):
                turned = got[place * BLK : (place + 1) * BLK, cols].T
                values[p, :BLK, pl.ds(row_at[place], BLK)] = turned.astype(BF16)
    for b in range(2, SLOT_DEV):

        @pl.when(b >= length)
        def _():
            values[:, :BLK, b * BLK : (b + 1) * BLK] = jnp.zeros((pairs, BLK, BLK), BF16)

    visit_blocks(info, (1, 2), query, keys, values, context)
    across[...] = context[0]
    far[...] = context[1]
    keep.wait()


def rest_kernel(query, keys, values, facts, near, own, context, info, sems):
    load = pltpu.make_async_copy(facts, info, sems.at[0])
    load.start()
    width = query.shape[1]
    pairs = width // BLK
    context[...] = jnp.zeros_like(context)
    load.wait()
    length = info[0, GROUP]
    video = info[0, GROUP + 1]
    visit_blocks(info, (0, 3), query, keys, values, context)
    near[...] = context[0]
    own[:BLK, :] = context[1]

    heads = width // HEAD_DIM
    sub = 8
    qe = query[CLIP_ROWS:END, :].astype(F32)[:sub]
    qe = jnp.concatenate([qe] * heads, axis=0)
    row_head = lax.broadcasted_iota(jnp.int32, (heads * sub, width), 0) // sub
    col_head = lax.broadcasted_iota(jnp.int32, (heads * sub, width), 1) // HEAD_DIM
    qe = jnp.where(row_head == col_head, qe, 0.0).astype(BF16)
    s = lax.dot_general(qe, keys[:END, :], NT, preferred_element_type=F32)
    col = lax.broadcasted_iota(jnp.int32, s.shape, 1)
    bottle = (col >= CLIP_ROWS) & (col < CLIP_ROWS + NB)
    parts = []
    for allowed in (
        bottle | (col < video * BLK),
        bottle | ((col >= video * BLK) & (col < length * BLK)),
    ):
        masked = jnp.where(allowed, s, -1e30)
        e = jnp.exp(masked - jnp.max(masked, axis=-1, keepdims=True))
        parts.append((e / jnp.sum(e, axis=-1, keepdims=True)).astype(BF16))
    first_head = lax.broadcasted_iota(jnp.int32, (sub, BLK), 1) < HEAD_DIM
    for p in range(pairs):
        rows = slice(2 * p * sub, (2 * p + 2) * sub)
        both = jnp.concatenate([parts[0][rows], parts[1][rows]], axis=0)
        o = lax.dot_general(both, values[p, :BLK, :END], NT, preferred_element_type=F32)
        o = 0.5 * (o[: 2 * sub] + o[2 * sub :])
        o = jnp.where(first_head, o[:sub], o[sub:])
        own[BLK:, p * BLK : (p + 1) * BLK] = jnp.concatenate([o, jnp.zeros_like(o)], axis=0).astype(BF16)


def feed_kernel(
    store_map,
    stored,
    own,
    arrived,
    w_out,
    w_out_other,
    gain,
    w_up,
    w_down,
    base,
    send,
    context,
    after,
    normed,
    active,
):
    member = lax.axis_index("clip")
    core = lax.axis_index("mp")
    half = base.shape[1]
    hidden = w_up.shape[1]
    sides = (core, 1 - core)
    for s in range(STORE_DEV):
        entry = store_map[s, member]
        step = jnp.where(entry >= 0, (entry // SLOT_DEV) ^ member, -1)
        at = jnp.where(step == 1, 0, jnp.where(step == 3, 1, 2))
        at = pl.multiple_of(at * BLK, BLK)
        rows = slice(s * BLK, (s + 1) * BLK)

        @pl.when(step == 0)
        def _():
            for k in range(2):
                context[k, rows, :] = own[sides[k], :BLK, :]

        @pl.when(step > 0)
        def _():
            for k in range(2):
                context[k, rows, :] = arrived[sides[k], pl.ds(at, BLK), :]

        @pl.when(step < 0)
        def _():
            for k in range(2):
                context[k, rows, :] = jnp.zeros((BLK, half), BF16)

    for k in range(2):
        context[k, STORED:, :] = own[sides[k], BLK:, :]

    tile = 256
    for j in range(0, 2 * half, tile):
        got = jnp.dot(context[0], w_out[:, j : j + tile], preferred_element_type=F32)
        got = got + jnp.dot(context[1], w_out_other[:, j : j + tile], preferred_element_type=F32)
        side, off = divmod(j, half)
        got = got + stored[side, :, off : off + tile].astype(F32)
        after[:, j : j + tile] = got.astype(BF16)
    gains = gain[...]
    for r in range(0, ROWS, 80):
        norm_into(after[r : r + 80, :half], after[r : r + 80, half:], gains, normed, r, 80)
    for j in range(0, hidden, tile):
        got = jnp.dot(normed[...], w_up[:, j : j + tile], preferred_element_type=F32)
        active[:, j : j + tile] = jax.nn.gelu(got, approximate=True).astype(BF16)
    for j in range(0, half, tile):
        other = pl.multiple_of((1 - core) * half + j, tile)
        got = jnp.dot(active[...], w_down[:, pl.ds(other, tile)], preferred_element_type=F32)
        send[:, j : j + tile] = got.astype(BF16)
        mine = pl.multiple_of(core * half + j, tile)
        got = jnp.dot(active[...], w_down[:, pl.ds(mine, tile)], preferred_element_type=F32)
        base[:, j : j + tile] = got + after[:, pl.ds(mine, tile)].astype(F32)


def finish_kernel(store_map, base, sums, mixed, merged):
    member = lax.axis_index("clip")
    core = lax.axis_index("mp")
    other = 1 - core
    for s in range(STORE_DEV):
        rows = slice(s * BLK, (s + 1) * BLK)
        got = base[rows, :] + sums[other, rows, :].astype(F32)
        keep = store_map[s, member] >= 0
        mixed[s] = jnp.where(keep, got, 0.0).astype(BF16)
    got = base[STORED:, :] + sums[other, STORED:, :].astype(F32)
    merged[0] = got[:NB].astype(BF16)


def stay(x):
    return pltpu.with_memory_space_constraint(x, pltpu.HBM)


def ready(slots, gain1, w_qkv, stored_all):
    model = w_qkv.shape[1]
    width = w_qkv.shape[2]
    pairs = width // BLK
    return pl.pallas_call(
        ready_kernel,
        name="ready",
        out_shape=(
            spec(w_qkv.shape),
            spec((BLK + PAD, width)),
            spec((BLK + PAD, width)),
            spec((pairs, BLK, BLK + PAD)),
        ),
        in_specs=[HBM, HBM, HBM, VMEM],
        out_specs=(VMEM,) * 4,
        scratch_shapes=[
            pltpu.VMEM((BLK + PAD, model), BF16),
            pltpu.VMEM((1, model), F32),
            pltpu.SMEM(slots.shape, jnp.int32),
            DMA((5,)),
        ],
        compiler_params=pltpu.CompilerParams(vmem_limit_bytes=8 << 20),
        cost_estimate=pl.CostEstimate(flops=450000000, bytes_accessed=4000000, transcendentals=0),
    )(stay(slots), stay(gain1), stay(w_qkv), stored_all)


def attend(slots, clip_lengths, video_blocks, gain1, arrived, weights, own_qkv):
    model = weights.shape[1]
    width = weights.shape[2]
    pairs = width // BLK
    rows = CLIP_ROWS + 2 * BLK
    block = spec((BLK, width))
    info = (1, 2 * GROUP)
    return pl.pallas_call(
        attend_kernel,
        name="attend",
        out_shape=(
            block,
            block,
            spec((rows, width)),
            spec((rows, width)),
            spec((pairs, BLK + PAD, rows)),
            spec(info, jnp.int32),
        ),
        in_specs=[HBM] * 4 + [VMEM] * 5,
        out_specs=(VMEM,) * 6,
        scratch_shapes=[
            pltpu.VMEM(((GROUP - 1) * BLK, model), BF16),
            pltpu.VMEM((2, BLK, width), BF16),
            pltpu.SMEM(info, jnp.int32),
            pltpu.VMEM((1, model), F32),
            pltpu.SMEM(slots.shape, jnp.int32),
            pltpu.SMEM(clip_lengths.shape, jnp.int32),
            pltpu.SMEM(video_blocks.shape, jnp.int32),
            DMA((5,)),
        ],
        compiler_params=pltpu.CompilerParams(vmem_limit_bytes=16 << 20),
        cost_estimate=pl.CostEstimate(flops=1800000000, bytes_accessed=6000000, transcendentals=1500000),
    )(
        stay(slots),
        stay(clip_lengths),
        stay(video_blocks),
        stay(gain1),
        arrived,
        weights,
        *own_qkv,
    )


def rest(query, keys, values, facts):
    width = query.shape[1]
    info = (1, 2 * GROUP)
    return pl.pallas_call(
        rest_kernel,
        name="rest",
        out_shape=(spec((BLK, width)), spec((BLK + PAD, width))),
        in_specs=[VMEM] * 4,
        out_specs=(VMEM,) * 2,
        scratch_shapes=[
            pltpu.VMEM((2, BLK, width), BF16),
            pltpu.SMEM(info, jnp.int32),
            DMA((1,)),
        ],
        compiler_params=pltpu.CompilerParams(vmem_limit_bytes=16 << 20),
        cost_estimate=pl.CostEstimate(flops=700000000, bytes_accessed=3000000, transcendentals=1500000),
    )(query, keys, values, facts)


def feed(slots, stored_all, own_all, arrived, w_out, w_out_other, gain2, w_up, w_down):
    width = stored_all.shape[2]
    model = 2 * width
    hidden = w_up.shape[1]
    return pl.pallas_call(
        feed_kernel,
        name="feed",
        out_shape=(spec((ROWS, width), F32), spec((ROWS, width))),
        in_specs=[SMEM] + [VMEM] * 8,
        out_specs=(VMEM,) * 2,
        scratch_shapes=[
            pltpu.VMEM((2, ROWS, width), BF16),
            pltpu.VMEM((ROWS, model), BF16),
            pltpu.VMEM((ROWS, model), BF16),
            pltpu.VMEM((ROWS, hidden), BF16),
        ],
        compiler_params=pltpu.CompilerParams(vmem_limit_bytes=16 << 20),
        cost_estimate=pl.CostEstimate(flops=4100000000, bytes_accessed=14000000, transcendentals=820000),
    )(slots, stored_all, own_all, arrived, w_out, w_out_other, gain2, w_up, w_down)


def body(
    tokens,
    bottleneck,
    clip_lengths,
    video_blocks,
    store_map,
    norm1_gain,
    w_qkv,
    w_out,
    norm2_gain,
    w_up,
    w_down,
):
    width = tokens.shape[2]
    model = 2 * width
    gain1 = norm1_gain.reshape(1, model)
    gain2 = norm2_gain.reshape(1, model)
    block = spec((BLK, width))
    w_out_other = lax.ppermute(w_out, "mp", [(0, 1), (1, 0)])
    slots = store_map.T

    near, across, far, stored = pl.pallas_call(
        pack_kernel,
        name="pack",
        out_shape=(block, block, block, spec((ROWS, width))),
        in_specs=[HBM, HBM, HBM],
        out_specs=(HBM,) * 4,
        scratch_shapes=[
            pltpu.SMEM(slots.shape, jnp.int32),
            pltpu.VMEM(bottleneck.shape, BF16),
            pltpu.VMEM((PAD, width), BF16),
            DMA((2 * STORE_DEV + 3,)),
        ],
        compiler_params=pltpu.CompilerParams(vmem_limit_bytes=4 << 20),
    )(stay(slots), stay(tokens), stay(bottleneck))
    across = partner(across, 3)
    near = partner(near, 1)
    far = partner(far, 2)
    stored_all = lax.all_gather(stored, "mp", axis=0)
    weights, *own_qkv = ready(slots, gain1, w_qkv, stored_all)
    arrived = lax.all_gather(jnp.concatenate([near, across, far], axis=0), "mp", axis=0)

    across, far, query, keys, values, facts = attend(
        slots, clip_lengths, video_blocks, gain1, arrived, weights, own_qkv
    )
    far = partner(far, 2)
    across = partner(across, 3)
    near, own = rest(query, keys, values, facts)
    near = partner(near, 1)
    own, far, across = lax.optimization_barrier((own, far, across))
    own_all = lax.all_gather(own, "mp", axis=0)
    arrived = lax.all_gather(jnp.concatenate([near, across, far], axis=0), "mp", axis=0)

    base, send = feed(
        slots, stored_all, own_all, arrived, w_out, w_out_other, gain2, w_up, w_down
    )
    sums = lax.all_gather(send, "mp", axis=0)

    mixed, merged = pl.pallas_call(
        finish_kernel,
        name="finish",
        out_shape=(spec(tokens.shape), spec(bottleneck.shape)),
        in_specs=[SMEM, VMEM, VMEM],
        out_specs=(VMEM,) * 2,
        compiler_params=pltpu.CompilerParams(vmem_limit_bytes=8 << 20),
    )(slots, base, sums)
    return mixed, merged


def solution(mesh):
    placed = (
        P("clip", None, "mp"),
        P("clip", None, "mp"),
        P(),
        P(),
        P(),
        P(),
        P(None, None, "mp"),
        P("mp", None),
        P(),
        P(None, "mp"),
        P("mp", None),
    )
    return jax.shard_map(
        body,
        mesh=mesh,
        in_specs=placed,
        out_specs=(P("clip", None, "mp"), P("clip", None, "mp")),
        check_vma=False,
    )
```

```python
import jax
import jax.numpy as jnp
from jax import lax
from jax.experimental import pallas as pl
from jax.experimental.pallas import tpu as pltpu
from jax.sharding import PartitionSpec as P

HEAD_DIM = 64
BLK = 128
NB = 4
SLOT_DEV = 4
STORE_DEV = 3
GROUP = 4
PAD = 16
STORED = STORE_DEV * BLK
ROWS = STORED + PAD
CLIP_ROWS = SLOT_DEV * BLK
BF16 = jnp.bfloat16
F32 = jnp.float32

VMEM = pl.BlockSpec(memory_space=pltpu.VMEM)
HBM = pl.BlockSpec(memory_space=pltpu.HBM)
DMA = pltpu.SemaphoreType.DMA
SMEM = pl.BlockSpec(memory_space=pltpu.SMEM)


def spec(shape, dtype=BF16):
    return jax.ShapeDtypeStruct(shape, dtype)


def partner(x, step):
    return lax.ppermute(x, "clip", [(i, i ^ step) for i in range(lax.axis_size("clip"))])


def slot_for(store_map, device, owner):
    slot = jnp.int32(-1)
    block = jnp.int32(-1)
    for s in range(STORE_DEV):
        entry = store_map[s, device]
        hit = (entry >= 0) & (entry // SLOT_DEV == owner)
        slot = jnp.where(hit, s, slot)
        block = jnp.where(hit, entry % SLOT_DEV, block)
    return slot, block


def norm_into(x0, x1, gain, out, at, rows):
    half = x0.shape[1]
    x0 = x0.astype(F32)
    x1 = x1.astype(F32)
    scale = 1.0 / (2 * half)
    mean = (jnp.sum(x0, axis=-1, keepdims=True) + jnp.sum(x1, axis=-1, keepdims=True)) * scale
    x0 = x0 - mean
    x1 = x1 - mean
    moment = (
        jnp.sum(x0 * x0, axis=-1, keepdims=True) + jnp.sum(x1 * x1, axis=-1, keepdims=True)
    ) * scale
    inv = lax.rsqrt(moment + 1e-05)
    out[pl.ds(at, rows), :half] = (x0 * inv * gain[:, :half]).astype(BF16)
    out[pl.ds(at, rows), half:] = (x1 * inv * gain[:, half:]).astype(BF16)


def pack_kernel(slots, tokens, extra, near, across, far, stored, store_map, few, tail, sems):
    member = lax.axis_index("clip")
    load_map = pltpu.make_async_copy(slots, store_map, sems.at[0])
    load_few = pltpu.make_async_copy(extra, few, sems.at[1])
    load_map.start()
    load_few.start()
    copies = [
        pltpu.make_async_copy(tokens.at[s], stored.at[pl.ds(s * BLK, BLK), :], sems.at[2 + s])
        for s in range(STORE_DEV)
    ]
    load_map.wait()
    for k, (step, out) in enumerate(((1, near), (3, across), (2, far))):
        slot, _ = slot_for(store_map, member, member ^ step)
        copies.append(
            pltpu.make_async_copy(tokens.at[jnp.maximum(slot, 0)], out, sems.at[2 + STORE_DEV + k])
        )
    for copy in copies:
        copy.start()
    load_few.wait()
    width = stored.shape[1]
    tail[...] = jnp.concatenate(
        [few[0].astype(F32), jnp.zeros((PAD - NB, width), F32)], axis=0
    ).astype(BF16)
    last = pltpu.make_async_copy(tail, stored.at[pl.ds(STORED, PAD), :], sems.at[2 + 2 * STORE_DEV])
    last.start()
    for copy in copies + [last]:
        copy.wait()


def ready_kernel(slots, gain_in, w_qkv, stored, weights, query, keys, values, normed, gain, store_map, sems):
    member = lax.axis_index("clip")
    small = [
        pltpu.make_async_copy(x, y, sems.at[i])
        for i, (x, y) in enumerate(((gain_in, gain), (slots, store_map)))
    ]
    loads = [pltpu.make_async_copy(w_qkv.at[i], weights.at[i], sems.at[2 + i]) for i in range(3)]
    for load in small + loads:
        load.start()
    small[0].wait()
    gains = gain[...]
    norm_into(stored[0, STORED:, :], stored[1, STORED:, :], gains, normed, BLK, PAD)
    small[1].wait()
    slot, _ = slot_for(store_map, member, member)
    here = pl.multiple_of(jnp.maximum(slot, 0) * BLK, BLK)
    norm_into(
        stored[0, pl.ds(here, BLK), :], stored[1, pl.ds(here, BLK), :], gains, normed, 0, BLK
    )
    width = query.shape[1]
    tile = 256
    for which, out in ((0, query), (1, keys)):
        loads[which].wait()
        for j in range(0, width, tile):
            got = jnp.dot(normed[...], weights[which, :, j : j + tile], preferred_element_type=F32)
            if which == 0:
                got = got * HEAD_DIM ** (-0.5)
            out[:, j : j + tile] = got.astype(BF16)
    loads[2].wait()
    for j in range(0, width, tile):
        got = jnp.dot(normed[...], weights[2, :, j : j + tile], preferred_element_type=F32)
        for k in range(tile // BLK):
            p = j // BLK + k
            cols = slice(k * BLK, (k + 1) * BLK)
            values[p, :, :BLK] = got[:BLK, cols].T.astype(BF16)
            values[p, :, BLK:] = got[BLK:, cols].T.astype(BF16)


NT = (((1,), (1,)), ((), ()))
END = CLIP_ROWS + PAD


def token_block(query, keys, values, context, place, block, first, count):
    pairs = values.shape[0]
    low = lax.broadcasted_iota(jnp.int32, (BLK, BLK), 1) < HEAD_DIM
    real = lax.broadcasted_iota(jnp.int32, (PAD, 2 * BLK), 0) < NB
    start = pl.multiple_of(first * BLK, BLK)
    at = pl.multiple_of(block * BLK, BLK)
    seen = count * BLK
    cols = [slice(p * BLK, (p + 1) * BLK) for p in range(pairs)]
    scores = []
    for p in range(pairs):
        q = query[pl.ds(at, BLK), cols[p]]
        none = jnp.zeros_like(q)
        both = jnp.concatenate([jnp.where(low, q, none), jnp.where(low, none, q)], axis=0)
        k = jnp.concatenate([keys[pl.ds(start, seen), cols[p]], keys[CLIP_ROWS:END, cols[p]]], axis=0)
        s = lax.dot_general(k, both, NT, preferred_element_type=F32)
        scores.append((s[:seen], jnp.where(real, s[seen:], -1e30)))
    tops = [
        jnp.maximum(jnp.max(s, axis=0, keepdims=True), jnp.max(se, axis=0, keepdims=True))
        for s, se in scores
    ]
    parts = [
        jnp.concatenate([jnp.exp(s - top).astype(BF16), jnp.exp(se - top).astype(BF16)], axis=0)
        for (s, se), top in zip(scores, tops)
    ]
    sums = []
    for p in range(pairs):
        v = jnp.concatenate([values[p, :, pl.ds(start, seen)], values[p, :, CLIP_ROWS:END]], axis=1)
        sums.append(jnp.dot(v, parts[p], preferred_element_type=F32))
    for p in range(pairs):
        o = sums[p]
        total = o[BLK : BLK + 1]
        o = jnp.concatenate(
            [o[:HEAD_DIM, :BLK] / total[:, :BLK], o[HEAD_DIM:BLK, BLK:] / total[:, BLK:]], axis=0
        )
        context[place, :, cols[p]] = o.T.astype(BF16)


def visit_blocks(info, places, query, keys, values, context):
    def visit(i, carry):
        place = places[0] + i * (places[1] - places[0])
        block = info[0, place]
        length = info[0, GROUP]
        video = info[0, GROUP + 1]
        is_video = block < video
        first = jnp.where(is_video, 0, video)
        seen = jnp.where(is_video, video, length - video)
        for count in range(1, SLOT_DEV):

            @pl.when((block >= 0) & (seen == count))
            def _():
                token_block(query, keys, values, context, i, block, first, count)

        return carry

    lax.fori_loop(0, 2, visit, 0)


def attend_kernel(
    slots,
    all_lengths,
    all_videos,
    gain_in,
    arrived,
    weights,
    own_query,
    own_keys,
    own_values,
    across,
    far,
    query,
    keys,
    values,
    facts,
    normed,
    context,
    info,
    gain,
    store_map,
    lengths,
    videos,
    sems,
):
    member = lax.axis_index("clip")
    small = [
        pltpu.make_async_copy(x, y, sems.at[i])
        for i, (x, y) in enumerate(
            ((gain_in, gain), (slots, store_map), (all_lengths, lengths), (all_videos, videos))
        )
    ]
    for load in small:
        load.start()
    width = query.shape[1]
    pairs = width // BLK
    context[...] = jnp.zeros_like(context)
    small[0].wait()
    gains = gain[...]
    for k in range(GROUP - 1):
        rows = slice(k * BLK, (k + 1) * BLK)
        norm_into(arrived[0, rows, :], arrived[1, rows, :], gains, normed, k * BLK, BLK)
    for load in small[1:]:
        load.wait()
    length = lengths[member]
    video = videos[member]
    block_at = [slot_for(store_map, member ^ step, member)[1] for step in (1, 3, 2, 0)]
    row_at = [
        pl.multiple_of(jnp.where(block < 0, SLOT_DEV + 1, block) * BLK, BLK) for block in block_at
    ]
    for place in range(GROUP):
        info[0, place] = block_at[place]
    info[0, GROUP] = length
    info[0, GROUP + 1] = video
    keep = pltpu.make_async_copy(info, facts, sems.at[4])
    keep.start()

    last = GROUP - 1
    for own, out in ((own_query, query), (own_keys, keys)):
        out[pl.ds(row_at[last], BLK), :] = own[:BLK, :]
        out[CLIP_ROWS:END, :] = own[BLK:, :]
    for p in range(pairs):
        values[p, :BLK, pl.ds(row_at[last], BLK)] = own_values[p, :, :BLK]
        values[p, :BLK, CLIP_ROWS:END] = own_values[p, :, BLK:]
        values[p, BLK:, :END] = jnp.ones((PAD, END), BF16)
    tile = 256
    for which, out in ((0, query), (1, keys)):
        for j in range(0, width, tile):
            got = jnp.dot(normed[...], weights[which, :, j : j + tile], preferred_element_type=F32)
            if which == 0:
                got = got * HEAD_DIM ** (-0.5)
            got = got.astype(BF16)
            for place in range(last):
                out[pl.ds(row_at[place], BLK), j : j + tile] = got[place * BLK : (place + 1) * BLK]
    for j in range(0, width, tile):
        got = jnp.dot(normed[...], weights[2, :, j : j + tile], preferred_element_type=F32)
        for k in range(tile // BLK):
            p = j // BLK + k
            cols = slice(k * BLK, (k + 1) * BLK)
            for place in range(last):
                turned = got[place * BLK : (place + 1) * BLK, cols].T
                values[p, :BLK, pl.ds(row_at[place], BLK)] = turned.astype(BF16)
    for b in range(2, SLOT_DEV):

        @pl.when(b >= length)
        def _():
            values[:, :BLK, b * BLK : (b + 1) * BLK] = jnp.zeros((pairs, BLK, BLK), BF16)

    visit_blocks(info, (1, 2), query, keys, values, context)
    across[...] = context[0]
    far[...] = context[1]
    keep.wait()


def rest_kernel(query, keys, values, facts, near, own, context, info, sems):
    load = pltpu.make_async_copy(facts, info, sems.at[0])
    load.start()
    width = query.shape[1]
    pairs = width // BLK
    context[...] = jnp.zeros_like(context)
    load.wait()
    length = info[0, GROUP]
    video = info[0, GROUP + 1]
    visit_blocks(info, (0, 3), query, keys, values, context)
    near[...] = context[0]
    own[:BLK, :] = context[1]

    heads = width // HEAD_DIM
    sub = 8
    qe = query[CLIP_ROWS:END, :].astype(F32)[:sub]
    qe = jnp.concatenate([qe] * heads, axis=0)
    row_head = lax.broadcasted_iota(jnp.int32, (heads * sub, width), 0) // sub
    col_head = lax.broadcasted_iota(jnp.int32, (heads * sub, width), 1) // HEAD_DIM
    qe = jnp.where(row_head == col_head, qe, 0.0).astype(BF16)
    s = lax.dot_general(qe, keys[:END, :], NT, preferred_element_type=F32)
    col = lax.broadcasted_iota(jnp.int32, s.shape, 1)
    bottle = (col >= CLIP_ROWS) & (col < CLIP_ROWS + NB)
    parts = []
    for allowed in (
        bottle | (col < video * BLK),
        bottle | ((col >= video * BLK) & (col < length * BLK)),
    ):
        masked = jnp.where(allowed, s, -1e30)
        e = jnp.exp(masked - jnp.max(masked, axis=-1, keepdims=True))
        parts.append((e / jnp.sum(e, axis=-1, keepdims=True)).astype(BF16))
    first_head = lax.broadcasted_iota(jnp.int32, (sub, BLK), 1) < HEAD_DIM
    for p in range(pairs):
        rows = slice(2 * p * sub, (2 * p + 2) * sub)
        both = jnp.concatenate([parts[0][rows], parts[1][rows]], axis=0)
        o = lax.dot_general(both, values[p, :BLK, :END], NT, preferred_element_type=F32)
        o = 0.5 * (o[: 2 * sub] + o[2 * sub :])
        o = jnp.where(first_head, o[:sub], o[sub:])
        own[BLK:, p * BLK : (p + 1) * BLK] = jnp.concatenate([o, jnp.zeros_like(o)], axis=0).astype(BF16)


def feed_kernel(
    store_map,
    stored,
    own,
    arrived,
    w_out,
    w_out_other,
    gain,
    w_up,
    w_down,
    base,
    send,
    context,
    after,
    normed,
    active,
):
    member = lax.axis_index("clip")
    core = lax.axis_index("mp")
    half = base.shape[1]
    hidden = w_up.shape[1]
    sides = (core, 1 - core)
    kept = [
        (slice(s * BLK, (s + 1) * BLK), store_map[s, member] >= 0) for s in range(STORE_DEV)
    ] + [(slice(STORED, ROWS), True)]
    for s in range(STORE_DEV):
        entry = store_map[s, member]
        step = jnp.where(entry >= 0, (entry // SLOT_DEV) ^ member, -1)
        at = jnp.where(step == 1, 0, jnp.where(step == 3, 1, 2))
        at = pl.multiple_of(at * BLK, BLK)
        rows = slice(s * BLK, (s + 1) * BLK)

        @pl.when(step == 0)
        def _():
            for k in range(2):
                context[k, rows, :] = own[sides[k], :BLK, :]

        @pl.when(step > 0)
        def _():
            for k in range(2):
                context[k, rows, :] = arrived[sides[k], pl.ds(at, BLK), :]

        @pl.when(step < 0)
        def _():
            for k in range(2):
                context[k, rows, :] = jnp.zeros((BLK, half), BF16)

    for k in range(2):
        context[k, STORED:, :] = own[sides[k], BLK:, :]

    tile = 256
    for j in range(0, 2 * half, tile):
        got = jnp.dot(context[0], w_out[:, j : j + tile], preferred_element_type=F32)
        got = got + jnp.dot(context[1], w_out_other[:, j : j + tile], preferred_element_type=F32)
        side, off = divmod(j, half)
        got = got + stored[side, :, off : off + tile].astype(F32)
        after[:, j : j + tile] = got.astype(BF16)
    gains = gain[...]
    for r in range(0, ROWS, 80):
        norm_into(after[r : r + 80, :half], after[r : r + 80, half:], gains, normed, r, 80)
    for j in range(0, hidden, tile):
        got = jnp.dot(normed[...], w_up[:, j : j + tile], preferred_element_type=F32)
        active[:, j : j + tile] = jax.nn.gelu(got, approximate=True).astype(BF16)
    for j in range(0, half, tile):
        other = pl.multiple_of((1 - core) * half + j, tile)
        got = jnp.dot(active[...], w_down[:, pl.ds(other, tile)], preferred_element_type=F32)
        for rows, keep in kept:
            send[rows, j : j + tile] = jnp.where(keep, got[rows], 0.0).astype(BF16)
        mine = pl.multiple_of(core * half + j, tile)
        got = jnp.dot(active[...], w_down[:, pl.ds(mine, tile)], preferred_element_type=F32)
        got = got + after[:, pl.ds(mine, tile)].astype(F32)
        for rows, keep in kept:
            base[rows, j : j + tile] = jnp.where(keep, got[rows], 0.0)


def finish_kernel(base, sums, mixed, merged):
    other = 1 - lax.axis_index("mp")
    for s in range(STORE_DEV):
        rows = slice(s * BLK, (s + 1) * BLK)
        mixed[s] = (base[rows, :] + sums[other, rows, :].astype(F32)).astype(BF16)
    got = base[STORED:, :] + sums[other, STORED:, :].astype(F32)
    merged[0] = got[:NB].astype(BF16)


def stay(x):
    return pltpu.with_memory_space_constraint(x, pltpu.HBM)


def ready(slots, gain1, w_qkv, stored_all):
    model = w_qkv.shape[1]
    width = w_qkv.shape[2]
    pairs = width // BLK
    return pl.pallas_call(
        ready_kernel,
        name="ready",
        out_shape=(
            spec(w_qkv.shape),
            spec((BLK + PAD, width)),
            spec((BLK + PAD, width)),
            spec((pairs, BLK, BLK + PAD)),
        ),
        in_specs=[HBM, HBM, HBM, VMEM],
        out_specs=(VMEM,) * 4,
        scratch_shapes=[
            pltpu.VMEM((BLK + PAD, model), BF16),
            pltpu.VMEM((1, model), F32),
            pltpu.SMEM(slots.shape, jnp.int32),
            DMA((5,)),
        ],
        compiler_params=pltpu.CompilerParams(vmem_limit_bytes=8 << 20),
        cost_estimate=pl.CostEstimate(flops=450000000, bytes_accessed=4000000, transcendentals=0),
    )(stay(slots), stay(gain1), stay(w_qkv), stored_all)


def attend(slots, clip_lengths, video_blocks, gain1, arrived, weights, own_qkv):
    model = weights.shape[1]
    width = weights.shape[2]
    pairs = width // BLK
    rows = CLIP_ROWS + 2 * BLK
    block = spec((BLK, width))
    info = (1, 2 * GROUP)
    return pl.pallas_call(
        attend_kernel,
        name="attend",
        out_shape=(
            block,
            block,
            spec((rows, width)),
            spec((rows, width)),
            spec((pairs, BLK + PAD, rows)),
            spec(info, jnp.int32),
        ),
        in_specs=[HBM] * 4 + [VMEM] * 5,
        out_specs=(VMEM,) * 6,
        scratch_shapes=[
            pltpu.VMEM(((GROUP - 1) * BLK, model), BF16),
            pltpu.VMEM((2, BLK, width), BF16),
            pltpu.SMEM(info, jnp.int32),
            pltpu.VMEM((1, model), F32),
            pltpu.SMEM(slots.shape, jnp.int32),
            pltpu.SMEM(clip_lengths.shape, jnp.int32),
            pltpu.SMEM(video_blocks.shape, jnp.int32),
            DMA((5,)),
        ],
        compiler_params=pltpu.CompilerParams(vmem_limit_bytes=16 << 20),
        cost_estimate=pl.CostEstimate(flops=1800000000, bytes_accessed=6000000, transcendentals=1500000),
    )(
        stay(slots),
        stay(clip_lengths),
        stay(video_blocks),
        stay(gain1),
        arrived,
        weights,
        *own_qkv,
    )


def rest(query, keys, values, facts):
    width = query.shape[1]
    info = (1, 2 * GROUP)
    return pl.pallas_call(
        rest_kernel,
        name="rest",
        out_shape=(spec((BLK, width)), spec((BLK + PAD, width))),
        in_specs=[VMEM] * 4,
        out_specs=(VMEM,) * 2,
        scratch_shapes=[
            pltpu.VMEM((2, BLK, width), BF16),
            pltpu.SMEM(info, jnp.int32),
            DMA((1,)),
        ],
        compiler_params=pltpu.CompilerParams(vmem_limit_bytes=16 << 20),
        cost_estimate=pl.CostEstimate(flops=700000000, bytes_accessed=3000000, transcendentals=1500000),
    )(query, keys, values, facts)


def feed(slots, stored_all, own_all, arrived, w_out, w_out_other, gain2, w_up, w_down):
    width = stored_all.shape[2]
    model = 2 * width
    hidden = w_up.shape[1]
    return pl.pallas_call(
        feed_kernel,
        name="feed",
        out_shape=(spec((ROWS, width), F32), spec((ROWS, width))),
        in_specs=[SMEM] + [VMEM] * 8,
        out_specs=(VMEM,) * 2,
        scratch_shapes=[
            pltpu.VMEM((2, ROWS, width), BF16),
            pltpu.VMEM((ROWS, model), BF16),
            pltpu.VMEM((ROWS, model), BF16),
            pltpu.VMEM((ROWS, hidden), BF16),
        ],
        compiler_params=pltpu.CompilerParams(vmem_limit_bytes=16 << 20),
        cost_estimate=pl.CostEstimate(flops=4100000000, bytes_accessed=14000000, transcendentals=820000),
    )(slots, stored_all, own_all, arrived, w_out, w_out_other, gain2, w_up, w_down)


def body(
    tokens,
    bottleneck,
    clip_lengths,
    video_blocks,
    store_map,
    norm1_gain,
    w_qkv,
    w_out,
    norm2_gain,
    w_up,
    w_down,
):
    width = tokens.shape[2]
    model = 2 * width
    gain1 = norm1_gain.reshape(1, model)
    gain2 = norm2_gain.reshape(1, model)
    block = spec((BLK, width))
    slots = store_map.T

    near, across, far, stored = pl.pallas_call(
        pack_kernel,
        name="pack",
        out_shape=(block, block, block, spec((ROWS, width))),
        in_specs=[HBM, HBM, HBM],
        out_specs=(HBM,) * 4,
        scratch_shapes=[
            pltpu.SMEM(slots.shape, jnp.int32),
            pltpu.VMEM(bottleneck.shape, BF16),
            pltpu.VMEM((PAD, width), BF16),
            DMA((2 * STORE_DEV + 3,)),
        ],
        compiler_params=pltpu.CompilerParams(vmem_limit_bytes=4 << 20),
    )(stay(slots), stay(tokens), stay(bottleneck))
    across = partner(across, 3)
    far = partner(far, 2)
    near = partner(near, 1)
    stored_all = lax.all_gather(stored, "mp", axis=0)
    stored_all, w_out_late = lax.optimization_barrier((stored_all, w_out))
    w_out_other = lax.ppermute(w_out_late, "mp", [(0, 1), (1, 0)])
    weights, *own_qkv = ready(slots, gain1, w_qkv, stored_all)
    arrived = lax.all_gather(jnp.concatenate([near, across, far], axis=0), "mp", axis=0)

    across, far, query, keys, values, facts = attend(
        slots, clip_lengths, video_blocks, gain1, arrived, weights, own_qkv
    )
    far = partner(far, 2)
    across = partner(across, 3)
    near, own = rest(query, keys, values, facts)
    near = partner(near, 1)
    own, far = lax.optimization_barrier((own, far))
    own_all = lax.all_gather(own, "mp", axis=0)
    arrived = lax.all_gather(jnp.concatenate([near, across, far], axis=0), "mp", axis=0)

    base, send = feed(
        slots, stored_all, own_all, arrived, w_out, w_out_other, gain2, w_up, w_down
    )
    sums = lax.all_gather(send, "mp", axis=0)

    mixed, merged = pl.pallas_call(
        finish_kernel,
        name="finish",
        out_shape=(spec(tokens.shape), spec(bottleneck.shape)),
        in_specs=[VMEM, VMEM],
        out_specs=(VMEM,) * 2,
        compiler_params=pltpu.CompilerParams(vmem_limit_bytes=8 << 20),
    )(base, sums)
    return mixed, merged


def solution(mesh):
    placed = (
        P("clip", None, "mp"),
        P("clip", None, "mp"),
        P(),
        P(),
        P(),
        P(),
        P(None, None, "mp"),
        P("mp", None),
        P(),
        P(None, "mp"),
        P("mp", None),
    )
    return jax.shard_map(
        body,
        mesh=mesh,
        in_specs=placed,
        out_specs=(P("clip", None, "mp"), P("clip", None, "mp")),
        check_vma=False,
    )
```

```python
import jax
import jax.numpy as jnp
from jax import lax
from jax.experimental import pallas as pl
from jax.experimental.pallas import tpu as pltpu
from jax.sharding import PartitionSpec as P

HEAD_DIM = 64
BLK = 128
NB = 4
SLOT_DEV = 4
STORE_DEV = 3
GROUP = 4
PAD = 16
STORED = STORE_DEV * BLK
ROWS = STORED + PAD
CLIP_ROWS = SLOT_DEV * BLK
STEPS = (2, 1, 3)
BF16 = jnp.bfloat16
F32 = jnp.float32

VMEM = pl.BlockSpec(memory_space=pltpu.VMEM)
HBM = pl.BlockSpec(memory_space=pltpu.HBM)
DMA = pltpu.SemaphoreType.DMA
SMEM = pl.BlockSpec(memory_space=pltpu.SMEM)


def spec(shape, dtype=BF16):
    return jax.ShapeDtypeStruct(shape, dtype)


def partner(x, step):
    return lax.ppermute(x, "clip", [(i, i ^ step) for i in range(lax.axis_size("clip"))])


def slot_for(store_map, device, owner):
    slot = jnp.int32(-1)
    block = jnp.int32(-1)
    for s in range(STORE_DEV):
        entry = store_map[s, device]
        hit = (entry >= 0) & (entry // SLOT_DEV == owner)
        slot = jnp.where(hit, s, slot)
        block = jnp.where(hit, entry % SLOT_DEV, block)
    return slot, block


def norm_into(x0, x1, gain, out, at, rows):
    half = x0.shape[1]
    x0 = x0.astype(F32)
    x1 = x1.astype(F32)
    scale = 1.0 / (2 * half)
    mean = (jnp.sum(x0, axis=-1, keepdims=True) + jnp.sum(x1, axis=-1, keepdims=True)) * scale
    x0 = x0 - mean
    x1 = x1 - mean
    moment = (
        jnp.sum(x0 * x0, axis=-1, keepdims=True) + jnp.sum(x1 * x1, axis=-1, keepdims=True)
    ) * scale
    inv = lax.rsqrt(moment + 1e-05)
    out[pl.ds(at, rows), :half] = (x0 * inv * gain[:, :half]).astype(BF16)
    out[pl.ds(at, rows), half:] = (x1 * inv * gain[:, half:]).astype(BF16)


def pack_kernel(slots, tokens, extra, far, near, across, stored, store_map, blocks, few, sems):
    member = lax.axis_index("clip")
    loads = [
        pltpu.make_async_copy(x, y, sems.at[i])
        for i, (x, y) in enumerate(((slots, store_map), (tokens, blocks), (extra, few)))
    ]
    for load in loads:
        load.start()
    for load in loads:
        load.wait()
    for step, out in zip(STEPS, (far, near, across)):
        slot, _ = slot_for(store_map, member, member ^ step)
        out[...] = blocks[jnp.maximum(slot, 0)]
    for s in range(STORE_DEV):
        stored[s * BLK : (s + 1) * BLK, :] = blocks[s]
    width = stored.shape[1]
    stored[STORED:, :] = jnp.concatenate(
        [few[0].astype(F32), jnp.zeros((PAD - NB, width), F32)], axis=0
    ).astype(BF16)


def ready_kernel(
    slots,
    all_lengths,
    all_videos,
    gain_in,
    w_qkv,
    stored,
    weights,
    query,
    keys,
    values,
    gain,
    facts,
    normed,
    info,
    store_map,
    lengths,
    videos,
    sems,
):
    member = lax.axis_index("clip")
    small = [
        pltpu.make_async_copy(x, y, sems.at[i])
        for i, (x, y) in enumerate(
            ((gain_in, gain), (slots, store_map), (all_lengths, lengths), (all_videos, videos))
        )
    ]
    loads = [pltpu.make_async_copy(w_qkv.at[i], weights.at[i], sems.at[5 + i]) for i in range(3)]
    for load in small + loads:
        load.start()
    small[0].wait()
    gains = gain[...]
    norm_into(stored[0, STORED:, :], stored[1, STORED:, :], gains, normed, BLK, PAD)
    for load in small[1:]:
        load.wait()
    slot, block = slot_for(store_map, member, member)
    for place, step in enumerate(STEPS):
        info[0, place] = slot_for(store_map, member ^ step, member)[1]
    info[0, GROUP - 1] = block
    info[0, GROUP] = lengths[member]
    info[0, GROUP + 1] = videos[member]
    keep = pltpu.make_async_copy(info, facts, sems.at[4])
    keep.start()
    here = pl.multiple_of(jnp.maximum(slot, 0) * BLK, BLK)
    norm_into(
        stored[0, pl.ds(here, BLK), :], stored[1, pl.ds(here, BLK), :], gains, normed, 0, BLK
    )
    width = query.shape[1]
    tile = 256
    for which, out in ((0, query), (1, keys)):
        loads[which].wait()
        for j in range(0, width, tile):
            got = jnp.dot(normed[...], weights[which, :, j : j + tile], preferred_element_type=F32)
            if which == 0:
                got = got * HEAD_DIM ** (-0.5)
            out[:, j : j + tile] = got.astype(BF16)
    loads[2].wait()
    for j in range(0, width, tile):
        got = jnp.dot(normed[...], weights[2, :, j : j + tile], preferred_element_type=F32)
        for k in range(tile // BLK):
            p = j // BLK + k
            cols = slice(k * BLK, (k + 1) * BLK)
            values[p, :, :BLK] = got[:BLK, cols].T.astype(BF16)
            values[p, :, BLK:] = got[BLK:, cols].T.astype(BF16)
    keep.wait()


NT = (((1,), (1,)), ((), ()))
END = CLIP_ROWS + PAD


def token_block(query, keys, values, context, place, block, first, count):
    pairs = values.shape[0]
    low = lax.broadcasted_iota(jnp.int32, (BLK, BLK), 1) < HEAD_DIM
    real = lax.broadcasted_iota(jnp.int32, (PAD, 2 * BLK), 0) < NB
    start = pl.multiple_of(first * BLK, BLK)
    at = pl.multiple_of(block * BLK, BLK)
    seen = count * BLK
    cols = [slice(p * BLK, (p + 1) * BLK) for p in range(pairs)]
    scores = []
    for p in range(pairs):
        q = query[pl.ds(at, BLK), cols[p]]
        none = jnp.zeros_like(q)
        both = jnp.concatenate([jnp.where(low, q, none), jnp.where(low, none, q)], axis=0)
        k = jnp.concatenate([keys[pl.ds(start, seen), cols[p]], keys[CLIP_ROWS:END, cols[p]]], axis=0)
        s = lax.dot_general(k, both, NT, preferred_element_type=F32)
        scores.append((s[:seen], jnp.where(real, s[seen:], -1e30)))
    tops = [
        jnp.maximum(jnp.max(s, axis=0, keepdims=True), jnp.max(se, axis=0, keepdims=True))
        for s, se in scores
    ]
    parts = [
        jnp.concatenate([jnp.exp(s - top).astype(BF16), jnp.exp(se - top).astype(BF16)], axis=0)
        for (s, se), top in zip(scores, tops)
    ]
    sums = []
    for p in range(pairs):
        v = jnp.concatenate([values[p, :, pl.ds(start, seen)], values[p, :, CLIP_ROWS:END]], axis=1)
        sums.append(jnp.dot(v, parts[p], preferred_element_type=F32))
    for p in range(pairs):
        o = sums[p]
        total = o[BLK : BLK + 1]
        o = jnp.concatenate(
            [o[:HEAD_DIM, :BLK] / total[:, :BLK], o[HEAD_DIM:BLK, BLK:] / total[:, BLK:]], axis=0
        )
        context[place, :, cols[p]] = o.T.astype(BF16)


def visit_blocks(info, places, query, keys, values, context):
    def visit(i, carry):
        place = places[0] + i * (places[1] - places[0])
        block = info[0, place]
        length = info[0, GROUP]
        video = info[0, GROUP + 1]
        is_video = block < video
        first = jnp.where(is_video, 0, video)
        seen = jnp.where(is_video, video, length - video)
        for count in range(1, SLOT_DEV):

            @pl.when((block >= 0) & (seen == count))
            def _():
                token_block(query, keys, values, context, i, block, first, count)

        return carry

    lax.fori_loop(0, 2, visit, 0)


def attend_kernel(
    facts,
    gain,
    arrived,
    weights,
    own_query,
    own_keys,
    own_values,
    far,
    across,
    query,
    keys,
    values,
    normed,
    context,
    info,
    sems,
):
    load = pltpu.make_async_copy(facts, info, sems.at[0])
    load.start()
    width = query.shape[1]
    pairs = width // BLK
    context[...] = jnp.zeros_like(context)
    gains = gain[...]
    for k in range(GROUP - 1):
        rows = slice(k * BLK, (k + 1) * BLK)
        norm_into(arrived[0, rows, :], arrived[1, rows, :], gains, normed, k * BLK, BLK)
    load.wait()
    length = info[0, GROUP]
    row_at = []
    for place in range(GROUP):
        block = info[0, place]
        row_at.append(pl.multiple_of(jnp.where(block < 0, SLOT_DEV + 1, block) * BLK, BLK))

    last = GROUP - 1
    for own, out in ((own_query, query), (own_keys, keys)):
        out[pl.ds(row_at[last], BLK), :] = own[:BLK, :]
        out[CLIP_ROWS:END, :] = own[BLK:, :]
    for p in range(pairs):
        values[p, :BLK, pl.ds(row_at[last], BLK)] = own_values[p, :, :BLK]
        values[p, :BLK, CLIP_ROWS:END] = own_values[p, :, BLK:]
        values[p, BLK:, :END] = jnp.ones((PAD, END), BF16)
    tile = 256
    for which, out in ((0, query), (1, keys)):
        for j in range(0, width, tile):
            got = jnp.dot(normed[...], weights[which, :, j : j + tile], preferred_element_type=F32)
            if which == 0:
                got = got * HEAD_DIM ** (-0.5)
            got = got.astype(BF16)
            for place in range(last):
                out[pl.ds(row_at[place], BLK), j : j + tile] = got[place * BLK : (place + 1) * BLK]
    for j in range(0, width, tile):
        got = jnp.dot(normed[...], weights[2, :, j : j + tile], preferred_element_type=F32)
        for k in range(tile // BLK):
            p = j // BLK + k
            cols = slice(k * BLK, (k + 1) * BLK)
            for place in range(last):
                turned = got[place * BLK : (place + 1) * BLK, cols].T
                values[p, :BLK, pl.ds(row_at[place], BLK)] = turned.astype(BF16)
    for b in range(2, SLOT_DEV):

        @pl.when(b >= length)
        def _():
            values[:, :BLK, b * BLK : (b + 1) * BLK] = jnp.zeros((pairs, BLK, BLK), BF16)

    visit_blocks(info, (0, 2), query, keys, values, context)
    far[...] = context[0]
    across[...] = context[1]


def rest_kernel(query, keys, values, facts, near, own, context, info, sems):
    load = pltpu.make_async_copy(facts, info, sems.at[0])
    load.start()
    width = query.shape[1]
    pairs = width // BLK
    context[...] = jnp.zeros_like(context)
    load.wait()
    length = info[0, GROUP]
    video = info[0, GROUP + 1]
    visit_blocks(info, (1, 3), query, keys, values, context)
    near[...] = context[0]
    own[:BLK, :] = context[1]

    heads = width // HEAD_DIM
    sub = 8
    qe = query[CLIP_ROWS:END, :].astype(F32)[:sub]
    qe = jnp.concatenate([qe] * heads, axis=0)
    row_head = lax.broadcasted_iota(jnp.int32, (heads * sub, width), 0) // sub
    col_head = lax.broadcasted_iota(jnp.int32, (heads * sub, width), 1) // HEAD_DIM
    qe = jnp.where(row_head == col_head, qe, 0.0).astype(BF16)
    s = lax.dot_general(qe, keys[:END, :], NT, preferred_element_type=F32)
    col = lax.broadcasted_iota(jnp.int32, s.shape, 1)
    bottle = (col >= CLIP_ROWS) & (col < CLIP_ROWS + NB)
    parts = []
    for allowed in (
        bottle | (col < video * BLK),
        bottle | ((col >= video * BLK) & (col < length * BLK)),
    ):
        masked = jnp.where(allowed, s, -1e30)
        e = jnp.exp(masked - jnp.max(masked, axis=-1, keepdims=True))
        parts.append((e / jnp.sum(e, axis=-1, keepdims=True)).astype(BF16))
    first_head = lax.broadcasted_iota(jnp.int32, (sub, BLK), 1) < HEAD_DIM
    for p in range(pairs):
        rows = slice(2 * p * sub, (2 * p + 2) * sub)
        both = jnp.concatenate([parts[0][rows], parts[1][rows]], axis=0)
        o = lax.dot_general(both, values[p, :BLK, :END], NT, preferred_element_type=F32)
        o = 0.5 * (o[: 2 * sub] + o[2 * sub :])
        o = jnp.where(first_head, o[:sub], o[sub:])
        own[BLK:, p * BLK : (p + 1) * BLK] = jnp.concatenate([o, jnp.zeros_like(o)], axis=0).astype(BF16)


def feed_kernel(
    store_map,
    stored,
    own,
    arrived,
    w_out,
    w_out_other,
    gain,
    w_up,
    w_down,
    base,
    send,
    context,
    after,
    normed,
    active,
):
    member = lax.axis_index("clip")
    core = lax.axis_index("mp")
    half = base.shape[1]
    hidden = w_up.shape[1]
    sides = (core, 1 - core)
    kept = [
        (slice(s * BLK, (s + 1) * BLK), store_map[s, member] >= 0) for s in range(STORE_DEV)
    ] + [(slice(STORED, ROWS), True)]
    for s in range(STORE_DEV):
        entry = store_map[s, member]
        step = jnp.where(entry >= 0, (entry // SLOT_DEV) ^ member, -1)
        at = jnp.where(step == STEPS[0], 0, jnp.where(step == STEPS[1], 1, 2))
        at = pl.multiple_of(at * BLK, BLK)
        rows = slice(s * BLK, (s + 1) * BLK)

        @pl.when(step == 0)
        def _():
            for k in range(2):
                context[k, rows, :] = own[sides[k], :BLK, :]

        @pl.when(step > 0)
        def _():
            for k in range(2):
                context[k, rows, :] = arrived[sides[k], pl.ds(at, BLK), :]

        @pl.when(step < 0)
        def _():
            for k in range(2):
                context[k, rows, :] = jnp.zeros((BLK, half), BF16)

    for k in range(2):
        context[k, STORED:, :] = own[sides[k], BLK:, :]

    tile = 256
    for j in range(0, 2 * half, tile):
        got = jnp.dot(context[0], w_out[:, j : j + tile], preferred_element_type=F32)
        got = got + jnp.dot(context[1], w_out_other[:, j : j + tile], preferred_element_type=F32)
        side, off = divmod(j, half)
        got = got + stored[side, :, off : off + tile].astype(F32)
        after[:, j : j + tile] = got.astype(BF16)
    gains = gain[...]
    for r in range(0, ROWS, 80):
        norm_into(after[r : r + 80, :half], after[r : r + 80, half:], gains, normed, r, 80)
    for j in range(0, hidden, tile):
        got = jnp.dot(normed[...], w_up[:, j : j + tile], preferred_element_type=F32)
        active[:, j : j + tile] = jax.nn.gelu(got, approximate=True).astype(BF16)
    for j in range(0, half, tile):
        other = pl.multiple_of((1 - core) * half + j, tile)
        got = jnp.dot(active[...], w_down[:, pl.ds(other, tile)], preferred_element_type=F32)
        for rows, keep in kept:
            send[rows, j : j + tile] = jnp.where(keep, got[rows], 0.0).astype(BF16)
        mine = pl.multiple_of(core * half + j, tile)
        got = jnp.dot(active[...], w_down[:, pl.ds(mine, tile)], preferred_element_type=F32)
        got = got + after[:, pl.ds(mine, tile)].astype(F32)
        for rows, keep in kept:
            base[rows, j : j + tile] = jnp.where(keep, got[rows], 0.0)


def finish_kernel(base, sums, mixed, merged):
    other = 1 - lax.axis_index("mp")
    for s in range(STORE_DEV):
        rows = slice(s * BLK, (s + 1) * BLK)
        mixed[s] = (base[rows, :] + sums[other, rows, :].astype(F32)).astype(BF16)
    got = base[STORED:, :] + sums[other, STORED:, :].astype(F32)
    merged[0] = got[:NB].astype(BF16)


def stay(x):
    return pltpu.with_memory_space_constraint(x, pltpu.HBM)


def ready(slots, clip_lengths, video_blocks, gain1, w_qkv, stored_all):
    model = w_qkv.shape[1]
    width = w_qkv.shape[2]
    pairs = width // BLK
    info = (1, 2 * GROUP)
    return pl.pallas_call(
        ready_kernel,
        name="ready",
        out_shape=(
            spec(w_qkv.shape),
            spec((BLK + PAD, width)),
            spec((BLK + PAD, width)),
            spec((pairs, BLK, BLK + PAD)),
            spec((1, model), F32),
            spec(info, jnp.int32),
        ),
        in_specs=[HBM] * 5 + [VMEM],
        out_specs=(VMEM,) * 6,
        scratch_shapes=[
            pltpu.VMEM((BLK + PAD, model), BF16),
            pltpu.SMEM(info, jnp.int32),
            pltpu.SMEM(slots.shape, jnp.int32),
            pltpu.SMEM(clip_lengths.shape, jnp.int32),
            pltpu.SMEM(video_blocks.shape, jnp.int32),
            DMA((8,)),
        ],
        compiler_params=pltpu.CompilerParams(vmem_limit_bytes=8 << 20),
        cost_estimate=pl.CostEstimate(flops=450000000, bytes_accessed=4000000, transcendentals=0),
    )(stay(slots), stay(clip_lengths), stay(video_blocks), stay(gain1), stay(w_qkv), stored_all)


def attend(facts, gain, arrived, weights, own_qkv):
    model = weights.shape[1]
    width = weights.shape[2]
    pairs = width // BLK
    rows = CLIP_ROWS + 2 * BLK
    block = spec((BLK, width))
    return pl.pallas_call(
        attend_kernel,
        name="attend",
        out_shape=(
            block,
            block,
            spec((rows, width)),
            spec((rows, width)),
            spec((pairs, BLK + PAD, rows)),
        ),
        in_specs=[VMEM] * 7,
        out_specs=(VMEM,) * 5,
        scratch_shapes=[
            pltpu.VMEM(((GROUP - 1) * BLK, model), BF16),
            pltpu.VMEM((2, BLK, width), BF16),
            pltpu.SMEM(facts.shape, jnp.int32),
            DMA((1,)),
        ],
        compiler_params=pltpu.CompilerParams(vmem_limit_bytes=16 << 20),
        cost_estimate=pl.CostEstimate(flops=1800000000, bytes_accessed=6000000, transcendentals=1500000),
    )(facts, gain, arrived, weights, *own_qkv)


def rest(query, keys, values, facts):
    width = query.shape[1]
    info = (1, 2 * GROUP)
    return pl.pallas_call(
        rest_kernel,
        name="rest",
        out_shape=(spec((BLK, width)), spec((BLK + PAD, width))),
        in_specs=[VMEM] * 4,
        out_specs=(VMEM,) * 2,
        scratch_shapes=[
            pltpu.VMEM((2, BLK, width), BF16),
            pltpu.SMEM(info, jnp.int32),
            DMA((1,)),
        ],
        compiler_params=pltpu.CompilerParams(vmem_limit_bytes=16 << 20),
        cost_estimate=pl.CostEstimate(flops=700000000, bytes_accessed=3000000, transcendentals=1500000),
    )(query, keys, values, facts)


def feed(slots, stored_all, own_all, arrived, w_out, w_out_other, gain2, w_up, w_down):
    width = stored_all.shape[2]
    model = 2 * width
    hidden = w_up.shape[1]
    return pl.pallas_call(
        feed_kernel,
        name="feed",
        out_shape=(spec((ROWS, width), F32), spec((ROWS, width))),
        in_specs=[SMEM] + [VMEM] * 8,
        out_specs=(VMEM,) * 2,
        scratch_shapes=[
            pltpu.VMEM((2, ROWS, width), BF16),
            pltpu.VMEM((ROWS, model), BF16),
            pltpu.VMEM((ROWS, model), BF16),
            pltpu.VMEM((ROWS, hidden), BF16),
        ],
        compiler_params=pltpu.CompilerParams(vmem_limit_bytes=16 << 20),
        cost_estimate=pl.CostEstimate(flops=4100000000, bytes_accessed=14000000, transcendentals=820000),
    )(slots, stored_all, own_all, arrived, w_out, w_out_other, gain2, w_up, w_down)


def body(
    tokens,
    bottleneck,
    clip_lengths,
    video_blocks,
    store_map,
    norm1_gain,
    w_qkv,
    w_out,
    norm2_gain,
    w_up,
    w_down,
):
    width = tokens.shape[2]
    model = 2 * width
    gain1 = norm1_gain.reshape(1, model)
    gain2 = norm2_gain.reshape(1, model)
    block = spec((BLK, width))
    slots = store_map.T

    far, near, across, stored = pl.pallas_call(
        pack_kernel,
        name="pack",
        out_shape=(block, block, block, spec((ROWS, width))),
        in_specs=[HBM, HBM, HBM],
        out_specs=(VMEM,) * 4,
        scratch_shapes=[
            pltpu.SMEM(slots.shape, jnp.int32),
            pltpu.VMEM(tokens.shape, BF16),
            pltpu.VMEM(bottleneck.shape, BF16),
            DMA((3,)),
        ],
        compiler_params=pltpu.CompilerParams(vmem_limit_bytes=4 << 20),
    )(stay(slots), stay(tokens), stay(bottleneck))
    far = partner(far, 2)
    near = partner(near, 1)
    across = partner(across, 3)
    stored_all = lax.all_gather(stored, "mp", axis=0)
    stored_all, w_out_late = lax.optimization_barrier((stored_all, w_out))
    w_out_other = lax.ppermute(w_out_late, "mp", [(0, 1), (1, 0)])
    weights, *own_qkv, gain, facts = ready(
        slots, clip_lengths, video_blocks, gain1, w_qkv, stored_all
    )
    arrived = lax.all_gather(jnp.concatenate([far, near, across], axis=0), "mp", axis=0)

    far, across, query, keys, values = attend(facts, gain, arrived, weights, own_qkv)
    far = partner(far, 2)
    across = partner(across, 3)
    near, own = rest(query, keys, values, facts)
    near = partner(near, 1)
    own, far = lax.optimization_barrier((own, far))
    own_all = lax.all_gather(own, "mp", axis=0)
    arrived = lax.all_gather(jnp.concatenate([far, near, across], axis=0), "mp", axis=0)

    base, send = feed(
        slots, stored_all, own_all, arrived, w_out, w_out_other, gain2, w_up, w_down
    )
    sums = lax.all_gather(send, "mp", axis=0)

    mixed, merged = pl.pallas_call(
        finish_kernel,
        name="finish",
        out_shape=(spec(tokens.shape), spec(bottleneck.shape)),
        in_specs=[VMEM, VMEM],
        out_specs=(VMEM,) * 2,
        compiler_params=pltpu.CompilerParams(vmem_limit_bytes=8 << 20),
    )(base, sums)
    return mixed, merged


def solution(mesh):
    placed = (
        P("clip", None, "mp"),
        P("clip", None, "mp"),
        P(),
        P(),
        P(),
        P(),
        P(None, None, "mp"),
        P("mp", None),
        P(),
        P(None, "mp"),
        P("mp", None),
    )
    return jax.shard_map(
        body,
        mesh=mesh,
        in_specs=placed,
        out_specs=(P("clip", None, "mp"), P("clip", None, "mp")),
        check_vma=False,
    )
```

```python
import jax
import jax.numpy as jnp
from jax import lax
from jax.experimental import pallas as pl
from jax.experimental.pallas import tpu as pltpu
from jax.sharding import PartitionSpec as P

HEAD_DIM = 64
BLK = 128
NB = 4
SLOT_DEV = 4
STORE_DEV = 3
GROUP = 4
PAD = 16
STORED = STORE_DEV * BLK
ROWS = STORED + PAD
CLIP_ROWS = SLOT_DEV * BLK
STEPS = (2, 1, 3)
BF16 = jnp.bfloat16
F32 = jnp.float32

VMEM = pl.BlockSpec(memory_space=pltpu.VMEM)
HBM = pl.BlockSpec(memory_space=pltpu.HBM)
DMA = pltpu.SemaphoreType.DMA
SMEM = pl.BlockSpec(memory_space=pltpu.SMEM)


def spec(shape, dtype=BF16):
    return jax.ShapeDtypeStruct(shape, dtype)


def partner(x, step):
    return lax.ppermute(x, "clip", [(i, i ^ step) for i in range(lax.axis_size("clip"))])


def slot_for(store_map, device, owner):
    slot = jnp.int32(-1)
    block = jnp.int32(-1)
    for s in range(STORE_DEV):
        entry = store_map[s, device]
        hit = (entry >= 0) & (entry // SLOT_DEV == owner)
        slot = jnp.where(hit, s, slot)
        block = jnp.where(hit, entry % SLOT_DEV, block)
    return slot, block


def norm_into(x0, x1, gain, out, at, rows):
    half = x0.shape[1]
    x0 = x0.astype(F32)
    x1 = x1.astype(F32)
    scale = 1.0 / (2 * half)
    mean = (jnp.sum(x0, axis=-1, keepdims=True) + jnp.sum(x1, axis=-1, keepdims=True)) * scale
    x0 = x0 - mean
    x1 = x1 - mean
    moment = (
        jnp.sum(x0 * x0, axis=-1, keepdims=True) + jnp.sum(x1 * x1, axis=-1, keepdims=True)
    ) * scale
    inv = lax.rsqrt(moment + 1e-05)
    out[pl.ds(at, rows), :half] = (x0 * inv * gain[:, :half]).astype(BF16)
    out[pl.ds(at, rows), half:] = (x1 * inv * gain[:, half:]).astype(BF16)


def pack_kernel(slots, tokens, extra, far, near, across, stored, store_map, blocks, few, sems):
    member = lax.axis_index("clip")
    loads = [
        pltpu.make_async_copy(x, y, sems.at[i])
        for i, (x, y) in enumerate(((slots, store_map), (tokens, blocks), (extra, few)))
    ]
    for load in loads:
        load.start()
    for load in loads:
        load.wait()
    for step, out in zip(STEPS, (far, near, across)):
        slot, _ = slot_for(store_map, member, member ^ step)
        out[...] = blocks[jnp.maximum(slot, 0)]
    for s in range(STORE_DEV):
        stored[s * BLK : (s + 1) * BLK, :] = blocks[s]
    width = stored.shape[1]
    stored[STORED:, :] = jnp.concatenate(
        [few[0].astype(F32), jnp.zeros((PAD - NB, width), F32)], axis=0
    ).astype(BF16)


def ready_kernel(
    slots,
    all_lengths,
    all_videos,
    gain_in,
    w_qkv,
    stored,
    weights,
    query,
    keys,
    values,
    gain,
    facts,
    normed,
    info,
    store_map,
    lengths,
    videos,
    sems,
):
    member = lax.axis_index("clip")
    small = [
        pltpu.make_async_copy(x, y, sems.at[i])
        for i, (x, y) in enumerate(
            ((gain_in, gain), (slots, store_map), (all_lengths, lengths), (all_videos, videos))
        )
    ]
    loads = [pltpu.make_async_copy(w_qkv.at[i], weights.at[i], sems.at[5 + i]) for i in range(3)]
    for load in small + loads:
        load.start()
    small[0].wait()
    gains = gain[...]
    norm_into(stored[0, STORED:, :], stored[1, STORED:, :], gains, normed, BLK, PAD)
    for load in small[1:]:
        load.wait()
    slot, block = slot_for(store_map, member, member)
    for place, step in enumerate(STEPS):
        info[0, place] = slot_for(store_map, member ^ step, member)[1]
    info[0, GROUP - 1] = block
    info[0, GROUP] = lengths[member]
    info[0, GROUP + 1] = videos[member]
    keep = pltpu.make_async_copy(info, facts, sems.at[4])
    keep.start()
    here = pl.multiple_of(jnp.maximum(slot, 0) * BLK, BLK)
    norm_into(
        stored[0, pl.ds(here, BLK), :], stored[1, pl.ds(here, BLK), :], gains, normed, 0, BLK
    )
    width = query.shape[1]
    tile = 256
    for which, out in ((0, query), (1, keys)):
        loads[which].wait()
        for j in range(0, width, tile):
            got = jnp.dot(normed[...], weights[which, :, j : j + tile], preferred_element_type=F32)
            if which == 0:
                got = got * HEAD_DIM ** (-0.5)
            out[:, j : j + tile] = got.astype(BF16)
    loads[2].wait()
    for j in range(0, width, tile):
        got = jnp.dot(normed[...], weights[2, :, j : j + tile], preferred_element_type=F32)
        for k in range(tile // BLK):
            p = j // BLK + k
            cols = slice(k * BLK, (k + 1) * BLK)
            values[p, :, :BLK] = got[:BLK, cols].T.astype(BF16)
            values[p, :, BLK:] = got[BLK:, cols].T.astype(BF16)
    keep.wait()


NT = (((1,), (1,)), ((), ()))
END = CLIP_ROWS + PAD


def token_block(query, keys, values, context, place, block, first, count):
    pairs = values.shape[0]
    low = lax.broadcasted_iota(jnp.int32, (BLK, BLK), 1) < HEAD_DIM
    real = lax.broadcasted_iota(jnp.int32, (PAD, 2 * BLK), 0) < NB
    start = pl.multiple_of(first * BLK, BLK)
    at = pl.multiple_of(block * BLK, BLK)
    seen = count * BLK
    cols = [slice(p * BLK, (p + 1) * BLK) for p in range(pairs)]
    scores = []
    for p in range(pairs):
        q = query[pl.ds(at, BLK), cols[p]]
        none = jnp.zeros_like(q)
        both = jnp.concatenate([jnp.where(low, q, none), jnp.where(low, none, q)], axis=0)
        k = jnp.concatenate([keys[pl.ds(start, seen), cols[p]], keys[CLIP_ROWS:END, cols[p]]], axis=0)
        s = lax.dot_general(k, both, NT, preferred_element_type=F32)
        scores.append((s[:seen], jnp.where(real, s[seen:], -1e30)))
    tops = [
        jnp.maximum(jnp.max(s, axis=0, keepdims=True), jnp.max(se, axis=0, keepdims=True))
        for s, se in scores
    ]
    parts = [
        jnp.concatenate([jnp.exp(s - top).astype(BF16), jnp.exp(se - top).astype(BF16)], axis=0)
        for (s, se), top in zip(scores, tops)
    ]
    sums = []
    for p in range(pairs):
        v = jnp.concatenate([values[p, :, pl.ds(start, seen)], values[p, :, CLIP_ROWS:END]], axis=1)
        sums.append(jnp.dot(v, parts[p], preferred_element_type=F32))
    for p in range(pairs):
        o = sums[p]
        total = o[BLK : BLK + 1]
        o = jnp.concatenate(
            [o[:HEAD_DIM, :BLK] / total[:, :BLK], o[HEAD_DIM:BLK, BLK:] / total[:, BLK:]], axis=0
        )
        context[place, :, cols[p]] = o.T.astype(BF16)


def visit_blocks(info, places, query, keys, values, context):
    def visit(i, carry):
        place = places[0] + i * (places[-1] - places[0])
        block = info[0, place]
        length = info[0, GROUP]
        video = info[0, GROUP + 1]
        is_video = block < video
        first = jnp.where(is_video, 0, video)
        seen = jnp.where(is_video, video, length - video)
        for count in range(1, SLOT_DEV):

            @pl.when((block >= 0) & (seen == count))
            def _():
                token_block(query, keys, values, context, i, block, first, count)

        return carry

    lax.fori_loop(0, len(places), visit, 0)


def attend_kernel(
    facts,
    gain,
    arrived,
    weights,
    own_query,
    own_keys,
    own_values,
    far,
    across,
    query,
    keys,
    values,
    normed,
    context,
    info,
    sems,
):
    load = pltpu.make_async_copy(facts, info, sems.at[0])
    load.start()
    width = query.shape[1]
    pairs = width // BLK
    context[...] = jnp.zeros_like(context)
    gains = gain[...]
    for k in range(GROUP - 1):
        rows = slice(k * BLK, (k + 1) * BLK)
        norm_into(arrived[0, rows, :], arrived[1, rows, :], gains, normed, k * BLK, BLK)
    load.wait()
    length = info[0, GROUP]
    row_at = []
    for place in range(GROUP):
        block = info[0, place]
        row_at.append(pl.multiple_of(jnp.where(block < 0, SLOT_DEV + 1, block) * BLK, BLK))

    last = GROUP - 1
    for own, out in ((own_query, query), (own_keys, keys)):
        out[pl.ds(row_at[last], BLK), :] = own[:BLK, :]
        out[CLIP_ROWS:END, :] = own[BLK:, :]
    for p in range(pairs):
        values[p, :BLK, pl.ds(row_at[last], BLK)] = own_values[p, :, :BLK]
        values[p, :BLK, CLIP_ROWS:END] = own_values[p, :, BLK:]
        values[p, BLK:, :END] = jnp.ones((PAD, END), BF16)
    tile = 256
    for which, out in ((0, query), (1, keys)):
        for j in range(0, width, tile):
            got = jnp.dot(normed[...], weights[which, :, j : j + tile], preferred_element_type=F32)
            if which == 0:
                got = got * HEAD_DIM ** (-0.5)
            got = got.astype(BF16)
            for place in range(last):
                out[pl.ds(row_at[place], BLK), j : j + tile] = got[place * BLK : (place + 1) * BLK]
    for j in range(0, width, tile):
        got = jnp.dot(normed[...], weights[2, :, j : j + tile], preferred_element_type=F32)
        for k in range(tile // BLK):
            p = j // BLK + k
            cols = slice(k * BLK, (k + 1) * BLK)
            for place in range(last):
                turned = got[place * BLK : (place + 1) * BLK, cols].T
                values[p, :BLK, pl.ds(row_at[place], BLK)] = turned.astype(BF16)
    for b in range(2, SLOT_DEV):

        @pl.when(b >= length)
        def _():
            values[:, :BLK, b * BLK : (b + 1) * BLK] = jnp.zeros((pairs, BLK, BLK), BF16)

    visit_blocks(info, (0, 2), query, keys, values, context)
    far[...] = context[0]
    across[...] = context[1]


def near_kernel(query, keys, values, facts, near, context, info, sems):
    load = pltpu.make_async_copy(facts, info, sems.at[0])
    load.start()
    context[...] = jnp.zeros_like(context)
    load.wait()
    visit_blocks(info, (1,), query, keys, values, context)
    near[...] = context[0]


def own_kernel(query, keys, values, facts, own, context, info, sems):
    load = pltpu.make_async_copy(facts, info, sems.at[0])
    load.start()
    width = query.shape[1]
    pairs = width // BLK
    context[...] = jnp.zeros_like(context)
    load.wait()
    length = info[0, GROUP]
    video = info[0, GROUP + 1]
    visit_blocks(info, (GROUP - 1,), query, keys, values, context)
    own[:BLK, :] = context[0]

    heads = width // HEAD_DIM
    sub = 8
    qe = query[CLIP_ROWS:END, :].astype(F32)[:sub]
    qe = jnp.concatenate([qe] * heads, axis=0)
    row_head = lax.broadcasted_iota(jnp.int32, (heads * sub, width), 0) // sub
    col_head = lax.broadcasted_iota(jnp.int32, (heads * sub, width), 1) // HEAD_DIM
    qe = jnp.where(row_head == col_head, qe, 0.0).astype(BF16)
    s = lax.dot_general(qe, keys[:END, :], NT, preferred_element_type=F32)
    col = lax.broadcasted_iota(jnp.int32, s.shape, 1)
    bottle = (col >= CLIP_ROWS) & (col < CLIP_ROWS + NB)
    parts = []
    for allowed in (
        bottle | (col < video * BLK),
        bottle | ((col >= video * BLK) & (col < length * BLK)),
    ):
        masked = jnp.where(allowed, s, -1e30)
        e = jnp.exp(masked - jnp.max(masked, axis=-1, keepdims=True))
        parts.append((e / jnp.sum(e, axis=-1, keepdims=True)).astype(BF16))
    first_head = lax.broadcasted_iota(jnp.int32, (sub, BLK), 1) < HEAD_DIM
    for p in range(pairs):
        rows = slice(2 * p * sub, (2 * p + 2) * sub)
        both = jnp.concatenate([parts[0][rows], parts[1][rows]], axis=0)
        o = lax.dot_general(both, values[p, :BLK, :END], NT, preferred_element_type=F32)
        o = 0.5 * (o[: 2 * sub] + o[2 * sub :])
        o = jnp.where(first_head, o[:sub], o[sub:])
        own[BLK:, p * BLK : (p + 1) * BLK] = jnp.concatenate([o, jnp.zeros_like(o)], axis=0).astype(BF16)


def feed_kernel(
    store_map,
    stored,
    own,
    arrived,
    w_out,
    w_out_other,
    gain,
    w_up,
    w_down,
    base,
    send,
    context,
    after,
    normed,
    active,
):
    member = lax.axis_index("clip")
    core = lax.axis_index("mp")
    half = base.shape[1]
    hidden = w_up.shape[1]
    sides = (core, 1 - core)
    kept = [
        (slice(s * BLK, (s + 1) * BLK), store_map[s, member] >= 0) for s in range(STORE_DEV)
    ] + [(slice(STORED, ROWS), True)]
    for s in range(STORE_DEV):
        entry = store_map[s, member]
        step = jnp.where(entry >= 0, (entry // SLOT_DEV) ^ member, -1)
        at = jnp.where(step == STEPS[0], 0, jnp.where(step == STEPS[1], 1, 2))
        at = pl.multiple_of(at * BLK, BLK)
        rows = slice(s * BLK, (s + 1) * BLK)

        @pl.when(step == 0)
        def _():
            for k in range(2):
                context[k, rows, :] = own[sides[k], :BLK, :]

        @pl.when(step > 0)
        def _():
            for k in range(2):
                context[k, rows, :] = arrived[sides[k], pl.ds(at, BLK), :]

        @pl.when(step < 0)
        def _():
            for k in range(2):
                context[k, rows, :] = jnp.zeros((BLK, half), BF16)

    for k in range(2):
        context[k, STORED:, :] = own[sides[k], BLK:, :]

    tile = 256
    for j in range(0, 2 * half, tile):
        got = jnp.dot(context[0], w_out[:, j : j + tile], preferred_element_type=F32)
        got = got + jnp.dot(context[1], w_out_other[:, j : j + tile], preferred_element_type=F32)
        side, off = divmod(j, half)
        got = got + stored[side, :, off : off + tile].astype(F32)
        after[:, j : j + tile] = got.astype(BF16)
    gains = gain[...]
    for r in range(0, ROWS, 80):
        norm_into(after[r : r + 80, :half], after[r : r + 80, half:], gains, normed, r, 80)
    for j in range(0, hidden, tile):
        got = jnp.dot(normed[...], w_up[:, j : j + tile], preferred_element_type=F32)
        active[:, j : j + tile] = jax.nn.gelu(got, approximate=True).astype(BF16)
    for j in range(0, half, tile):
        other = pl.multiple_of((1 - core) * half + j, tile)
        got = jnp.dot(active[...], w_down[:, pl.ds(other, tile)], preferred_element_type=F32)
        for rows, keep in kept:
            send[rows, j : j + tile] = jnp.where(keep, got[rows], 0.0).astype(BF16)
        mine = pl.multiple_of(core * half + j, tile)
        got = jnp.dot(active[...], w_down[:, pl.ds(mine, tile)], preferred_element_type=F32)
        got = got + after[:, pl.ds(mine, tile)].astype(F32)
        for rows, keep in kept:
            base[rows, j : j + tile] = jnp.where(keep, got[rows], 0.0)


def finish_kernel(base, sums, mixed, merged):
    other = 1 - lax.axis_index("mp")
    for s in range(STORE_DEV):
        rows = slice(s * BLK, (s + 1) * BLK)
        mixed[s] = (base[rows, :] + sums[other, rows, :].astype(F32)).astype(BF16)
    got = base[STORED:, :] + sums[other, STORED:, :].astype(F32)
    merged[0] = got[:NB].astype(BF16)


def stay(x):
    return pltpu.with_memory_space_constraint(x, pltpu.HBM)


def ready(slots, clip_lengths, video_blocks, gain1, w_qkv, stored_all):
    model = w_qkv.shape[1]
    width = w_qkv.shape[2]
    pairs = width // BLK
    info = (1, 2 * GROUP)
    return pl.pallas_call(
        ready_kernel,
        name="ready",
        out_shape=(
            spec(w_qkv.shape),
            spec((BLK + PAD, width)),
            spec((BLK + PAD, width)),
            spec((pairs, BLK, BLK + PAD)),
            spec((1, model), F32),
            spec(info, jnp.int32),
        ),
        in_specs=[HBM] * 5 + [VMEM],
        out_specs=(VMEM,) * 6,
        scratch_shapes=[
            pltpu.VMEM((BLK + PAD, model), BF16),
            pltpu.SMEM(info, jnp.int32),
            pltpu.SMEM(slots.shape, jnp.int32),
            pltpu.SMEM(clip_lengths.shape, jnp.int32),
            pltpu.SMEM(video_blocks.shape, jnp.int32),
            DMA((8,)),
        ],
        compiler_params=pltpu.CompilerParams(vmem_limit_bytes=8 << 20),
        cost_estimate=pl.CostEstimate(flops=450000000, bytes_accessed=4000000, transcendentals=0),
    )(stay(slots), stay(clip_lengths), stay(video_blocks), stay(gain1), stay(w_qkv), stored_all)


def attend(facts, gain, arrived, weights, own_qkv):
    model = weights.shape[1]
    width = weights.shape[2]
    pairs = width // BLK
    rows = CLIP_ROWS + 2 * BLK
    block = spec((BLK, width))
    return pl.pallas_call(
        attend_kernel,
        name="attend",
        out_shape=(
            block,
            block,
            spec((rows, width)),
            spec((rows, width)),
            spec((pairs, BLK + PAD, rows)),
        ),
        in_specs=[VMEM] * 7,
        out_specs=(VMEM,) * 5,
        scratch_shapes=[
            pltpu.VMEM(((GROUP - 1) * BLK, model), BF16),
            pltpu.VMEM((2, BLK, width), BF16),
            pltpu.SMEM(facts.shape, jnp.int32),
            DMA((1,)),
        ],
        compiler_params=pltpu.CompilerParams(vmem_limit_bytes=16 << 20),
        cost_estimate=pl.CostEstimate(flops=1800000000, bytes_accessed=6000000, transcendentals=1500000),
    )(facts, gain, arrived, weights, *own_qkv)


def part(kernel, name, rows, query, keys, values, facts):
    width = query.shape[1]
    return pl.pallas_call(
        kernel,
        name=name,
        out_shape=spec((rows, width)),
        in_specs=[VMEM] * 4,
        out_specs=VMEM,
        scratch_shapes=[
            pltpu.VMEM((1, BLK, width), BF16),
            pltpu.SMEM(facts.shape, jnp.int32),
            DMA((1,)),
        ],
        compiler_params=pltpu.CompilerParams(vmem_limit_bytes=16 << 20),
        cost_estimate=pl.CostEstimate(flops=400000000, bytes_accessed=3000000, transcendentals=700000),
    )(query, keys, values, facts)


def feed(slots, stored_all, own_all, arrived, w_out, w_out_other, gain2, w_up, w_down):
    width = stored_all.shape[2]
    model = 2 * width
    hidden = w_up.shape[1]
    return pl.pallas_call(
        feed_kernel,
        name="feed",
        out_shape=(spec((ROWS, width), F32), spec((ROWS, width))),
        in_specs=[SMEM] + [VMEM] * 8,
        out_specs=(VMEM,) * 2,
        scratch_shapes=[
            pltpu.VMEM((2, ROWS, width), BF16),
            pltpu.VMEM((ROWS, model), BF16),
            pltpu.VMEM((ROWS, model), BF16),
            pltpu.VMEM((ROWS, hidden), BF16),
        ],
        compiler_params=pltpu.CompilerParams(vmem_limit_bytes=16 << 20),
        cost_estimate=pl.CostEstimate(flops=4100000000, bytes_accessed=14000000, transcendentals=820000),
    )(slots, stored_all, own_all, arrived, w_out, w_out_other, gain2, w_up, w_down)


def body(
    tokens,
    bottleneck,
    clip_lengths,
    video_blocks,
    store_map,
    norm1_gain,
    w_qkv,
    w_out,
    norm2_gain,
    w_up,
    w_down,
):
    width = tokens.shape[2]
    model = 2 * width
    gain1 = norm1_gain.reshape(1, model)
    gain2 = norm2_gain.reshape(1, model)
    block = spec((BLK, width))
    slots = store_map.T

    far, near, across, stored = pl.pallas_call(
        pack_kernel,
        name="pack",
        out_shape=(block, block, block, spec((ROWS, width))),
        in_specs=[HBM, HBM, HBM],
        out_specs=(VMEM,) * 4,
        scratch_shapes=[
            pltpu.SMEM(slots.shape, jnp.int32),
            pltpu.VMEM(tokens.shape, BF16),
            pltpu.VMEM(bottleneck.shape, BF16),
            DMA((3,)),
        ],
        compiler_params=pltpu.CompilerParams(vmem_limit_bytes=4 << 20),
    )(stay(slots), stay(tokens), stay(bottleneck))
    far = partner(far, 2)
    near = partner(near, 1)
    across = partner(across, 3)
    stored_all = lax.all_gather(stored, "mp", axis=0)
    stored_all, w_out_late = lax.optimization_barrier((stored_all, w_out))
    w_out_other = lax.ppermute(w_out_late, "mp", [(0, 1), (1, 0)])
    weights, *own_qkv, gain, facts = ready(
        slots, clip_lengths, video_blocks, gain1, w_qkv, stored_all
    )
    arrived = lax.all_gather(jnp.concatenate([far, near, across], axis=0), "mp", axis=0)

    far, across, query, keys, values = attend(facts, gain, arrived, weights, own_qkv)
    far = partner(far, 2)
    across = partner(across, 3)
    near = part(near_kernel, "near", BLK, query, keys, values, facts)
    near = partner(near, 1)
    facts, far = lax.optimization_barrier((facts, far))
    own = part(own_kernel, "own", BLK + PAD, query, keys, values, facts)
    own_all = lax.all_gather(own, "mp", axis=0)
    arrived = lax.all_gather(jnp.concatenate([far, near, across], axis=0), "mp", axis=0)

    base, send = feed(
        slots, stored_all, own_all, arrived, w_out, w_out_other, gain2, w_up, w_down
    )
    sums = lax.all_gather(send, "mp", axis=0)

    mixed, merged = pl.pallas_call(
        finish_kernel,
        name="finish",
        out_shape=(spec(tokens.shape), spec(bottleneck.shape)),
        in_specs=[VMEM, VMEM],
        out_specs=(VMEM,) * 2,
        compiler_params=pltpu.CompilerParams(vmem_limit_bytes=8 << 20),
    )(base, sums)
    return mixed, merged


def solution(mesh):
    placed = (
        P("clip", None, "mp"),
        P("clip", None, "mp"),
        P(),
        P(),
        P(),
        P(),
        P(None, None, "mp"),
        P("mp", None),
        P(),
        P(None, "mp"),
        P("mp", None),
    )
    return jax.shard_map(
        body,
        mesh=mesh,
        in_specs=placed,
        out_specs=(P("clip", None, "mp"), P("clip", None, "mp")),
        check_vma=False,
    )
```

```python
import jax
import jax.numpy as jnp
from jax import lax
from jax.experimental import pallas as pl
from jax.experimental.pallas import tpu as pltpu
from jax.sharding import PartitionSpec as P

HEAD_DIM = 64
BLK = 128
NB = 4
SLOT_DEV = 4
STORE_DEV = 3
GROUP = 4
PAD = 16
STORED = STORE_DEV * BLK
ROWS = STORED + PAD
CLIP_ROWS = SLOT_DEV * BLK
STEPS = (2, 1, 3)
BF16 = jnp.bfloat16
F32 = jnp.float32

VMEM = pl.BlockSpec(memory_space=pltpu.VMEM)
HBM = pl.BlockSpec(memory_space=pltpu.HBM)
DMA = pltpu.SemaphoreType.DMA
SMEM = pl.BlockSpec(memory_space=pltpu.SMEM)


def spec(shape, dtype=BF16):
    return jax.ShapeDtypeStruct(shape, dtype)


def partner(x, step):
    return lax.ppermute(x, "clip", [(i, i ^ step) for i in range(lax.axis_size("clip"))])


def slot_for(store_map, device, owner):
    slot = jnp.int32(-1)
    block = jnp.int32(-1)
    for s in range(STORE_DEV):
        entry = store_map[s, device]
        hit = (entry >= 0) & (entry // SLOT_DEV == owner)
        slot = jnp.where(hit, s, slot)
        block = jnp.where(hit, entry % SLOT_DEV, block)
    return slot, block


def norm_into(x0, x1, gain, out, at, rows):
    half = x0.shape[1]
    x0 = x0.astype(F32)
    x1 = x1.astype(F32)
    scale = 1.0 / (2 * half)
    mean = (jnp.sum(x0, axis=-1, keepdims=True) + jnp.sum(x1, axis=-1, keepdims=True)) * scale
    x0 = x0 - mean
    x1 = x1 - mean
    moment = (
        jnp.sum(x0 * x0, axis=-1, keepdims=True) + jnp.sum(x1 * x1, axis=-1, keepdims=True)
    ) * scale
    inv = lax.rsqrt(moment + 1e-05)
    out[pl.ds(at, rows), :half] = (x0 * inv * gain[:, :half]).astype(BF16)
    out[pl.ds(at, rows), half:] = (x1 * inv * gain[:, half:]).astype(BF16)


def pack_kernel(slots, tokens, extra, far, near, across, stored, store_map, blocks, few, sems):
    member = lax.axis_index("clip")
    loads = [
        pltpu.make_async_copy(x, y, sems.at[i])
        for i, (x, y) in enumerate(((slots, store_map), (tokens, blocks), (extra, few)))
    ]
    for load in loads:
        load.start()
    for load in loads:
        load.wait()
    for step, out in zip(STEPS, (far, near, across)):
        slot, _ = slot_for(store_map, member, member ^ step)
        out[...] = blocks[jnp.maximum(slot, 0)]
    for s in range(STORE_DEV):
        stored[s * BLK : (s + 1) * BLK, :] = blocks[s]
    width = stored.shape[1]
    stored[STORED:, :] = jnp.concatenate(
        [few[0].astype(F32), jnp.zeros((PAD - NB, width), F32)], axis=0
    ).astype(BF16)


def ready_kernel(
    slots,
    all_lengths,
    all_videos,
    gain_in,
    w_qkv,
    stored,
    weights,
    query,
    keys,
    values,
    gain,
    facts,
    normed,
    info,
    store_map,
    lengths,
    videos,
    sems,
):
    member = lax.axis_index("clip")
    small = [
        pltpu.make_async_copy(x, y, sems.at[i])
        for i, (x, y) in enumerate(
            ((gain_in, gain), (slots, store_map), (all_lengths, lengths), (all_videos, videos))
        )
    ]
    loads = [pltpu.make_async_copy(w_qkv.at[i], weights.at[i], sems.at[5 + i]) for i in range(3)]
    for load in small + loads:
        load.start()
    small[0].wait()
    gains = gain[...]
    norm_into(stored[0, STORED:, :], stored[1, STORED:, :], gains, normed, BLK, PAD)
    for load in small[1:]:
        load.wait()
    slot, block = slot_for(store_map, member, member)
    for place, step in enumerate(STEPS):
        info[0, place] = slot_for(store_map, member ^ step, member)[1]
    info[0, GROUP - 1] = block
    info[0, GROUP] = lengths[member]
    info[0, GROUP + 1] = videos[member]
    keep = pltpu.make_async_copy(info, facts, sems.at[4])
    keep.start()
    here = pl.multiple_of(jnp.maximum(slot, 0) * BLK, BLK)
    norm_into(
        stored[0, pl.ds(here, BLK), :], stored[1, pl.ds(here, BLK), :], gains, normed, 0, BLK
    )
    width = query.shape[1]
    tile = 256
    for which, out in ((0, query), (1, keys)):
        loads[which].wait()
        for j in range(0, width, tile):
            got = jnp.dot(normed[...], weights[which, :, j : j + tile], preferred_element_type=F32)
            if which == 0:
                got = got * HEAD_DIM ** (-0.5)
            out[:, j : j + tile] = got.astype(BF16)
    loads[2].wait()
    for j in range(0, width, tile):
        got = jnp.dot(normed[...], weights[2, :, j : j + tile], preferred_element_type=F32)
        for k in range(tile // BLK):
            p = j // BLK + k
            cols = slice(k * BLK, (k + 1) * BLK)
            values[p, :, :BLK] = got[:BLK, cols].T.astype(BF16)
            values[p, :, BLK:] = got[BLK:, cols].T.astype(BF16)
    keep.wait()


NT = (((1,), (1,)), ((), ()))
END = CLIP_ROWS + PAD


def token_block(query, keys, values, context, place, block, first, count):
    pairs = values.shape[0]
    low = lax.broadcasted_iota(jnp.int32, (BLK, BLK), 1) < HEAD_DIM
    real = lax.broadcasted_iota(jnp.int32, (PAD, 2 * BLK), 0) < NB
    start = pl.multiple_of(first * BLK, BLK)
    at = pl.multiple_of(block * BLK, BLK)
    seen = count * BLK
    cols = [slice(p * BLK, (p + 1) * BLK) for p in range(pairs)]
    scores = []
    for p in range(pairs):
        q = query[pl.ds(at, BLK), cols[p]]
        none = jnp.zeros_like(q)
        both = jnp.concatenate([jnp.where(low, q, none), jnp.where(low, none, q)], axis=0)
        k = jnp.concatenate([keys[pl.ds(start, seen), cols[p]], keys[CLIP_ROWS:END, cols[p]]], axis=0)
        s = lax.dot_general(k, both, NT, preferred_element_type=F32)
        scores.append((s[:seen], jnp.where(real, s[seen:], -1e30)))
    tops = [
        jnp.maximum(jnp.max(s, axis=0, keepdims=True), jnp.max(se, axis=0, keepdims=True))
        for s, se in scores
    ]
    parts = [
        jnp.concatenate([jnp.exp(s - top).astype(BF16), jnp.exp(se - top).astype(BF16)], axis=0)
        for (s, se), top in zip(scores, tops)
    ]
    sums = []
    for p in range(pairs):
        v = jnp.concatenate([values[p, :, pl.ds(start, seen)], values[p, :, CLIP_ROWS:END]], axis=1)
        sums.append(jnp.dot(v, parts[p], preferred_element_type=F32))
    for p in range(pairs):
        o = sums[p]
        total = o[BLK : BLK + 1]
        o = jnp.concatenate(
            [o[:HEAD_DIM, :BLK] / total[:, :BLK], o[HEAD_DIM:BLK, BLK:] / total[:, BLK:]], axis=0
        )
        context[place, :, cols[p]] = o.T.astype(BF16)


def visit_blocks(info, places, query, keys, values, context):
    def visit(i, carry):
        place = places[0] + i * (places[-1] - places[0])
        block = info[0, place]
        length = info[0, GROUP]
        video = info[0, GROUP + 1]
        is_video = block < video
        first = jnp.where(is_video, 0, video)
        seen = jnp.where(is_video, video, length - video)
        for count in range(1, SLOT_DEV):

            @pl.when((block >= 0) & (seen == count))
            def _():
                token_block(query, keys, values, context, i, block, first, count)

        return carry

    lax.fori_loop(0, len(places), visit, 0)


def attend_kernel(
    facts,
    gain,
    arrived,
    weights,
    own_query,
    own_keys,
    own_values,
    far,
    across,
    query,
    keys,
    values,
    normed,
    context,
    info,
    sems,
):
    load = pltpu.make_async_copy(facts, info, sems.at[0])
    load.start()
    width = query.shape[1]
    pairs = width // BLK
    context[...] = jnp.zeros_like(context)
    gains = gain[...]
    for k in range(GROUP - 1):
        rows = slice(k * BLK, (k + 1) * BLK)
        norm_into(arrived[0, rows, :], arrived[1, rows, :], gains, normed, k * BLK, BLK)
    load.wait()
    length = info[0, GROUP]
    row_at = []
    for place in range(GROUP):
        block = info[0, place]
        row_at.append(pl.multiple_of(jnp.where(block < 0, SLOT_DEV + 1, block) * BLK, BLK))

    last = GROUP - 1
    for own, out in ((own_query, query), (own_keys, keys)):
        out[pl.ds(row_at[last], BLK), :] = own[:BLK, :]
        out[CLIP_ROWS:END, :] = own[BLK:, :]
    for p in range(pairs):
        values[p, :BLK, pl.ds(row_at[last], BLK)] = own_values[p, :, :BLK]
        values[p, :BLK, CLIP_ROWS:END] = own_values[p, :, BLK:]
        values[p, BLK:, :END] = jnp.ones((PAD, END), BF16)
    tile = 256
    for which, out in ((0, query), (1, keys)):
        for j in range(0, width, tile):
            got = jnp.dot(normed[...], weights[which, :, j : j + tile], preferred_element_type=F32)
            if which == 0:
                got = got * HEAD_DIM ** (-0.5)
            got = got.astype(BF16)
            for place in range(last):
                out[pl.ds(row_at[place], BLK), j : j + tile] = got[place * BLK : (place + 1) * BLK]
    for j in range(0, width, tile):
        got = jnp.dot(normed[...], weights[2, :, j : j + tile], preferred_element_type=F32)
        for k in range(tile // BLK):
            p = j // BLK + k
            cols = slice(k * BLK, (k + 1) * BLK)
            for place in range(last):
                turned = got[place * BLK : (place + 1) * BLK, cols].T
                values[p, :BLK, pl.ds(row_at[place], BLK)] = turned.astype(BF16)
    for b in range(2, SLOT_DEV):

        @pl.when(b >= length)
        def _():
            values[:, :BLK, b * BLK : (b + 1) * BLK] = jnp.zeros((pairs, BLK, BLK), BF16)

    visit_blocks(info, (0, 2), query, keys, values, context)
    far[...] = context[0]
    across[...] = context[1]


def near_kernel(query, keys, values, facts, near, context, info, sems):
    load = pltpu.make_async_copy(facts, info, sems.at[0])
    load.start()
    context[...] = jnp.zeros_like(context)
    load.wait()
    visit_blocks(info, (1,), query, keys, values, context)
    near[...] = context[0]


def own_kernel(query, keys, values, facts, own, context, info, sems):
    load = pltpu.make_async_copy(facts, info, sems.at[0])
    load.start()
    width = query.shape[1]
    pairs = width // BLK
    context[...] = jnp.zeros_like(context)
    load.wait()
    length = info[0, GROUP]
    video = info[0, GROUP + 1]
    visit_blocks(info, (GROUP - 1,), query, keys, values, context)
    own[:BLK, :] = context[0]

    heads = width // HEAD_DIM
    sub = 8
    qe = query[CLIP_ROWS:END, :].astype(F32)[:sub]
    qe = jnp.concatenate([qe] * heads, axis=0)
    row_head = lax.broadcasted_iota(jnp.int32, (heads * sub, width), 0) // sub
    col_head = lax.broadcasted_iota(jnp.int32, (heads * sub, width), 1) // HEAD_DIM
    qe = jnp.where(row_head == col_head, qe, 0.0).astype(BF16)
    s = lax.dot_general(qe, keys[:END, :], NT, preferred_element_type=F32)
    col = lax.broadcasted_iota(jnp.int32, s.shape, 1)
    bottle = (col >= CLIP_ROWS) & (col < CLIP_ROWS + NB)
    parts = []
    for allowed in (
        bottle | (col < video * BLK),
        bottle | ((col >= video * BLK) & (col < length * BLK)),
    ):
        masked = jnp.where(allowed, s, -1e30)
        e = jnp.exp(masked - jnp.max(masked, axis=-1, keepdims=True))
        parts.append((e / jnp.sum(e, axis=-1, keepdims=True)).astype(BF16))
    first_head = lax.broadcasted_iota(jnp.int32, (sub, BLK), 1) < HEAD_DIM
    for p in range(pairs):
        rows = slice(2 * p * sub, (2 * p + 2) * sub)
        both = jnp.concatenate([parts[0][rows], parts[1][rows]], axis=0)
        o = lax.dot_general(both, values[p, :BLK, :END], NT, preferred_element_type=F32)
        o = 0.5 * (o[: 2 * sub] + o[2 * sub :])
        o = jnp.where(first_head, o[:sub], o[sub:])
        own[BLK:, p * BLK : (p + 1) * BLK] = jnp.concatenate([o, jnp.zeros_like(o)], axis=0).astype(BF16)


def feed_kernel(
    store_map,
    stored,
    own,
    arrived,
    w_out,
    w_out_other,
    gain,
    w_up,
    w_down,
    base,
    send,
    context,
    after,
    normed,
    active,
):
    member = lax.axis_index("clip")
    core = lax.axis_index("mp")
    half = base.shape[1]
    hidden = w_up.shape[1]
    sides = (core, 1 - core)
    kept = [
        (slice(s * BLK, (s + 1) * BLK), store_map[s, member] >= 0) for s in range(STORE_DEV)
    ] + [(slice(STORED, ROWS), True)]
    for s in range(STORE_DEV):
        entry = store_map[s, member]
        step = jnp.where(entry >= 0, (entry // SLOT_DEV) ^ member, -1)
        at = jnp.where(step == STEPS[0], 0, jnp.where(step == STEPS[1], 1, 2))
        at = pl.multiple_of(at * BLK, BLK)
        rows = slice(s * BLK, (s + 1) * BLK)

        @pl.when(step == 0)
        def _():
            for k in range(2):
                context[k, rows, :] = own[sides[k], :BLK, :]

        @pl.when(step > 0)
        def _():
            for k in range(2):
                context[k, rows, :] = arrived[sides[k], pl.ds(at, BLK), :]

        @pl.when(step < 0)
        def _():
            for k in range(2):
                context[k, rows, :] = jnp.zeros((BLK, half), BF16)

    for k in range(2):
        context[k, STORED:, :] = own[sides[k], BLK:, :]

    tile = 256
    for j in range(0, 2 * half, tile):
        got = jnp.dot(context[0], w_out[:, j : j + tile], preferred_element_type=F32)
        got = got + jnp.dot(context[1], w_out_other[:, j : j + tile], preferred_element_type=F32)
        side, off = divmod(j, half)
        got = got + stored[side, :, off : off + tile].astype(F32)
        after[:, j : j + tile] = got.astype(BF16)
    gains = gain[...]
    for r in range(0, ROWS, 80):
        norm_into(after[r : r + 80, :half], after[r : r + 80, half:], gains, normed, r, 80)
    for j in range(0, hidden, tile):
        got = jnp.dot(normed[...], w_up[:, j : j + tile], preferred_element_type=F32)
        active[:, j : j + tile] = jax.nn.gelu(got, approximate=True).astype(BF16)
    for j in range(0, half, tile):
        other = pl.multiple_of((1 - core) * half + j, tile)
        got = jnp.dot(active[...], w_down[:, pl.ds(other, tile)], preferred_element_type=F32)
        for rows, keep in kept:
            send[rows, j : j + tile] = jnp.where(keep, got[rows], 0.0).astype(BF16)
        mine = pl.multiple_of(core * half + j, tile)
        got = jnp.dot(active[...], w_down[:, pl.ds(mine, tile)], preferred_element_type=F32)
        got = got + after[:, pl.ds(mine, tile)].astype(F32)
        for rows, keep in kept:
            base[rows, j : j + tile] = jnp.where(keep, got[rows], 0.0)


def finish_kernel(base, sums, mixed, merged):
    other = 1 - lax.axis_index("mp")
    for s in range(STORE_DEV):
        rows = slice(s * BLK, (s + 1) * BLK)
        mixed[s] = (base[rows, :] + sums[other, rows, :].astype(F32)).astype(BF16)
    got = base[STORED:, :] + sums[other, STORED:, :].astype(F32)
    merged[0] = got[:NB].astype(BF16)


def stay(x):
    return pltpu.with_memory_space_constraint(x, pltpu.HBM)


def ready(slots, clip_lengths, video_blocks, gain1, w_qkv, stored_all):
    model = w_qkv.shape[1]
    width = w_qkv.shape[2]
    pairs = width // BLK
    info = (1, 2 * GROUP)
    return pl.pallas_call(
        ready_kernel,
        name="ready",
        out_shape=(
            spec(w_qkv.shape),
            spec((BLK + PAD, width)),
            spec((BLK + PAD, width)),
            spec((pairs, BLK, BLK + PAD)),
            spec((1, model), F32),
            spec(info, jnp.int32),
        ),
        in_specs=[HBM] * 5 + [VMEM],
        out_specs=(VMEM,) * 6,
        scratch_shapes=[
            pltpu.VMEM((BLK + PAD, model), BF16),
            pltpu.SMEM(info, jnp.int32),
            pltpu.SMEM(slots.shape, jnp.int32),
            pltpu.SMEM(clip_lengths.shape, jnp.int32),
            pltpu.SMEM(video_blocks.shape, jnp.int32),
            DMA((8,)),
        ],
        compiler_params=pltpu.CompilerParams(vmem_limit_bytes=8 << 20),
        cost_estimate=pl.CostEstimate(flops=450000000, bytes_accessed=4000000, transcendentals=0),
    )(stay(slots), stay(clip_lengths), stay(video_blocks), stay(gain1), stay(w_qkv), stored_all)


def attend(facts, gain, arrived, weights, own_qkv):
    model = weights.shape[1]
    width = weights.shape[2]
    pairs = width // BLK
    rows = CLIP_ROWS + 2 * BLK
    block = spec((BLK, width))
    return pl.pallas_call(
        attend_kernel,
        name="attend",
        out_shape=(
            block,
            block,
            spec((rows, width)),
            spec((rows, width)),
            spec((pairs, BLK + PAD, rows)),
        ),
        in_specs=[VMEM] * 7,
        out_specs=(VMEM,) * 5,
        scratch_shapes=[
            pltpu.VMEM(((GROUP - 1) * BLK, model), BF16),
            pltpu.VMEM((2, BLK, width), BF16),
            pltpu.SMEM(facts.shape, jnp.int32),
            DMA((1,)),
        ],
        compiler_params=pltpu.CompilerParams(vmem_limit_bytes=16 << 20),
        cost_estimate=pl.CostEstimate(flops=1800000000, bytes_accessed=6000000, transcendentals=1500000),
    )(facts, gain, arrived, weights, *own_qkv)


def part(kernel, name, rows, query, keys, values, facts):
    width = query.shape[1]
    return pl.pallas_call(
        kernel,
        name=name,
        out_shape=spec((rows, width)),
        in_specs=[VMEM] * 4,
        out_specs=VMEM,
        scratch_shapes=[
            pltpu.VMEM((1, BLK, width), BF16),
            pltpu.SMEM(facts.shape, jnp.int32),
            DMA((1,)),
        ],
        compiler_params=pltpu.CompilerParams(vmem_limit_bytes=16 << 20),
        cost_estimate=pl.CostEstimate(flops=400000000, bytes_accessed=3000000, transcendentals=700000),
    )(query, keys, values, facts)


def feed(slots, stored_all, own_all, arrived, w_out, w_out_other, gain2, w_up, w_down):
    width = stored_all.shape[2]
    model = 2 * width
    hidden = w_up.shape[1]
    return pl.pallas_call(
        feed_kernel,
        name="feed",
        out_shape=(spec((ROWS, width), F32), spec((ROWS, width))),
        in_specs=[SMEM] + [VMEM] * 8,
        out_specs=(VMEM,) * 2,
        scratch_shapes=[
            pltpu.VMEM((2, ROWS, width), BF16),
            pltpu.VMEM((ROWS, model), BF16),
            pltpu.VMEM((ROWS, model), BF16),
            pltpu.VMEM((ROWS, hidden), BF16),
        ],
        compiler_params=pltpu.CompilerParams(vmem_limit_bytes=16 << 20),
        cost_estimate=pl.CostEstimate(flops=4100000000, bytes_accessed=14000000, transcendentals=820000),
    )(slots, stored_all, own_all, arrived, w_out, w_out_other, gain2, w_up, w_down)


def body(
    tokens,
    bottleneck,
    clip_lengths,
    video_blocks,
    store_map,
    norm1_gain,
    w_qkv,
    w_out,
    norm2_gain,
    w_up,
    w_down,
):
    width = tokens.shape[2]
    model = 2 * width
    gain1 = norm1_gain.reshape(1, model)
    gain2 = norm2_gain.reshape(1, model)
    block = spec((BLK, width))
    slots = store_map.T

    far, near, across, stored = pl.pallas_call(
        pack_kernel,
        name="pack",
        out_shape=(block, block, block, spec((ROWS, width))),
        in_specs=[HBM, HBM, HBM],
        out_specs=(VMEM,) * 4,
        scratch_shapes=[
            pltpu.SMEM(slots.shape, jnp.int32),
            pltpu.VMEM(tokens.shape, BF16),
            pltpu.VMEM(bottleneck.shape, BF16),
            DMA((3,)),
        ],
        compiler_params=pltpu.CompilerParams(vmem_limit_bytes=4 << 20),
    )(stay(slots), stay(tokens), stay(bottleneck))
    far = partner(far, 2)
    near = partner(near, 1)
    across = partner(across, 3)
    stored_all = lax.all_gather(stored, "mp", axis=0)
    stored_all, w_out_late = lax.optimization_barrier((stored_all, w_out))
    w_out_other = lax.ppermute(w_out_late, "mp", [(0, 1), (1, 0)])
    weights, *own_qkv, gain, facts = ready(
        slots, clip_lengths, video_blocks, gain1, w_qkv, stored_all
    )
    arrived = lax.all_gather(jnp.concatenate([far, near, across], axis=0), "mp", axis=0)

    far, across, query, keys, values = attend(facts, gain, arrived, weights, own_qkv)
    far = partner(far, 2)
    across = partner(across, 3)
    near = part(near_kernel, "near", BLK, query, keys, values, facts)
    near = partner(near, 1)
    own = part(own_kernel, "own", BLK + PAD, query, keys, values, facts)
    own, far = lax.optimization_barrier((own, far))
    own_all = lax.all_gather(own, "mp", axis=0)
    arrived = lax.all_gather(jnp.concatenate([far, near, across], axis=0), "mp", axis=0)

    base, send = feed(
        slots, stored_all, own_all, arrived, w_out, w_out_other, gain2, w_up, w_down
    )
    sums = lax.all_gather(send, "mp", axis=0)

    mixed, merged = pl.pallas_call(
        finish_kernel,
        name="finish",
        out_shape=(spec(tokens.shape), spec(bottleneck.shape)),
        in_specs=[VMEM, VMEM],
        out_specs=(VMEM,) * 2,
        compiler_params=pltpu.CompilerParams(vmem_limit_bytes=8 << 20),
    )(base, sums)
    return mixed, merged


def solution(mesh):
    placed = (
        P("clip", None, "mp"),
        P("clip", None, "mp"),
        P(),
        P(),
        P(),
        P(),
        P(None, None, "mp"),
        P("mp", None),
        P(),
        P(None, "mp"),
        P("mp", None),
    )
    return jax.shard_map(
        body,
        mesh=mesh,
        in_specs=placed,
        out_specs=(P("clip", None, "mp"), P("clip", None, "mp")),
        check_vma=False,
    )
```

```python
import jax
import jax.numpy as jnp
from jax import lax
from jax.experimental import pallas as pl
from jax.experimental.pallas import tpu as pltpu
from jax.sharding import PartitionSpec as P

HEAD_DIM = 64
BLK = 128
NB = 4
SLOT_DEV = 4
STORE_DEV = 3
GROUP = 4
PAD = 16
STORED = STORE_DEV * BLK
ROWS = STORED + PAD
CLIP_ROWS = SLOT_DEV * BLK
STEPS = (2, 1, 3)
BF16 = jnp.bfloat16
F32 = jnp.float32

VMEM = pl.BlockSpec(memory_space=pltpu.VMEM)
HBM = pl.BlockSpec(memory_space=pltpu.HBM)
DMA = pltpu.SemaphoreType.DMA
SMEM = pl.BlockSpec(memory_space=pltpu.SMEM)


def spec(shape, dtype=BF16):
    return jax.ShapeDtypeStruct(shape, dtype)


def partner(x, step):
    return lax.ppermute(x, "clip", [(i, i ^ step) for i in range(lax.axis_size("clip"))])


def slot_for(store_map, device, owner):
    slot = jnp.int32(-1)
    block = jnp.int32(-1)
    for s in range(STORE_DEV):
        entry = store_map[s, device]
        hit = (entry >= 0) & (entry // SLOT_DEV == owner)
        slot = jnp.where(hit, s, slot)
        block = jnp.where(hit, entry % SLOT_DEV, block)
    return slot, block


def norm_into(x0, x1, gain, out, at, rows):
    half = x0.shape[1]
    x0 = x0.astype(F32)
    x1 = x1.astype(F32)
    scale = 1.0 / (2 * half)
    mean = (jnp.sum(x0, axis=-1, keepdims=True) + jnp.sum(x1, axis=-1, keepdims=True)) * scale
    x0 = x0 - mean
    x1 = x1 - mean
    moment = (
        jnp.sum(x0 * x0, axis=-1, keepdims=True) + jnp.sum(x1 * x1, axis=-1, keepdims=True)
    ) * scale
    inv = lax.rsqrt(moment + 1e-05)
    out[pl.ds(at, rows), :half] = (x0 * inv * gain[:, :half]).astype(BF16)
    out[pl.ds(at, rows), half:] = (x1 * inv * gain[:, half:]).astype(BF16)


def pack_kernel(slots, tokens, extra, far, near, across, stored, store_map, blocks, few, sems):
    member = lax.axis_index("clip")
    loads = [
        pltpu.make_async_copy(x, y, sems.at[i])
        for i, (x, y) in enumerate(((slots, store_map), (tokens, blocks), (extra, few)))
    ]
    for load in loads:
        load.start()
    for load in loads:
        load.wait()
    for step, out in zip(STEPS, (far, near, across)):
        slot, _ = slot_for(store_map, member, member ^ step)
        out[...] = blocks[jnp.maximum(slot, 0)]
    for s in range(STORE_DEV):
        stored[s * BLK : (s + 1) * BLK, :] = blocks[s]
    width = stored.shape[1]
    stored[STORED:, :] = jnp.concatenate(
        [few[0].astype(F32), jnp.zeros((PAD - NB, width), F32)], axis=0
    ).astype(BF16)


def ready_kernel(
    slots,
    all_lengths,
    all_videos,
    gain_in,
    w_qkv,
    stored,
    weights,
    query,
    keys,
    values,
    gain,
    facts,
    normed,
    info,
    store_map,
    lengths,
    videos,
    sems,
):
    member = lax.axis_index("clip")
    small = [
        pltpu.make_async_copy(x, y, sems.at[i])
        for i, (x, y) in enumerate(
            ((gain_in, gain), (slots, store_map), (all_lengths, lengths), (all_videos, videos))
        )
    ]
    loads = [pltpu.make_async_copy(w_qkv.at[i], weights.at[i], sems.at[5 + i]) for i in range(3)]
    for load in small + loads:
        load.start()
    small[0].wait()
    gains = gain[...]
    norm_into(stored[0, STORED:, :], stored[1, STORED:, :], gains, normed, BLK, PAD)
    for load in small[1:]:
        load.wait()
    slot, block = slot_for(store_map, member, member)
    for place, step in enumerate(STEPS):
        info[0, place] = slot_for(store_map, member ^ step, member)[1]
    info[0, GROUP - 1] = block
    info[0, GROUP] = lengths[member]
    info[0, GROUP + 1] = videos[member]
    keep = pltpu.make_async_copy(info, facts, sems.at[4])
    keep.start()
    here = pl.multiple_of(jnp.maximum(slot, 0) * BLK, BLK)
    norm_into(
        stored[0, pl.ds(here, BLK), :], stored[1, pl.ds(here, BLK), :], gains, normed, 0, BLK
    )
    width = query.shape[1]
    tile = 256
    for which, out in ((0, query), (1, keys)):
        loads[which].wait()
        for j in range(0, width, tile):
            got = jnp.dot(normed[...], weights[which, :, j : j + tile], preferred_element_type=F32)
            if which == 0:
                got = got * HEAD_DIM ** (-0.5)
            out[:, j : j + tile] = got.astype(BF16)
    loads[2].wait()
    for j in range(0, width, tile):
        got = jnp.dot(normed[...], weights[2, :, j : j + tile], preferred_element_type=F32)
        for k in range(tile // BLK):
            p = j // BLK + k
            cols = slice(k * BLK, (k + 1) * BLK)
            values[p, :, :BLK] = got[:BLK, cols].T.astype(BF16)
            values[p, :, BLK:] = got[BLK:, cols].T.astype(BF16)
    keep.wait()


NT = (((1,), (1,)), ((), ()))
END = CLIP_ROWS + PAD


def token_blocks(query, keys, values, context, targets, count):
    pairs = values.shape[0]
    low = lax.broadcasted_iota(jnp.int32, (BLK, BLK), 1) < HEAD_DIM
    real = lax.broadcasted_iota(jnp.int32, (PAD, 2 * BLK), 0) < NB
    seen = count * BLK
    chains = [(place, block, first, p) for p in range(pairs) for place, block, first in targets]
    scores = []
    for place, block, first, p in chains:
        cols = slice(p * BLK, (p + 1) * BLK)
        start = pl.multiple_of(first * BLK, BLK)
        q = query[pl.ds(pl.multiple_of(block * BLK, BLK), BLK), cols]
        none = jnp.zeros_like(q)
        both = jnp.concatenate([jnp.where(low, q, none), jnp.where(low, none, q)], axis=0)
        k = jnp.concatenate([keys[pl.ds(start, seen), cols], keys[CLIP_ROWS:END, cols]], axis=0)
        s = lax.dot_general(k, both, NT, preferred_element_type=F32)
        scores.append((s[:seen], jnp.where(real, s[seen:], -1e30)))
    parts = []
    for s, se in scores:
        top = jnp.maximum(jnp.max(s, axis=0, keepdims=True), jnp.max(se, axis=0, keepdims=True))
        parts.append(
            jnp.concatenate([jnp.exp(s - top).astype(BF16), jnp.exp(se - top).astype(BF16)], axis=0)
        )
    sums = []
    for (place, block, first, p), part in zip(chains, parts):
        start = pl.multiple_of(first * BLK, BLK)
        v = jnp.concatenate([values[p, :, pl.ds(start, seen)], values[p, :, CLIP_ROWS:END]], axis=1)
        sums.append(jnp.dot(v, part, preferred_element_type=F32))
    for (place, block, first, p), o in zip(chains, sums):
        total = o[BLK : BLK + 1]
        o = jnp.concatenate(
            [o[:HEAD_DIM, :BLK] / total[:, :BLK], o[HEAD_DIM:BLK, BLK:] / total[:, BLK:]], axis=0
        )
        context[place, :, p * BLK : (p + 1) * BLK] = o.T.astype(BF16)


def sight(info, place):
    block = info[0, place]
    length = info[0, GROUP]
    video = info[0, GROUP + 1]
    is_video = block < video
    first = jnp.where(is_video, 0, video)
    seen = jnp.where(is_video, video, length - video)
    return block, first, jnp.where(block < 0, 0, seen)


def visit_blocks(info, places, query, keys, values, context):
    sights = [sight(info, place) for place in places]
    if len(places) == 2:
        alike = sights[0][2] == sights[1][2]
        for count in range(1, SLOT_DEV):

            @pl.when(alike & (sights[0][2] == count))
            def _():
                targets = [(i, block, first) for i, (block, first, _) in enumerate(sights)]
                token_blocks(query, keys, values, context, targets, count)

    else:
        alike = False

    def visit(i, carry):
        block, first, seen = sight(info, places[0] + i * (places[-1] - places[0]))
        for count in range(1, SLOT_DEV):

            @pl.when(jnp.logical_not(alike) & (seen == count))
            def _():
                token_blocks(query, keys, values, context, [(i, block, first)], count)

        return carry

    lax.fori_loop(0, len(places), visit, 0)


def attend_kernel(
    facts,
    gain,
    arrived,
    weights,
    own_query,
    own_keys,
    own_values,
    far,
    across,
    query,
    keys,
    values,
    normed,
    context,
    info,
    sems,
):
    load = pltpu.make_async_copy(facts, info, sems.at[0])
    load.start()
    width = query.shape[1]
    pairs = width // BLK
    context[...] = jnp.zeros_like(context)
    gains = gain[...]
    for k in range(GROUP - 1):
        rows = slice(k * BLK, (k + 1) * BLK)
        norm_into(arrived[0, rows, :], arrived[1, rows, :], gains, normed, k * BLK, BLK)
    load.wait()
    length = info[0, GROUP]
    row_at = []
    for place in range(GROUP):
        block = info[0, place]
        row_at.append(pl.multiple_of(jnp.where(block < 0, SLOT_DEV + 1, block) * BLK, BLK))

    last = GROUP - 1
    for own, out in ((own_query, query), (own_keys, keys)):
        out[pl.ds(row_at[last], BLK), :] = own[:BLK, :]
        out[CLIP_ROWS:END, :] = own[BLK:, :]
    for p in range(pairs):
        values[p, :BLK, pl.ds(row_at[last], BLK)] = own_values[p, :, :BLK]
        values[p, :BLK, CLIP_ROWS:END] = own_values[p, :, BLK:]
        values[p, BLK:, :END] = jnp.ones((PAD, END), BF16)
    tile = 256
    for which, out in ((0, query), (1, keys)):
        for j in range(0, width, tile):
            got = jnp.dot(normed[...], weights[which, :, j : j + tile], preferred_element_type=F32)
            if which == 0:
                got = got * HEAD_DIM ** (-0.5)
            got = got.astype(BF16)
            for place in range(last):
                out[pl.ds(row_at[place], BLK), j : j + tile] = got[place * BLK : (place + 1) * BLK]
    for j in range(0, width, tile):
        got = jnp.dot(normed[...], weights[2, :, j : j + tile], preferred_element_type=F32)
        for k in range(tile // BLK):
            p = j // BLK + k
            cols = slice(k * BLK, (k + 1) * BLK)
            for place in range(last):
                turned = got[place * BLK : (place + 1) * BLK, cols].T
                values[p, :BLK, pl.ds(row_at[place], BLK)] = turned.astype(BF16)
    for b in range(2, SLOT_DEV):

        @pl.when(b >= length)
        def _():
            values[:, :BLK, b * BLK : (b + 1) * BLK] = jnp.zeros((pairs, BLK, BLK), BF16)

    visit_blocks(info, (0, 2), query, keys, values, context)
    far[...] = context[0]
    across[...] = context[1]


def near_kernel(query, keys, values, facts, near, context, info, sems):
    load = pltpu.make_async_copy(facts, info, sems.at[0])
    load.start()
    context[...] = jnp.zeros_like(context)
    load.wait()
    visit_blocks(info, (1,), query, keys, values, context)
    near[...] = context[0]


def own_kernel(query, keys, values, facts, own, context, info, sems):
    load = pltpu.make_async_copy(facts, info, sems.at[0])
    load.start()
    width = query.shape[1]
    pairs = width // BLK
    context[...] = jnp.zeros_like(context)
    load.wait()
    length = info[0, GROUP]
    video = info[0, GROUP + 1]
    visit_blocks(info, (GROUP - 1,), query, keys, values, context)
    own[:BLK, :] = context[0]

    heads = width // HEAD_DIM
    sub = 8
    qe = query[CLIP_ROWS:END, :].astype(F32)[:sub]
    qe = jnp.concatenate([qe] * heads, axis=0)
    row_head = lax.broadcasted_iota(jnp.int32, (heads * sub, width), 0) // sub
    col_head = lax.broadcasted_iota(jnp.int32, (heads * sub, width), 1) // HEAD_DIM
    qe = jnp.where(row_head == col_head, qe, 0.0).astype(BF16)
    s = lax.dot_general(qe, keys[:END, :], NT, preferred_element_type=F32)
    col = lax.broadcasted_iota(jnp.int32, s.shape, 1)
    bottle = (col >= CLIP_ROWS) & (col < CLIP_ROWS + NB)
    parts = []
    for allowed in (
        bottle | (col < video * BLK),
        bottle | ((col >= video * BLK) & (col < length * BLK)),
    ):
        masked = jnp.where(allowed, s, -1e30)
        e = jnp.exp(masked - jnp.max(masked, axis=-1, keepdims=True))
        parts.append((e / jnp.sum(e, axis=-1, keepdims=True)).astype(BF16))
    first_head = lax.broadcasted_iota(jnp.int32, (sub, BLK), 1) < HEAD_DIM
    for p in range(pairs):
        rows = slice(2 * p * sub, (2 * p + 2) * sub)
        both = jnp.concatenate([parts[0][rows], parts[1][rows]], axis=0)
        o = lax.dot_general(both, values[p, :BLK, :END], NT, preferred_element_type=F32)
        o = 0.5 * (o[: 2 * sub] + o[2 * sub :])
        o = jnp.where(first_head, o[:sub], o[sub:])
        own[BLK:, p * BLK : (p + 1) * BLK] = jnp.concatenate([o, jnp.zeros_like(o)], axis=0).astype(BF16)


def feed_kernel(
    store_map,
    stored,
    own,
    arrived,
    w_out,
    w_out_other,
    gain,
    w_up,
    w_down,
    base,
    send,
    context,
    after,
    normed,
    active,
):
    member = lax.axis_index("clip")
    core = lax.axis_index("mp")
    half = base.shape[1]
    hidden = w_up.shape[1]
    sides = (core, 1 - core)
    kept = [
        (slice(s * BLK, (s + 1) * BLK), store_map[s, member] >= 0) for s in range(STORE_DEV)
    ] + [(slice(STORED, ROWS), True)]
    for s in range(STORE_DEV):
        entry = store_map[s, member]
        step = jnp.where(entry >= 0, (entry // SLOT_DEV) ^ member, -1)
        at = jnp.where(step == STEPS[0], 0, jnp.where(step == STEPS[1], 1, 2))
        at = pl.multiple_of(at * BLK, BLK)
        rows = slice(s * BLK, (s + 1) * BLK)
        mine = jnp.full((BLK, half), step, jnp.int32) == 0
        for k in range(2):
            context[k, rows, :] = jnp.where(
                mine, own[sides[k], :BLK, :], arrived[sides[k], pl.ds(at, BLK), :]
            )
    for k in range(2):
        context[k, STORED:, :] = own[sides[k], BLK:, :]

    tile = 512
    gains = gain[...]
    halves = (slice(0, 208), slice(208, ROWS))
    for rows in halves:
        for side in range(2):
            cols = slice(side * half, (side + 1) * half)
            got = jnp.dot(context[0, rows, :], w_out[:, cols], preferred_element_type=F32)
            got = got + jnp.dot(context[1, rows, :], w_out_other[:, cols], preferred_element_type=F32)
            after[rows, cols] = (got + stored[side, rows, :].astype(F32)).astype(BF16)
    for rows in halves:
        norm_into(
            after[rows, :half], after[rows, half:], gains, normed, rows.start, rows.stop - rows.start
        )
        for j in range(0, hidden, tile):
            got = jnp.dot(normed[rows, :], w_up[:, j : j + tile], preferred_element_type=F32)
            active[rows, j : j + tile] = jax.nn.gelu(got, approximate=True).astype(BF16)
    other = pl.multiple_of((1 - core) * half, half)
    got = jnp.dot(active[...], w_down[:, pl.ds(other, half)], preferred_element_type=F32)
    for rows, keep in kept:
        send[rows, :] = jnp.where(keep, got[rows], 0.0).astype(BF16)
    mine = pl.multiple_of(core * half, half)
    got = jnp.dot(active[...], w_down[:, pl.ds(mine, half)], preferred_element_type=F32)
    got = got + after[:, pl.ds(mine, half)].astype(F32)
    for rows, keep in kept:
        base[rows, :] = jnp.where(keep, got[rows], 0.0)


def finish_kernel(base, sums, mixed, merged):
    other = 1 - lax.axis_index("mp")
    for s in range(STORE_DEV):
        rows = slice(s * BLK, (s + 1) * BLK)
        mixed[s] = (base[rows, :] + sums[other, rows, :].astype(F32)).astype(BF16)
    got = base[STORED:, :] + sums[other, STORED:, :].astype(F32)
    merged[0] = got[:NB].astype(BF16)


def stay(x):
    return pltpu.with_memory_space_constraint(x, pltpu.HBM)


def ready(slots, clip_lengths, video_blocks, gain1, w_qkv, stored_all):
    model = w_qkv.shape[1]
    width = w_qkv.shape[2]
    pairs = width // BLK
    info = (1, 2 * GROUP)
    return pl.pallas_call(
        ready_kernel,
        name="ready",
        out_shape=(
            spec(w_qkv.shape),
            spec((BLK + PAD, width)),
            spec((BLK + PAD, width)),
            spec((pairs, BLK, BLK + PAD)),
            spec((1, model), F32),
            spec(info, jnp.int32),
        ),
        in_specs=[HBM] * 5 + [VMEM],
        out_specs=(VMEM,) * 6,
        scratch_shapes=[
            pltpu.VMEM((BLK + PAD, model), BF16),
            pltpu.SMEM(info, jnp.int32),
            pltpu.SMEM(slots.shape, jnp.int32),
            pltpu.SMEM(clip_lengths.shape, jnp.int32),
            pltpu.SMEM(video_blocks.shape, jnp.int32),
            DMA((8,)),
        ],
        compiler_params=pltpu.CompilerParams(vmem_limit_bytes=8 << 20),
        cost_estimate=pl.CostEstimate(flops=450000000, bytes_accessed=4000000, transcendentals=0),
    )(stay(slots), stay(clip_lengths), stay(video_blocks), stay(gain1), stay(w_qkv), stored_all)


def attend(facts, gain, arrived, weights, own_qkv):
    model = weights.shape[1]
    width = weights.shape[2]
    pairs = width // BLK
    rows = CLIP_ROWS + 2 * BLK
    block = spec((BLK, width))
    return pl.pallas_call(
        attend_kernel,
        name="attend",
        out_shape=(
            block,
            block,
            spec((rows, width)),
            spec((rows, width)),
            spec((pairs, BLK + PAD, rows)),
        ),
        in_specs=[VMEM] * 7,
        out_specs=(VMEM,) * 5,
        scratch_shapes=[
            pltpu.VMEM(((GROUP - 1) * BLK, model), BF16),
            pltpu.VMEM((2, BLK, width), BF16),
            pltpu.SMEM(facts.shape, jnp.int32),
            DMA((1,)),
        ],
        compiler_params=pltpu.CompilerParams(vmem_limit_bytes=16 << 20),
        cost_estimate=pl.CostEstimate(flops=1800000000, bytes_accessed=6000000, transcendentals=1500000),
    )(facts, gain, arrived, weights, *own_qkv)


def part(kernel, name, rows, query, keys, values, facts):
    width = query.shape[1]
    return pl.pallas_call(
        kernel,
        name=name,
        out_shape=spec((rows, width)),
        in_specs=[VMEM] * 4,
        out_specs=VMEM,
        scratch_shapes=[
            pltpu.VMEM((1, BLK, width), BF16),
            pltpu.SMEM(facts.shape, jnp.int32),
            DMA((1,)),
        ],
        compiler_params=pltpu.CompilerParams(vmem_limit_bytes=16 << 20),
        cost_estimate=pl.CostEstimate(flops=400000000, bytes_accessed=3000000, transcendentals=700000),
    )(query, keys, values, facts)


def feed(slots, stored_all, own_all, arrived, w_out, w_out_other, gain2, w_up, w_down):
    width = stored_all.shape[2]
    model = 2 * width
    hidden = w_up.shape[1]
    return pl.pallas_call(
        feed_kernel,
        name="feed",
        out_shape=(spec((ROWS, width), F32), spec((ROWS, width))),
        in_specs=[SMEM] + [VMEM] * 8,
        out_specs=(VMEM,) * 2,
        scratch_shapes=[
            pltpu.VMEM((2, ROWS, width), BF16),
            pltpu.VMEM((ROWS, model), BF16),
            pltpu.VMEM((ROWS, model), BF16),
            pltpu.VMEM((ROWS, hidden), BF16),
        ],
        compiler_params=pltpu.CompilerParams(vmem_limit_bytes=16 << 20),
        cost_estimate=pl.CostEstimate(flops=4100000000, bytes_accessed=14000000, transcendentals=820000),
    )(slots, stored_all, own_all, arrived, w_out, w_out_other, gain2, w_up, w_down)


def body(
    tokens,
    bottleneck,
    clip_lengths,
    video_blocks,
    store_map,
    norm1_gain,
    w_qkv,
    w_out,
    norm2_gain,
    w_up,
    w_down,
):
    width = tokens.shape[2]
    model = 2 * width
    gain1 = norm1_gain.reshape(1, model)
    gain2 = norm2_gain.reshape(1, model)
    block = spec((BLK, width))
    slots = store_map.T

    far, near, across, stored = pl.pallas_call(
        pack_kernel,
        name="pack",
        out_shape=(block, block, block, spec((ROWS, width))),
        in_specs=[HBM, HBM, HBM],
        out_specs=(VMEM,) * 4,
        scratch_shapes=[
            pltpu.SMEM(slots.shape, jnp.int32),
            pltpu.VMEM(tokens.shape, BF16),
            pltpu.VMEM(bottleneck.shape, BF16),
            DMA((3,)),
        ],
        compiler_params=pltpu.CompilerParams(vmem_limit_bytes=4 << 20),
    )(stay(slots), stay(tokens), stay(bottleneck))
    far = partner(far, 2)
    near = partner(near, 1)
    across = partner(across, 3)
    stored_all = lax.all_gather(stored, "mp", axis=0)
    stored_all, w_out_late = lax.optimization_barrier((stored_all, w_out))
    w_out_other = lax.ppermute(w_out_late, "mp", [(0, 1), (1, 0)])
    weights, *own_qkv, gain, facts = ready(
        slots, clip_lengths, video_blocks, gain1, w_qkv, stored_all
    )
    arrived = lax.all_gather(jnp.concatenate([far, near, across], axis=0), "mp", axis=0)

    far, across, query, keys, values = attend(facts, gain, arrived, weights, own_qkv)
    far = partner(far, 2)
    across = partner(across, 3)
    near = part(near_kernel, "near", BLK, query, keys, values, facts)
    near = partner(near, 1)
    own = part(own_kernel, "own", BLK + PAD, query, keys, values, facts)
    own, far = lax.optimization_barrier((own, far))
    own_all = lax.all_gather(own, "mp", axis=0)
    arrived = lax.all_gather(jnp.concatenate([far, near, across], axis=0), "mp", axis=0)

    base, send = feed(
        slots, stored_all, own_all, arrived, w_out, w_out_other, gain2, w_up, w_down
    )
    sums = lax.all_gather(send, "mp", axis=0)

    mixed, merged = pl.pallas_call(
        finish_kernel,
        name="finish",
        out_shape=(spec(tokens.shape), spec(bottleneck.shape)),
        in_specs=[VMEM, VMEM],
        out_specs=(VMEM,) * 2,
        compiler_params=pltpu.CompilerParams(vmem_limit_bytes=8 << 20),
    )(base, sums)
    return mixed, merged


def solution(mesh):
    placed = (
        P("clip", None, "mp"),
        P("clip", None, "mp"),
        P(),
        P(),
        P(),
        P(),
        P(None, None, "mp"),
        P("mp", None),
        P(),
        P(None, "mp"),
        P("mp", None),
    )
    return jax.shard_map(
        body,
        mesh=mesh,
        in_specs=placed,
        out_specs=(P("clip", None, "mp"), P("clip", None, "mp")),
        check_vma=False,
    )
```

```python
import jax
import jax.numpy as jnp
from jax import lax
from jax.experimental import pallas as pl
from jax.experimental.pallas import tpu as pltpu
from jax.sharding import PartitionSpec as P

HEAD_DIM = 64
BLK = 128
NB = 4
SLOT_DEV = 4
STORE_DEV = 3
GROUP = 4
PAD = 16
STORED = STORE_DEV * BLK
ROWS = STORED + PAD
CLIP_ROWS = SLOT_DEV * BLK
STEPS = (2, 1, 3)
BF16 = jnp.bfloat16
F32 = jnp.float32

VMEM = pl.BlockSpec(memory_space=pltpu.VMEM)
HBM = pl.BlockSpec(memory_space=pltpu.HBM)
DMA = pltpu.SemaphoreType.DMA
SMEM = pl.BlockSpec(memory_space=pltpu.SMEM)


def spec(shape, dtype=BF16):
    return jax.ShapeDtypeStruct(shape, dtype)


def partner(x, step):
    return lax.ppermute(x, "clip", [(i, i ^ step) for i in range(lax.axis_size("clip"))])


def slot_for(store_map, device, owner):
    slot = jnp.int32(-1)
    block = jnp.int32(-1)
    for s in range(STORE_DEV):
        entry = store_map[s, device]
        hit = (entry >= 0) & (entry // SLOT_DEV == owner)
        slot = jnp.where(hit, s, slot)
        block = jnp.where(hit, entry % SLOT_DEV, block)
    return slot, block


def norm_into(x0, x1, gain, out, at, rows):
    half = x0.shape[1]
    x0 = x0.astype(F32)
    x1 = x1.astype(F32)
    scale = 1.0 / (2 * half)
    mean = (jnp.sum(x0, axis=-1, keepdims=True) + jnp.sum(x1, axis=-1, keepdims=True)) * scale
    x0 = x0 - mean
    x1 = x1 - mean
    moment = (
        jnp.sum(x0 * x0, axis=-1, keepdims=True) + jnp.sum(x1 * x1, axis=-1, keepdims=True)
    ) * scale
    inv = lax.rsqrt(moment + 1e-05)
    out[pl.ds(at, rows), :half] = (x0 * inv * gain[:, :half]).astype(BF16)
    out[pl.ds(at, rows), half:] = (x1 * inv * gain[:, half:]).astype(BF16)


def pack_kernel(slots, tokens, extra, far, near, across, stored, store_map, blocks, few, sems):
    member = lax.axis_index("clip")
    loads = [
        pltpu.make_async_copy(x, y, sems.at[i])
        for i, (x, y) in enumerate(((slots, store_map), (tokens, blocks), (extra, few)))
    ]
    for load in loads:
        load.start()
    for load in loads:
        load.wait()
    for step, out in zip(STEPS, (far, near, across)):
        slot, _ = slot_for(store_map, member, member ^ step)
        out[...] = blocks[jnp.maximum(slot, 0)]
    for s in range(STORE_DEV):
        stored[s * BLK : (s + 1) * BLK, :] = blocks[s]
    width = stored.shape[1]
    stored[STORED:, :] = jnp.concatenate(
        [few[0].astype(F32), jnp.zeros((PAD - NB, width), F32)], axis=0
    ).astype(BF16)


def ready_kernel(
    slots,
    all_lengths,
    all_videos,
    gain_in,
    w_qkv,
    stored,
    weights,
    query,
    keys,
    values,
    gain,
    facts,
    normed,
    info,
    store_map,
    lengths,
    videos,
    sems,
):
    member = lax.axis_index("clip")
    small = [
        pltpu.make_async_copy(x, y, sems.at[i])
        for i, (x, y) in enumerate(
            ((gain_in, gain), (slots, store_map), (all_lengths, lengths), (all_videos, videos))
        )
    ]
    loads = [pltpu.make_async_copy(w_qkv.at[i], weights.at[i], sems.at[5 + i]) for i in range(3)]
    for load in small + loads:
        load.start()
    small[0].wait()
    gains = gain[...]
    norm_into(stored[0, STORED:, :], stored[1, STORED:, :], gains, normed, BLK, PAD)
    for load in small[1:]:
        load.wait()
    slot, block = slot_for(store_map, member, member)
    for place, step in enumerate(STEPS):
        info[0, place] = slot_for(store_map, member ^ step, member)[1]
    info[0, GROUP - 1] = block
    info[0, GROUP] = lengths[member]
    info[0, GROUP + 1] = videos[member]
    keep = pltpu.make_async_copy(info, facts, sems.at[4])
    keep.start()
    here = pl.multiple_of(jnp.maximum(slot, 0) * BLK, BLK)
    norm_into(
        stored[0, pl.ds(here, BLK), :], stored[1, pl.ds(here, BLK), :], gains, normed, 0, BLK
    )
    width = query.shape[1]
    tile = 256
    for which, out in ((0, query), (1, keys)):
        loads[which].wait()
        for j in range(0, width, tile):
            got = jnp.dot(normed[...], weights[which, :, j : j + tile], preferred_element_type=F32)
            if which == 0:
                got = got * HEAD_DIM ** (-0.5)
            out[:, j : j + tile] = got.astype(BF16)
    loads[2].wait()
    for j in range(0, width, tile):
        got = jnp.dot(normed[...], weights[2, :, j : j + tile], preferred_element_type=F32)
        for k in range(tile // BLK):
            p = j // BLK + k
            cols = slice(k * BLK, (k + 1) * BLK)
            values[p, :, :BLK] = got[:BLK, cols].T.astype(BF16)
            values[p, :, BLK:] = got[BLK:, cols].T.astype(BF16)
    keep.wait()


NT = (((1,), (1,)), ((), ()))
END = CLIP_ROWS + PAD


def token_blocks(query, keys, values, context, targets, count):
    pairs = values.shape[0]
    low = lax.broadcasted_iota(jnp.int32, (BLK, BLK), 1) < HEAD_DIM
    real = lax.broadcasted_iota(jnp.int32, (PAD, 2 * BLK), 0) < NB
    seen = count * BLK
    chains = [(place, block, first, p) for p in range(pairs) for place, block, first in targets]
    scores = []
    for place, block, first, p in chains:
        cols = slice(p * BLK, (p + 1) * BLK)
        start = pl.multiple_of(first * BLK, BLK)
        q = query[pl.ds(pl.multiple_of(block * BLK, BLK), BLK), cols]
        none = jnp.zeros_like(q)
        both = jnp.concatenate([jnp.where(low, q, none), jnp.where(low, none, q)], axis=0)
        k = jnp.concatenate([keys[pl.ds(start, seen), cols], keys[CLIP_ROWS:END, cols]], axis=0)
        s = lax.dot_general(k, both, NT, preferred_element_type=F32)
        scores.append((s[:seen], jnp.where(real, s[seen:], -1e30)))
    parts = []
    for s, se in scores:
        top = jnp.maximum(jnp.max(s, axis=0, keepdims=True), jnp.max(se, axis=0, keepdims=True))
        parts.append(
            jnp.concatenate([jnp.exp(s - top).astype(BF16), jnp.exp(se - top).astype(BF16)], axis=0)
        )
    sums = []
    for (place, block, first, p), part in zip(chains, parts):
        start = pl.multiple_of(first * BLK, BLK)
        v = jnp.concatenate([values[p, :, pl.ds(start, seen)], values[p, :, CLIP_ROWS:END]], axis=1)
        sums.append(jnp.dot(v, part, preferred_element_type=F32))
    for (place, block, first, p), o in zip(chains, sums):
        total = o[BLK : BLK + 1]
        o = jnp.concatenate(
            [o[:HEAD_DIM, :BLK] / total[:, :BLK], o[HEAD_DIM:BLK, BLK:] / total[:, BLK:]], axis=0
        )
        context[place, :, p * BLK : (p + 1) * BLK] = o.T.astype(BF16)


def sight(info, place):
    block = info[0, place]
    length = info[0, GROUP]
    video = info[0, GROUP + 1]
    is_video = block < video
    first = jnp.where(is_video, 0, video)
    seen = jnp.where(is_video, video, length - video)
    return block, first, jnp.where(block < 0, 0, seen)


def visit_blocks(info, places, query, keys, values, context):
    sights = [sight(info, place) for place in places]
    if len(places) == 2:
        alike = sights[0][2] == sights[1][2]
        for count in range(1, SLOT_DEV):

            @pl.when(alike & (sights[0][2] == count))
            def _():
                targets = [(i, block, first) for i, (block, first, _) in enumerate(sights)]
                token_blocks(query, keys, values, context, targets, count)

    else:
        alike = False

    def visit(i, carry):
        block, first, seen = sight(info, places[0] + i * (places[-1] - places[0]))
        for count in range(1, SLOT_DEV):

            @pl.when(jnp.logical_not(alike) & (seen == count))
            def _():
                token_blocks(query, keys, values, context, [(i, block, first)], count)

        return carry

    lax.fori_loop(0, len(places), visit, 0)


def attend_kernel(
    facts,
    gain,
    arrived,
    weights,
    own_query,
    own_keys,
    own_values,
    far,
    across,
    query,
    keys,
    values,
    normed,
    context,
    info,
    sems,
):
    load = pltpu.make_async_copy(facts, info, sems.at[0])
    load.start()
    width = query.shape[1]
    pairs = width // BLK
    context[...] = jnp.zeros_like(context)
    gains = gain[...]
    for k in range(GROUP - 1):
        rows = slice(k * BLK, (k + 1) * BLK)
        norm_into(arrived[0, rows, :], arrived[1, rows, :], gains, normed, k * BLK, BLK)
    load.wait()
    length = info[0, GROUP]
    row_at = []
    for place in range(GROUP):
        block = info[0, place]
        row_at.append(pl.multiple_of(jnp.where(block < 0, SLOT_DEV + 1, block) * BLK, BLK))

    last = GROUP - 1
    for own, out in ((own_query, query), (own_keys, keys)):
        out[pl.ds(row_at[last], BLK), :] = own[:BLK, :]
        out[CLIP_ROWS:END, :] = own[BLK:, :]
    for p in range(pairs):
        values[p, :BLK, pl.ds(row_at[last], BLK)] = own_values[p, :, :BLK]
        values[p, :BLK, CLIP_ROWS:END] = own_values[p, :, BLK:]
        values[p, BLK:, :END] = jnp.ones((PAD, END), BF16)
    tile = 256
    for which, out in ((0, query), (1, keys)):
        for j in range(0, width, tile):
            got = jnp.dot(normed[...], weights[which, :, j : j + tile], preferred_element_type=F32)
            if which == 0:
                got = got * HEAD_DIM ** (-0.5)
            got = got.astype(BF16)
            for place in range(last):
                out[pl.ds(row_at[place], BLK), j : j + tile] = got[place * BLK : (place + 1) * BLK]
    for j in range(0, width, tile):
        got = jnp.dot(normed[...], weights[2, :, j : j + tile], preferred_element_type=F32)
        for k in range(tile // BLK):
            p = j // BLK + k
            cols = slice(k * BLK, (k + 1) * BLK)
            for place in range(last):
                turned = got[place * BLK : (place + 1) * BLK, cols].T
                values[p, :BLK, pl.ds(row_at[place], BLK)] = turned.astype(BF16)
    for b in range(2, SLOT_DEV):

        @pl.when(b >= length)
        def _():
            values[:, :BLK, b * BLK : (b + 1) * BLK] = jnp.zeros((pairs, BLK, BLK), BF16)

    visit_blocks(info, (0, 2), query, keys, values, context)
    far[...] = context[0]
    across[...] = context[1]


def near_kernel(query, keys, values, facts, near, context, info, sems):
    load = pltpu.make_async_copy(facts, info, sems.at[0])
    load.start()
    context[...] = jnp.zeros_like(context)
    load.wait()
    visit_blocks(info, (1,), query, keys, values, context)
    near[...] = context[0]


def own_kernel(query, keys, values, facts, own, context, info, sems):
    load = pltpu.make_async_copy(facts, info, sems.at[0])
    load.start()
    width = query.shape[1]
    pairs = width // BLK
    context[...] = jnp.zeros_like(context)
    load.wait()
    length = info[0, GROUP]
    video = info[0, GROUP + 1]
    visit_blocks(info, (GROUP - 1,), query, keys, values, context)
    own[:BLK, :] = context[0]

    heads = width // HEAD_DIM
    sub = 8
    qe = query[CLIP_ROWS:END, :].astype(F32)[:sub]
    qe = jnp.concatenate([qe] * heads, axis=0)
    row_head = lax.broadcasted_iota(jnp.int32, (heads * sub, width), 0) // sub
    col_head = lax.broadcasted_iota(jnp.int32, (heads * sub, width), 1) // HEAD_DIM
    qe = jnp.where(row_head == col_head, qe, 0.0).astype(BF16)
    s = lax.dot_general(qe, keys[:END, :], NT, preferred_element_type=F32)
    col = lax.broadcasted_iota(jnp.int32, s.shape, 1)
    bottle = (col >= CLIP_ROWS) & (col < CLIP_ROWS + NB)
    parts = []
    for allowed in (
        bottle | (col < video * BLK),
        bottle | ((col >= video * BLK) & (col < length * BLK)),
    ):
        masked = jnp.where(allowed, s, -1e30)
        e = jnp.exp(masked - jnp.max(masked, axis=-1, keepdims=True))
        parts.append((e / jnp.sum(e, axis=-1, keepdims=True)).astype(BF16))
    first_head = lax.broadcasted_iota(jnp.int32, (sub, BLK), 1) < HEAD_DIM
    for p in range(pairs):
        rows = slice(2 * p * sub, (2 * p + 2) * sub)
        both = jnp.concatenate([parts[0][rows], parts[1][rows]], axis=0)
        o = lax.dot_general(both, values[p, :BLK, :END], NT, preferred_element_type=F32)
        o = 0.5 * (o[: 2 * sub] + o[2 * sub :])
        o = jnp.where(first_head, o[:sub], o[sub:])
        own[BLK:, p * BLK : (p + 1) * BLK] = jnp.concatenate([o, jnp.zeros_like(o)], axis=0).astype(BF16)


def feed_kernel(
    store_map,
    stored,
    own,
    arrived,
    w_out,
    w_out_other,
    gain,
    w_up,
    w_down,
    base,
    send,
    context,
    after,
    normed,
    active,
):
    member = lax.axis_index("clip")
    core = lax.axis_index("mp")
    half = base.shape[1]
    hidden = w_up.shape[1]
    sides = (core, 1 - core)
    kept = [
        (slice(s * BLK, (s + 1) * BLK), store_map[s, member] >= 0) for s in range(STORE_DEV)
    ] + [(slice(STORED, ROWS), True)]
    for s in range(STORE_DEV):
        entry = store_map[s, member]
        step = jnp.where(entry >= 0, (entry // SLOT_DEV) ^ member, -1)
        at = jnp.where(step == STEPS[0], 0, jnp.where(step == STEPS[1], 1, 2))
        at = pl.multiple_of(at * BLK, BLK)
        rows = slice(s * BLK, (s + 1) * BLK)
        mine = jnp.full((BLK, half), step, jnp.int32) == 0
        for k in range(2):
            context[k, rows, :] = jnp.where(
                mine, own[sides[k], :BLK, :], arrived[sides[k], pl.ds(at, BLK), :]
            )
    for k in range(2):
        context[k, STORED:, :] = own[sides[k], BLK:, :]

    tile = 512
    gains = gain[...]
    halves = (slice(0, 208), slice(208, ROWS))
    for rows in halves:
        for side in range(2):
            cols = slice(side * half, (side + 1) * half)
            got = jnp.dot(context[0, rows, :], w_out[:, cols], preferred_element_type=F32)
            got = got + jnp.dot(context[1, rows, :], w_out_other[:, cols], preferred_element_type=F32)
            after[rows, cols] = (got + stored[side, rows, :].astype(F32)).astype(BF16)
    for rows in halves:
        norm_into(
            after[rows, :half], after[rows, half:], gains, normed, rows.start, rows.stop - rows.start
        )
        for j in range(0, hidden, tile):
            got = jnp.dot(normed[rows, :], w_up[:, j : j + tile], preferred_element_type=F32)
            active[rows, j : j + tile] = jax.nn.gelu(got, approximate=True).astype(BF16)
    other = pl.multiple_of((1 - core) * half, half)
    got = jnp.dot(active[...], w_down[:, pl.ds(other, half)], preferred_element_type=F32)
    for rows, keep in kept:
        send[rows, :] = jnp.where(keep, got[rows], 0.0).astype(BF16)
    mine = pl.multiple_of(core * half, half)
    got = jnp.dot(active[...], w_down[:, pl.ds(mine, half)], preferred_element_type=F32)
    got = got + after[:, pl.ds(mine, half)].astype(F32)
    for rows, keep in kept:
        base[rows, :] = jnp.where(keep, got[rows], 0.0)


def finish_kernel(base, sums, mixed, merged):
    other = 1 - lax.axis_index("mp")
    for s in range(STORE_DEV):
        rows = slice(s * BLK, (s + 1) * BLK)
        mixed[s] = (base[rows, :] + sums[other, rows, :].astype(F32)).astype(BF16)
    got = base[STORED:, :] + sums[other, STORED:, :].astype(F32)
    merged[0] = got[:NB].astype(BF16)


def stay(x):
    return pltpu.with_memory_space_constraint(x, pltpu.HBM)


def ready(slots, clip_lengths, video_blocks, gain1, w_qkv, stored_all):
    model = w_qkv.shape[1]
    width = w_qkv.shape[2]
    pairs = width // BLK
    info = (1, 2 * GROUP)
    return pl.pallas_call(
        ready_kernel,
        name="ready",
        out_shape=(
            spec(w_qkv.shape),
            spec((BLK + PAD, width)),
            spec((BLK + PAD, width)),
            spec((pairs, BLK, BLK + PAD)),
            spec((1, model), F32),
            spec(info, jnp.int32),
        ),
        in_specs=[HBM] * 5 + [VMEM],
        out_specs=(VMEM,) * 6,
        scratch_shapes=[
            pltpu.VMEM((BLK + PAD, model), BF16),
            pltpu.SMEM(info, jnp.int32),
            pltpu.SMEM(slots.shape, jnp.int32),
            pltpu.SMEM(clip_lengths.shape, jnp.int32),
            pltpu.SMEM(video_blocks.shape, jnp.int32),
            DMA((8,)),
        ],
        compiler_params=pltpu.CompilerParams(vmem_limit_bytes=8 << 20),
        cost_estimate=pl.CostEstimate(flops=450000000, bytes_accessed=4000000, transcendentals=0),
    )(stay(slots), stay(clip_lengths), stay(video_blocks), stay(gain1), stay(w_qkv), stored_all)


def attend(facts, gain, arrived, weights, own_qkv):
    model = weights.shape[1]
    width = weights.shape[2]
    pairs = width // BLK
    rows = CLIP_ROWS + 2 * BLK
    block = spec((BLK, width))
    return pl.pallas_call(
        attend_kernel,
        name="attend",
        out_shape=(
            block,
            block,
            spec((rows, width)),
            spec((rows, width)),
            spec((pairs, BLK + PAD, rows)),
        ),
        in_specs=[VMEM] * 7,
        out_specs=(VMEM,) * 5,
        scratch_shapes=[
            pltpu.VMEM(((GROUP - 1) * BLK, model), BF16),
            pltpu.VMEM((2, BLK, width), BF16),
            pltpu.SMEM(facts.shape, jnp.int32),
            DMA((1,)),
        ],
        compiler_params=pltpu.CompilerParams(vmem_limit_bytes=16 << 20),
        cost_estimate=pl.CostEstimate(flops=1800000000, bytes_accessed=6000000, transcendentals=1500000),
    )(facts, gain, arrived, weights, *own_qkv)


def part(kernel, name, rows, query, keys, values, facts):
    width = query.shape[1]
    return pl.pallas_call(
        kernel,
        name=name,
        out_shape=spec((rows, width)),
        in_specs=[VMEM] * 4,
        out_specs=VMEM,
        scratch_shapes=[
            pltpu.VMEM((1, BLK, width), BF16),
            pltpu.SMEM(facts.shape, jnp.int32),
            DMA((1,)),
        ],
        compiler_params=pltpu.CompilerParams(vmem_limit_bytes=16 << 20),
        cost_estimate=pl.CostEstimate(flops=400000000, bytes_accessed=3000000, transcendentals=700000),
    )(query, keys, values, facts)


def feed(slots, stored_all, own_all, arrived, w_out, w_out_other, gain2, w_up, w_down):
    width = stored_all.shape[2]
    model = 2 * width
    hidden = w_up.shape[1]
    return pl.pallas_call(
        feed_kernel,
        name="feed",
        out_shape=(spec((ROWS, width), F32), spec((ROWS, width))),
        in_specs=[SMEM] + [VMEM] * 8,
        out_specs=(VMEM,) * 2,
        scratch_shapes=[
            pltpu.VMEM((2, ROWS, width), BF16),
            pltpu.VMEM((ROWS, model), BF16),
            pltpu.VMEM((ROWS, model), BF16),
            pltpu.VMEM((ROWS, hidden), BF16),
        ],
        compiler_params=pltpu.CompilerParams(vmem_limit_bytes=16 << 20),
        cost_estimate=pl.CostEstimate(flops=4100000000, bytes_accessed=14000000, transcendentals=820000),
    )(slots, stored_all, own_all, arrived, w_out, w_out_other, gain2, w_up, w_down)


def body(
    tokens,
    bottleneck,
    clip_lengths,
    video_blocks,
    store_map,
    norm1_gain,
    w_qkv,
    w_out,
    norm2_gain,
    w_up,
    w_down,
):
    width = tokens.shape[2]
    model = 2 * width
    gain1 = norm1_gain.reshape(1, model)
    gain2 = norm2_gain.reshape(1, model)
    block = spec((BLK, width))
    slots = store_map.T

    far, near, across, stored = pl.pallas_call(
        pack_kernel,
        name="pack",
        out_shape=(block, block, block, spec((ROWS, width))),
        in_specs=[HBM, HBM, HBM],
        out_specs=(VMEM,) * 4,
        scratch_shapes=[
            pltpu.SMEM(slots.shape, jnp.int32),
            pltpu.VMEM(tokens.shape, BF16),
            pltpu.VMEM(bottleneck.shape, BF16),
            DMA((3,)),
        ],
        compiler_params=pltpu.CompilerParams(vmem_limit_bytes=4 << 20),
    )(stay(slots), stay(tokens), stay(bottleneck))
    far = partner(far, 2)
    near = partner(near, 1)
    across = partner(across, 3)
    stored_all = lax.all_gather(stored, "mp", axis=0)
    stored_all, w_out_late = lax.optimization_barrier((stored_all, w_out))
    w_out_other = lax.ppermute(w_out_late, "mp", [(0, 1), (1, 0)])
    weights, *own_qkv, gain, facts = ready(
        slots, clip_lengths, video_blocks, gain1, w_qkv, stored_all
    )
    arrived = lax.all_gather(jnp.concatenate([far, near, across], axis=0), "mp", axis=0)

    far, across, query, keys, values = attend(facts, gain, arrived, weights, own_qkv)
    far = partner(far, 2)
    across = partner(across, 3)
    near = part(near_kernel, "near", BLK, query, keys, values, facts)
    near = partner(near, 1)
    own = part(own_kernel, "own", BLK + PAD, query, keys, values, facts)
    own, far, across = lax.optimization_barrier((own, far, across))
    own_all = lax.all_gather(own, "mp", axis=0)
    arrived = lax.all_gather(jnp.concatenate([far, near, across], axis=0), "mp", axis=0)

    base, send = feed(
        slots, stored_all, own_all, arrived, w_out, w_out_other, gain2, w_up, w_down
    )
    sums = lax.all_gather(send, "mp", axis=0)

    mixed, merged = pl.pallas_call(
        finish_kernel,
        name="finish",
        out_shape=(spec(tokens.shape), spec(bottleneck.shape)),
        in_specs=[VMEM, VMEM],
        out_specs=(VMEM,) * 2,
        compiler_params=pltpu.CompilerParams(vmem_limit_bytes=8 << 20),
    )(base, sums)
    return mixed, merged


def solution(mesh):
    placed = (
        P("clip", None, "mp"),
        P("clip", None, "mp"),
        P(),
        P(),
        P(),
        P(),
        P(None, None, "mp"),
        P("mp", None),
        P(),
        P(None, "mp"),
        P("mp", None),
    )
    return jax.shard_map(
        body,
        mesh=mesh,
        in_specs=placed,
        out_specs=(P("clip", None, "mp"), P("clip", None, "mp")),
        check_vma=False,
    )
```

```python
import itertools

import jax
import jax.numpy as jnp
from jax import lax
from jax.experimental import pallas as pl
from jax.experimental.pallas import tpu as pltpu
from jax.sharding import PartitionSpec as P

HEAD_DIM = 64
BLK = 128
NB = 4
SLOT_DEV = 4
STORE_DEV = 3
GROUP = 4
PAD = 16
STORED = STORE_DEV * BLK
ROWS = STORED + PAD
CLIP_ROWS = SLOT_DEV * BLK
STEPS = (2, 1, 3)
BF16 = jnp.bfloat16
F32 = jnp.float32

VMEM = pl.BlockSpec(memory_space=pltpu.VMEM)
HBM = pl.BlockSpec(memory_space=pltpu.HBM)
DMA = pltpu.SemaphoreType.DMA
SMEM = pl.BlockSpec(memory_space=pltpu.SMEM)


def spec(shape, dtype=BF16):
    return jax.ShapeDtypeStruct(shape, dtype)


def partner(x, step):
    return lax.ppermute(x, "clip", [(i, i ^ step) for i in range(lax.axis_size("clip"))])


def slot_for(store_map, device, owner):
    slot = jnp.int32(-1)
    block = jnp.int32(-1)
    for s in range(STORE_DEV):
        entry = store_map[s, device]
        hit = (entry >= 0) & (entry // SLOT_DEV == owner)
        slot = jnp.where(hit, s, slot)
        block = jnp.where(hit, entry % SLOT_DEV, block)
    return slot, block


def norm_into(x0, x1, gain, out, at, rows):
    half = x0.shape[1]
    x0 = x0.astype(F32)
    x1 = x1.astype(F32)
    scale = 1.0 / (2 * half)
    mean = (jnp.sum(x0, axis=-1, keepdims=True) + jnp.sum(x1, axis=-1, keepdims=True)) * scale
    x0 = x0 - mean
    x1 = x1 - mean
    moment = (
        jnp.sum(x0 * x0, axis=-1, keepdims=True) + jnp.sum(x1 * x1, axis=-1, keepdims=True)
    ) * scale
    inv = lax.rsqrt(moment + 1e-05)
    out[pl.ds(at, rows), :half] = (x0 * inv * gain[:, :half]).astype(BF16)
    out[pl.ds(at, rows), half:] = (x1 * inv * gain[:, half:]).astype(BF16)


def pack_kernel(slots, tokens, extra, far, near, across, stored, store_map, blocks, few, sems):
    member = lax.axis_index("clip")
    loads = [
        pltpu.make_async_copy(x, y, sems.at[i])
        for i, (x, y) in enumerate(((slots, store_map), (tokens, blocks), (extra, few)))
    ]
    for load in loads:
        load.start()
    for load in loads:
        load.wait()
    for step, out in zip(STEPS, (far, near, across)):
        slot, _ = slot_for(store_map, member, member ^ step)
        out[...] = blocks[jnp.maximum(slot, 0)]
    for s in range(STORE_DEV):
        stored[s * BLK : (s + 1) * BLK, :] = blocks[s]
    width = stored.shape[1]
    stored[STORED:, :] = jnp.concatenate(
        [few[0].astype(F32), jnp.zeros((PAD - NB, width), F32)], axis=0
    ).astype(BF16)


def ready_kernel(
    slots,
    all_lengths,
    all_videos,
    gain_in,
    w_qkv,
    stored,
    weights,
    query,
    keys,
    values,
    gain,
    facts,
    normed,
    info,
    store_map,
    lengths,
    videos,
    sems,
):
    member = lax.axis_index("clip")
    small = [
        pltpu.make_async_copy(x, y, sems.at[i])
        for i, (x, y) in enumerate(
            ((gain_in, gain), (slots, store_map), (all_lengths, lengths), (all_videos, videos))
        )
    ]
    loads = [pltpu.make_async_copy(w_qkv.at[i], weights.at[i], sems.at[5 + i]) for i in range(3)]
    for load in small + loads:
        load.start()
    small[0].wait()
    gains = gain[...]
    norm_into(stored[0, STORED:, :], stored[1, STORED:, :], gains, normed, BLK, PAD)
    for load in small[1:]:
        load.wait()
    slot, block = slot_for(store_map, member, member)
    for place, step in enumerate(STEPS):
        info[0, place] = slot_for(store_map, member ^ step, member)[1]
    info[0, GROUP - 1] = block
    info[0, GROUP] = lengths[member]
    info[0, GROUP + 1] = videos[member]
    keep = pltpu.make_async_copy(info, facts, sems.at[4])
    keep.start()
    here = pl.multiple_of(jnp.maximum(slot, 0) * BLK, BLK)
    norm_into(
        stored[0, pl.ds(here, BLK), :], stored[1, pl.ds(here, BLK), :], gains, normed, 0, BLK
    )
    width = query.shape[1]
    tile = 256
    for which, out in ((0, query), (1, keys)):
        loads[which].wait()
        for j in range(0, width, tile):
            got = jnp.dot(normed[...], weights[which, :, j : j + tile], preferred_element_type=F32)
            if which == 0:
                got = got * HEAD_DIM ** (-0.5)
            out[:, j : j + tile] = got.astype(BF16)
    loads[2].wait()
    for j in range(0, width, tile):
        got = jnp.dot(normed[...], weights[2, :, j : j + tile], preferred_element_type=F32)
        for k in range(tile // BLK):
            p = j // BLK + k
            cols = slice(k * BLK, (k + 1) * BLK)
            values[p, :, :BLK] = got[:BLK, cols].T.astype(BF16)
            values[p, :, BLK:] = got[BLK:, cols].T.astype(BF16)
    keep.wait()


NT = (((1,), (1,)), ((), ()))
END = CLIP_ROWS + PAD


def token_blocks(query, keys, values, context, targets):
    pairs = values.shape[0]
    low = lax.broadcasted_iota(jnp.int32, (BLK, BLK), 1) < HEAD_DIM
    real = lax.broadcasted_iota(jnp.int32, (PAD, 2 * BLK), 0) < NB
    chains = [
        (place, block, pl.multiple_of(first * BLK, BLK), count * BLK, p)
        for p in range(pairs)
        for place, block, first, count in targets
    ]
    scores = []
    for place, block, start, seen, p in chains:
        cols = slice(p * BLK, (p + 1) * BLK)
        q = query[pl.ds(pl.multiple_of(block * BLK, BLK), BLK), cols]
        none = jnp.zeros_like(q)
        both = jnp.concatenate([jnp.where(low, q, none), jnp.where(low, none, q)], axis=0)
        k = jnp.concatenate([keys[pl.ds(start, seen), cols], keys[CLIP_ROWS:END, cols]], axis=0)
        s = lax.dot_general(k, both, NT, preferred_element_type=F32)
        scores.append((s[:seen], jnp.where(real, s[seen:], -1e30)))
    parts = []
    for s, se in scores:
        top = jnp.maximum(jnp.max(s, axis=0, keepdims=True), jnp.max(se, axis=0, keepdims=True))
        parts.append(
            jnp.concatenate([jnp.exp(s - top).astype(BF16), jnp.exp(se - top).astype(BF16)], axis=0)
        )
    sums = []
    for (place, block, start, seen, p), part in zip(chains, parts):
        v = jnp.concatenate([values[p, :, pl.ds(start, seen)], values[p, :, CLIP_ROWS:END]], axis=1)
        sums.append(jnp.dot(v, part, preferred_element_type=F32))
    for (place, block, start, seen, p), o in zip(chains, sums):
        total = o[BLK : BLK + 1]
        o = jnp.concatenate(
            [o[:HEAD_DIM, :BLK] / total[:, :BLK], o[HEAD_DIM:BLK, BLK:] / total[:, BLK:]], axis=0
        )
        context[place, :, p * BLK : (p + 1) * BLK] = o.T.astype(BF16)


def sight(info, place):
    block = info[0, place]
    length = info[0, GROUP]
    video = info[0, GROUP + 1]
    is_video = block < video
    first = jnp.where(is_video, 0, video)
    seen = jnp.where(is_video, video, length - video)
    return block, first, jnp.where(block < 0, 0, seen)


def visit_blocks(info, places, query, keys, values, context):
    sights = [sight(info, place) for place in places]
    for counts in itertools.product(range(SLOT_DEV), repeat=len(places)):
        targets = [
            (i, block, first, count)
            for i, ((block, first, _), count) in enumerate(zip(sights, counts))
            if count
        ]
        if not targets:
            continue
        match = sights[0][2] == counts[0]
        for (_, _, seen), count in zip(sights[1:], counts[1:]):
            match = match & (seen == count)

        @pl.when(match)
        def _():
            token_blocks(query, keys, values, context, targets)


def attend_kernel(
    facts,
    gain,
    arrived,
    weights,
    own_query,
    own_keys,
    own_values,
    far,
    across,
    query,
    keys,
    values,
    normed,
    context,
    info,
    sems,
):
    load = pltpu.make_async_copy(facts, info, sems.at[0])
    load.start()
    width = query.shape[1]
    pairs = width // BLK
    context[...] = jnp.zeros_like(context)
    gains = gain[...]
    for k in range(GROUP - 1):
        rows = slice(k * BLK, (k + 1) * BLK)
        norm_into(arrived[0, rows, :], arrived[1, rows, :], gains, normed, k * BLK, BLK)
    load.wait()
    length = info[0, GROUP]
    row_at = []
    for place in range(GROUP):
        block = info[0, place]
        row_at.append(pl.multiple_of(jnp.where(block < 0, SLOT_DEV + 1, block) * BLK, BLK))

    last = GROUP - 1
    for own, out in ((own_query, query), (own_keys, keys)):
        out[pl.ds(row_at[last], BLK), :] = own[:BLK, :]
        out[CLIP_ROWS:END, :] = own[BLK:, :]
    for p in range(pairs):
        values[p, :BLK, pl.ds(row_at[last], BLK)] = own_values[p, :, :BLK]
        values[p, :BLK, CLIP_ROWS:END] = own_values[p, :, BLK:]
        values[p, BLK:, :END] = jnp.ones((PAD, END), BF16)
    tile = 256
    for which, out in ((0, query), (1, keys)):
        for j in range(0, width, tile):
            got = jnp.dot(normed[...], weights[which, :, j : j + tile], preferred_element_type=F32)
            if which == 0:
                got = got * HEAD_DIM ** (-0.5)
            got = got.astype(BF16)
            for place in range(last):
                out[pl.ds(row_at[place], BLK), j : j + tile] = got[place * BLK : (place + 1) * BLK]
    for j in range(0, width, tile):
        got = jnp.dot(normed[...], weights[2, :, j : j + tile], preferred_element_type=F32)
        for k in range(tile // BLK):
            p = j // BLK + k
            cols = slice(k * BLK, (k + 1) * BLK)
            for place in range(last):
                turned = got[place * BLK : (place + 1) * BLK, cols].T
                values[p, :BLK, pl.ds(row_at[place], BLK)] = turned.astype(BF16)
    for b in range(2, SLOT_DEV):

        @pl.when(b >= length)
        def _():
            values[:, :BLK, b * BLK : (b + 1) * BLK] = jnp.zeros((pairs, BLK, BLK), BF16)

    visit_blocks(info, (0, 2), query, keys, values, context)
    far[...] = context[0]
    across[...] = context[1]


def near_kernel(query, keys, values, facts, near, context, info, sems):
    load = pltpu.make_async_copy(facts, info, sems.at[0])
    load.start()
    context[...] = jnp.zeros_like(context)
    load.wait()
    visit_blocks(info, (1,), query, keys, values, context)
    near[...] = context[0]


def own_kernel(query, keys, values, facts, own, context, info, sems):
    load = pltpu.make_async_copy(facts, info, sems.at[0])
    load.start()
    width = query.shape[1]
    pairs = width // BLK
    context[...] = jnp.zeros_like(context)
    load.wait()
    length = info[0, GROUP]
    video = info[0, GROUP + 1]
    visit_blocks(info, (GROUP - 1,), query, keys, values, context)
    own[:BLK, :] = context[0]

    heads = width // HEAD_DIM
    sub = 8
    qe = query[CLIP_ROWS:END, :].astype(F32)[:sub]
    qe = jnp.concatenate([qe] * heads, axis=0)
    row_head = lax.broadcasted_iota(jnp.int32, (heads * sub, width), 0) // sub
    col_head = lax.broadcasted_iota(jnp.int32, (heads * sub, width), 1) // HEAD_DIM
    qe = jnp.where(row_head == col_head, qe, 0.0).astype(BF16)
    s = lax.dot_general(qe, keys[:END, :], NT, preferred_element_type=F32)
    col = lax.broadcasted_iota(jnp.int32, s.shape, 1)
    bottle = (col >= CLIP_ROWS) & (col < CLIP_ROWS + NB)
    parts = []
    for allowed in (
        bottle | (col < video * BLK),
        bottle | ((col >= video * BLK) & (col < length * BLK)),
    ):
        masked = jnp.where(allowed, s, -1e30)
        e = jnp.exp(masked - jnp.max(masked, axis=-1, keepdims=True))
        parts.append((e / jnp.sum(e, axis=-1, keepdims=True)).astype(BF16))
    first_head = lax.broadcasted_iota(jnp.int32, (sub, BLK), 1) < HEAD_DIM
    for p in range(pairs):
        rows = slice(2 * p * sub, (2 * p + 2) * sub)
        both = jnp.concatenate([parts[0][rows], parts[1][rows]], axis=0)
        o = lax.dot_general(both, values[p, :BLK, :END], NT, preferred_element_type=F32)
        o = 0.5 * (o[: 2 * sub] + o[2 * sub :])
        o = jnp.where(first_head, o[:sub], o[sub:])
        own[BLK:, p * BLK : (p + 1) * BLK] = jnp.concatenate([o, jnp.zeros_like(o)], axis=0).astype(BF16)


def feed_kernel(
    store_map,
    stored,
    own,
    arrived,
    w_out,
    w_out_other,
    gain,
    w_up,
    w_down,
    base,
    send,
    context,
    after,
    normed,
    active,
):
    member = lax.axis_index("clip")
    core = lax.axis_index("mp")
    half = base.shape[1]
    hidden = w_up.shape[1]
    sides = (core, 1 - core)
    kept = [
        (slice(s * BLK, (s + 1) * BLK), store_map[s, member] >= 0) for s in range(STORE_DEV)
    ] + [(slice(STORED, ROWS), True)]
    for s in range(STORE_DEV):
        entry = store_map[s, member]
        step = jnp.where(entry >= 0, (entry // SLOT_DEV) ^ member, -1)
        at = jnp.where(step == STEPS[0], 0, jnp.where(step == STEPS[1], 1, 2))
        at = pl.multiple_of(at * BLK, BLK)
        rows = slice(s * BLK, (s + 1) * BLK)
        mine = jnp.full((BLK, half), step, jnp.int32) == 0
        for k in range(2):
            context[k, rows, :] = jnp.where(
                mine, own[sides[k], :BLK, :], arrived[sides[k], pl.ds(at, BLK), :]
            )
    for k in range(2):
        context[k, STORED:, :] = own[sides[k], BLK:, :]

    tile = 512
    gains = gain[...]
    halves = (slice(0, 208), slice(208, ROWS))
    for rows in halves:
        for side in range(2):
            cols = slice(side * half, (side + 1) * half)
            got = jnp.dot(context[0, rows, :], w_out[:, cols], preferred_element_type=F32)
            got = got + jnp.dot(context[1, rows, :], w_out_other[:, cols], preferred_element_type=F32)
            after[rows, cols] = (got + stored[side, rows, :].astype(F32)).astype(BF16)
    for rows in halves:
        norm_into(
            after[rows, :half], after[rows, half:], gains, normed, rows.start, rows.stop - rows.start
        )
        for j in range(0, hidden, tile):
            got = jnp.dot(normed[rows, :], w_up[:, j : j + tile], preferred_element_type=F32)
            active[rows, j : j + tile] = jax.nn.gelu(got, approximate=True).astype(BF16)
    other = pl.multiple_of((1 - core) * half, half)
    got = jnp.dot(active[...], w_down[:, pl.ds(other, half)], preferred_element_type=F32)
    for rows, keep in kept:
        send[rows, :] = jnp.where(keep, got[rows], 0.0).astype(BF16)
    mine = pl.multiple_of(core * half, half)
    got = jnp.dot(active[...], w_down[:, pl.ds(mine, half)], preferred_element_type=F32)
    got = got + after[:, pl.ds(mine, half)].astype(F32)
    for rows, keep in kept:
        base[rows, :] = jnp.where(keep, got[rows], 0.0)


def finish_kernel(base, sums, mixed, merged):
    other = 1 - lax.axis_index("mp")
    for s in range(STORE_DEV):
        rows = slice(s * BLK, (s + 1) * BLK)
        mixed[s] = (base[rows, :] + sums[other, rows, :].astype(F32)).astype(BF16)
    got = base[STORED:, :] + sums[other, STORED:, :].astype(F32)
    merged[0] = got[:NB].astype(BF16)


def stay(x):
    return pltpu.with_memory_space_constraint(x, pltpu.HBM)


def ready(slots, clip_lengths, video_blocks, gain1, w_qkv, stored_all):
    model = w_qkv.shape[1]
    width = w_qkv.shape[2]
    pairs = width // BLK
    info = (1, 2 * GROUP)
    return pl.pallas_call(
        ready_kernel,
        name="ready",
        out_shape=(
            spec(w_qkv.shape),
            spec((BLK + PAD, width)),
            spec((BLK + PAD, width)),
            spec((pairs, BLK, BLK + PAD)),
            spec((1, model), F32),
            spec(info, jnp.int32),
        ),
        in_specs=[HBM] * 5 + [VMEM],
        out_specs=(VMEM,) * 6,
        scratch_shapes=[
            pltpu.VMEM((BLK + PAD, model), BF16),
            pltpu.SMEM(info, jnp.int32),
            pltpu.SMEM(slots.shape, jnp.int32),
            pltpu.SMEM(clip_lengths.shape, jnp.int32),
            pltpu.SMEM(video_blocks.shape, jnp.int32),
            DMA((8,)),
        ],
        compiler_params=pltpu.CompilerParams(vmem_limit_bytes=8 << 20),
        cost_estimate=pl.CostEstimate(flops=450000000, bytes_accessed=4000000, transcendentals=0),
    )(stay(slots), stay(clip_lengths), stay(video_blocks), stay(gain1), stay(w_qkv), stored_all)


def attend(facts, gain, arrived, weights, own_qkv):
    model = weights.shape[1]
    width = weights.shape[2]
    pairs = width // BLK
    rows = CLIP_ROWS + 2 * BLK
    block = spec((BLK, width))
    return pl.pallas_call(
        attend_kernel,
        name="attend",
        out_shape=(
            block,
            block,
            spec((rows, width)),
            spec((rows, width)),
            spec((pairs, BLK + PAD, rows)),
        ),
        in_specs=[VMEM] * 7,
        out_specs=(VMEM,) * 5,
        scratch_shapes=[
            pltpu.VMEM(((GROUP - 1) * BLK, model), BF16),
            pltpu.VMEM((2, BLK, width), BF16),
            pltpu.SMEM(facts.shape, jnp.int32),
            DMA((1,)),
        ],
        compiler_params=pltpu.CompilerParams(vmem_limit_bytes=16 << 20),
        cost_estimate=pl.CostEstimate(flops=1800000000, bytes_accessed=6000000, transcendentals=1500000),
    )(facts, gain, arrived, weights, *own_qkv)


def part(kernel, name, rows, query, keys, values, facts):
    width = query.shape[1]
    return pl.pallas_call(
        kernel,
        name=name,
        out_shape=spec((rows, width)),
        in_specs=[VMEM] * 4,
        out_specs=VMEM,
        scratch_shapes=[
            pltpu.VMEM((1, BLK, width), BF16),
            pltpu.SMEM(facts.shape, jnp.int32),
            DMA((1,)),
        ],
        compiler_params=pltpu.CompilerParams(vmem_limit_bytes=16 << 20),
        cost_estimate=pl.CostEstimate(flops=400000000, bytes_accessed=3000000, transcendentals=700000),
    )(query, keys, values, facts)


def feed(slots, stored_all, own_all, arrived, w_out, w_out_other, gain2, w_up, w_down):
    width = stored_all.shape[2]
    model = 2 * width
    hidden = w_up.shape[1]
    return pl.pallas_call(
        feed_kernel,
        name="feed",
        out_shape=(spec((ROWS, width), F32), spec((ROWS, width))),
        in_specs=[SMEM] + [VMEM] * 8,
        out_specs=(VMEM,) * 2,
        scratch_shapes=[
            pltpu.VMEM((2, ROWS, width), BF16),
            pltpu.VMEM((ROWS, model), BF16),
            pltpu.VMEM((ROWS, model), BF16),
            pltpu.VMEM((ROWS, hidden), BF16),
        ],
        compiler_params=pltpu.CompilerParams(vmem_limit_bytes=16 << 20),
        cost_estimate=pl.CostEstimate(flops=4100000000, bytes_accessed=14000000, transcendentals=820000),
    )(slots, stored_all, own_all, arrived, w_out, w_out_other, gain2, w_up, w_down)


def body(
    tokens,
    bottleneck,
    clip_lengths,
    video_blocks,
    store_map,
    norm1_gain,
    w_qkv,
    w_out,
    norm2_gain,
    w_up,
    w_down,
):
    width = tokens.shape[2]
    model = 2 * width
    gain1 = norm1_gain.reshape(1, model)
    gain2 = norm2_gain.reshape(1, model)
    block = spec((BLK, width))
    slots = store_map.T

    far, near, across, stored = pl.pallas_call(
        pack_kernel,
        name="pack",
        out_shape=(block, block, block, spec((ROWS, width))),
        in_specs=[HBM, HBM, HBM],
        out_specs=(VMEM,) * 4,
        scratch_shapes=[
            pltpu.SMEM(slots.shape, jnp.int32),
            pltpu.VMEM(tokens.shape, BF16),
            pltpu.VMEM(bottleneck.shape, BF16),
            DMA((3,)),
        ],
        compiler_params=pltpu.CompilerParams(vmem_limit_bytes=4 << 20),
    )(stay(slots), stay(tokens), stay(bottleneck))
    far = partner(far, 2)
    near = partner(near, 1)
    across = partner(across, 3)
    stored_all = lax.all_gather(stored, "mp", axis=0)
    stored_all, w_out_late = lax.optimization_barrier((stored_all, w_out))
    w_out_other = lax.ppermute(w_out_late, "mp", [(0, 1), (1, 0)])
    weights, *own_qkv, gain, facts = ready(
        slots, clip_lengths, video_blocks, gain1, w_qkv, stored_all
    )
    arrived = lax.all_gather(jnp.concatenate([far, near, across], axis=0), "mp", axis=0)

    far, across, query, keys, values = attend(facts, gain, arrived, weights, own_qkv)
    far = partner(far, 2)
    across = partner(across, 3)
    near = part(near_kernel, "near", BLK, query, keys, values, facts)
    near = partner(near, 1)
    own = part(own_kernel, "own", BLK + PAD, query, keys, values, facts)
    own, far = lax.optimization_barrier((own, far))
    own_all = lax.all_gather(own, "mp", axis=0)
    arrived = lax.all_gather(jnp.concatenate([far, near, across], axis=0), "mp", axis=0)

    base, send = feed(
        slots, stored_all, own_all, arrived, w_out, w_out_other, gain2, w_up, w_down
    )
    sums = lax.all_gather(send, "mp", axis=0)

    mixed, merged = pl.pallas_call(
        finish_kernel,
        name="finish",
        out_shape=(spec(tokens.shape), spec(bottleneck.shape)),
        in_specs=[VMEM, VMEM],
        out_specs=(VMEM,) * 2,
        compiler_params=pltpu.CompilerParams(vmem_limit_bytes=8 << 20),
    )(base, sums)
    return mixed, merged


def solution(mesh):
    placed = (
        P("clip", None, "mp"),
        P("clip", None, "mp"),
        P(),
        P(),
        P(),
        P(),
        P(None, None, "mp"),
        P("mp", None),
        P(),
        P(None, "mp"),
        P("mp", None),
    )
    return jax.shard_map(
        body,
        mesh=mesh,
        in_specs=placed,
        out_specs=(P("clip", None, "mp"), P("clip", None, "mp")),
        check_vma=False,
    )
```

```python
import jax
import jax.numpy as jnp
from jax import lax
from jax.experimental import pallas as pl
from jax.experimental.pallas import tpu as pltpu
from jax.sharding import PartitionSpec as P

HEAD_DIM = 64
BLK = 128
NB = 4
SLOT_DEV = 4
STORE_DEV = 3
GROUP = 4
PAD = 16
STORED = STORE_DEV * BLK
ROWS = STORED + PAD
CLIP_ROWS = SLOT_DEV * BLK
STEPS = (2, 1, 3)
BACK = (2, 3, 1)
BF16 = jnp.bfloat16
F32 = jnp.float32

VMEM = pl.BlockSpec(memory_space=pltpu.VMEM)
HBM = pl.BlockSpec(memory_space=pltpu.HBM)
DMA = pltpu.SemaphoreType.DMA
SMEM = pl.BlockSpec(memory_space=pltpu.SMEM)


def spec(shape, dtype=BF16):
    return jax.ShapeDtypeStruct(shape, dtype)


def partner(x, step):
    return lax.ppermute(x, "clip", [(i, i ^ step) for i in range(lax.axis_size("clip"))])


def slot_for(store_map, device, owner):
    slot = jnp.int32(-1)
    block = jnp.int32(-1)
    for s in range(STORE_DEV):
        entry = store_map[s, device]
        hit = (entry >= 0) & (entry // SLOT_DEV == owner)
        slot = jnp.where(hit, s, slot)
        block = jnp.where(hit, entry % SLOT_DEV, block)
    return slot, block


def norm_into(x0, x1, gain, out, at, rows):
    half = x0.shape[1]
    x0 = x0.astype(F32)
    x1 = x1.astype(F32)
    scale = 1.0 / (2 * half)
    mean = (jnp.sum(x0, axis=-1, keepdims=True) + jnp.sum(x1, axis=-1, keepdims=True)) * scale
    x0 = x0 - mean
    x1 = x1 - mean
    moment = (
        jnp.sum(x0 * x0, axis=-1, keepdims=True) + jnp.sum(x1 * x1, axis=-1, keepdims=True)
    ) * scale
    inv = lax.rsqrt(moment + 1e-05)
    out[pl.ds(at, rows), :half] = (x0 * inv * gain[:, :half]).astype(BF16)
    out[pl.ds(at, rows), half:] = (x1 * inv * gain[:, half:]).astype(BF16)


def pack_kernel(slots, tokens, extra, far, near, across, stored, store_map, blocks, few, sems):
    member = lax.axis_index("clip")
    loads = [
        pltpu.make_async_copy(x, y, sems.at[i])
        for i, (x, y) in enumerate(((slots, store_map), (tokens, blocks), (extra, few)))
    ]
    for load in loads:
        load.start()
    for load in loads:
        load.wait()
    for step, out in zip(STEPS, (far, near, across)):
        slot, _ = slot_for(store_map, member, member ^ step)
        out[...] = blocks[jnp.maximum(slot, 0)]
    for s in range(STORE_DEV):
        stored[s * BLK : (s + 1) * BLK, :] = blocks[s]
    width = stored.shape[1]
    stored[STORED:, :] = jnp.concatenate(
        [few[0].astype(F32), jnp.zeros((PAD - NB, width), F32)], axis=0
    ).astype(BF16)


def ready_kernel(
    slots,
    all_lengths,
    all_videos,
    gain_in,
    w_qkv,
    stored,
    weights,
    query,
    keys,
    values,
    gain,
    facts,
    normed,
    info,
    store_map,
    lengths,
    videos,
    sems,
):
    member = lax.axis_index("clip")
    small = [
        pltpu.make_async_copy(x, y, sems.at[i])
        for i, (x, y) in enumerate(
            ((gain_in, gain), (slots, store_map), (all_lengths, lengths), (all_videos, videos))
        )
    ]
    loads = [pltpu.make_async_copy(w_qkv.at[i], weights.at[i], sems.at[5 + i]) for i in range(3)]
    for load in small + loads:
        load.start()
    small[0].wait()
    gains = gain[...]
    norm_into(stored[0, STORED:, :], stored[1, STORED:, :], gains, normed, BLK, PAD)
    for load in small[1:]:
        load.wait()
    slot, block = slot_for(store_map, member, member)
    for place, step in enumerate(STEPS):
        info[0, place] = slot_for(store_map, member ^ step, member)[1]
    info[0, GROUP - 1] = block
    info[0, GROUP] = lengths[member]
    info[0, GROUP + 1] = videos[member]
    keep = pltpu.make_async_copy(info, facts, sems.at[4])
    keep.start()
    here = pl.multiple_of(jnp.maximum(slot, 0) * BLK, BLK)
    norm_into(
        stored[0, pl.ds(here, BLK), :], stored[1, pl.ds(here, BLK), :], gains, normed, 0, BLK
    )
    width = query.shape[1]
    tile = 256
    for which, out in ((0, query), (1, keys)):
        loads[which].wait()
        for j in range(0, width, tile):
            got = jnp.dot(normed[...], weights[which, :, j : j + tile], preferred_element_type=F32)
            if which == 0:
                got = got * HEAD_DIM ** (-0.5)
            out[:, j : j + tile] = got.astype(BF16)
    loads[2].wait()
    for j in range(0, width, tile):
        got = jnp.dot(normed[...], weights[2, :, j : j + tile], preferred_element_type=F32)
        for k in range(tile // BLK):
            p = j // BLK + k
            cols = slice(k * BLK, (k + 1) * BLK)
            values[p, :, :BLK] = got[:BLK, cols].T.astype(BF16)
            values[p, :, BLK:] = got[BLK:, cols].T.astype(BF16)
    keep.wait()


NT = (((1,), (1,)), ((), ()))
END = CLIP_ROWS + PAD


def token_blocks(query, keys, values, context, targets, count):
    pairs = values.shape[0]
    low = lax.broadcasted_iota(jnp.int32, (BLK, BLK), 1) < HEAD_DIM
    real = lax.broadcasted_iota(jnp.int32, (PAD, 2 * BLK), 0) < NB
    seen = count * BLK
    chains = [(place, block, first, p) for p in range(pairs) for place, block, first in targets]
    scores = []
    for place, block, first, p in chains:
        cols = slice(p * BLK, (p + 1) * BLK)
        start = pl.multiple_of(first * BLK, BLK)
        q = query[pl.ds(pl.multiple_of(block * BLK, BLK), BLK), cols]
        none = jnp.zeros_like(q)
        both = jnp.concatenate([jnp.where(low, q, none), jnp.where(low, none, q)], axis=0)
        k = jnp.concatenate([keys[pl.ds(start, seen), cols], keys[CLIP_ROWS:END, cols]], axis=0)
        s = lax.dot_general(k, both, NT, preferred_element_type=F32)
        scores.append((s[:seen], jnp.where(real, s[seen:], -1e30)))
    parts = []
    for s, se in scores:
        top = jnp.maximum(jnp.max(s, axis=0, keepdims=True), jnp.max(se, axis=0, keepdims=True))
        parts.append(
            jnp.concatenate([jnp.exp(s - top).astype(BF16), jnp.exp(se - top).astype(BF16)], axis=0)
        )
    sums = []
    for (place, block, first, p), part in zip(chains, parts):
        start = pl.multiple_of(first * BLK, BLK)
        v = jnp.concatenate([values[p, :, pl.ds(start, seen)], values[p, :, CLIP_ROWS:END]], axis=1)
        sums.append(jnp.dot(v, part, preferred_element_type=F32))
    for (place, block, first, p), o in zip(chains, sums):
        total = o[BLK : BLK + 1]
        o = jnp.concatenate(
            [o[:HEAD_DIM, :BLK] / total[:, :BLK], o[HEAD_DIM:BLK, BLK:] / total[:, BLK:]], axis=0
        )
        context[place, :, p * BLK : (p + 1) * BLK] = o.T.astype(BF16)


def sight(info, place):
    block = info[0, place]
    length = info[0, GROUP]
    video = info[0, GROUP + 1]
    is_video = block < video
    first = jnp.where(is_video, 0, video)
    seen = jnp.where(is_video, video, length - video)
    return block, first, jnp.where(block < 0, 0, seen)


def visit_blocks(info, places, query, keys, values, context):
    sights = [sight(info, place) for place in places]
    if len(places) == 2:
        alike = sights[0][2] == sights[1][2]
        for count in range(1, SLOT_DEV):

            @pl.when(alike & (sights[0][2] == count))
            def _():
                targets = [(i, block, first) for i, (block, first, _) in enumerate(sights)]
                token_blocks(query, keys, values, context, targets, count)

    else:
        alike = False

    def visit(i, carry):
        block, first, seen = sight(info, places[0] + i * (places[-1] - places[0]))
        for count in range(1, SLOT_DEV):

            @pl.when(jnp.logical_not(alike) & (seen == count))
            def _():
                token_blocks(query, keys, values, context, [(i, block, first)], count)

        return carry

    lax.fori_loop(0, len(places), visit, 0)


def attend_kernel(
    facts,
    gain,
    arrived,
    weights,
    own_query,
    own_keys,
    own_values,
    far,
    across,
    query,
    keys,
    values,
    normed,
    context,
    info,
    sems,
):
    load = pltpu.make_async_copy(facts, info, sems.at[0])
    load.start()
    width = query.shape[1]
    pairs = width // BLK
    context[...] = jnp.zeros_like(context)
    gains = gain[...]
    for k in range(GROUP - 1):
        rows = slice(k * BLK, (k + 1) * BLK)
        norm_into(arrived[0, rows, :], arrived[1, rows, :], gains, normed, k * BLK, BLK)
    load.wait()
    length = info[0, GROUP]
    row_at = []
    for place in range(GROUP):
        block = info[0, place]
        row_at.append(pl.multiple_of(jnp.where(block < 0, SLOT_DEV + 1, block) * BLK, BLK))

    last = GROUP - 1
    for own, out in ((own_query, query), (own_keys, keys)):
        out[pl.ds(row_at[last], BLK), :] = own[:BLK, :]
        out[CLIP_ROWS:END, :] = own[BLK:, :]
    for p in range(pairs):
        values[p, :BLK, pl.ds(row_at[last], BLK)] = own_values[p, :, :BLK]
        values[p, :BLK, CLIP_ROWS:END] = own_values[p, :, BLK:]
        values[p, BLK:, :END] = jnp.ones((PAD, END), BF16)
    tile = 256
    for which, out in ((0, query), (1, keys)):
        for j in range(0, width, tile):
            got = jnp.dot(normed[...], weights[which, :, j : j + tile], preferred_element_type=F32)
            if which == 0:
                got = got * HEAD_DIM ** (-0.5)
            got = got.astype(BF16)
            for place in range(last):
                out[pl.ds(row_at[place], BLK), j : j + tile] = got[place * BLK : (place + 1) * BLK]
    for j in range(0, width, tile):
        got = jnp.dot(normed[...], weights[2, :, j : j + tile], preferred_element_type=F32)
        for k in range(tile // BLK):
            p = j // BLK + k
            cols = slice(k * BLK, (k + 1) * BLK)
            for place in range(last):
                turned = got[place * BLK : (place + 1) * BLK, cols].T
                values[p, :BLK, pl.ds(row_at[place], BLK)] = turned.astype(BF16)
    for b in range(2, SLOT_DEV):

        @pl.when(b >= length)
        def _():
            values[:, :BLK, b * BLK : (b + 1) * BLK] = jnp.zeros((pairs, BLK, BLK), BF16)

    visit_blocks(info, (0, 2), query, keys, values, context)
    far[...] = context[0]
    across[...] = context[1]


def near_kernel(query, keys, values, facts, near, context, info, sems):
    load = pltpu.make_async_copy(facts, info, sems.at[0])
    load.start()
    context[...] = jnp.zeros_like(context)
    load.wait()
    visit_blocks(info, (1,), query, keys, values, context)
    near[...] = context[0]


def own_kernel(query, keys, values, facts, own, context, info, sems):
    load = pltpu.make_async_copy(facts, info, sems.at[0])
    load.start()
    width = query.shape[1]
    pairs = width // BLK
    context[...] = jnp.zeros_like(context)
    load.wait()
    length = info[0, GROUP]
    video = info[0, GROUP + 1]
    visit_blocks(info, (GROUP - 1,), query, keys, values, context)
    own[:BLK, :] = context[0]

    heads = width // HEAD_DIM
    sub = 8
    qe = query[CLIP_ROWS:END, :].astype(F32)[:sub]
    qe = jnp.concatenate([qe] * heads, axis=0)
    row_head = lax.broadcasted_iota(jnp.int32, (heads * sub, width), 0) // sub
    col_head = lax.broadcasted_iota(jnp.int32, (heads * sub, width), 1) // HEAD_DIM
    qe = jnp.where(row_head == col_head, qe, 0.0).astype(BF16)
    s = lax.dot_general(qe, keys[:END, :], NT, preferred_element_type=F32)
    col = lax.broadcasted_iota(jnp.int32, s.shape, 1)
    bottle = (col >= CLIP_ROWS) & (col < CLIP_ROWS + NB)
    parts = []
    for allowed in (
        bottle | (col < video * BLK),
        bottle | ((col >= video * BLK) & (col < length * BLK)),
    ):
        masked = jnp.where(allowed, s, -1e30)
        e = jnp.exp(masked - jnp.max(masked, axis=-1, keepdims=True))
        parts.append((e / jnp.sum(e, axis=-1, keepdims=True)).astype(BF16))
    first_head = lax.broadcasted_iota(jnp.int32, (sub, BLK), 1) < HEAD_DIM
    for p in range(pairs):
        rows = slice(2 * p * sub, (2 * p + 2) * sub)
        both = jnp.concatenate([parts[0][rows], parts[1][rows]], axis=0)
        o = lax.dot_general(both, values[p, :BLK, :END], NT, preferred_element_type=F32)
        o = 0.5 * (o[: 2 * sub] + o[2 * sub :])
        o = jnp.where(first_head, o[:sub], o[sub:])
        own[BLK:, p * BLK : (p + 1) * BLK] = jnp.concatenate([o, jnp.zeros_like(o)], axis=0).astype(BF16)


def feed_kernel(
    store_map,
    stored,
    own,
    arrived,
    w_out,
    w_out_other,
    gain,
    w_up,
    w_down,
    base,
    send,
    context,
    after,
    normed,
    active,
):
    member = lax.axis_index("clip")
    core = lax.axis_index("mp")
    half = base.shape[1]
    hidden = w_up.shape[1]
    sides = (core, 1 - core)
    kept = [
        (slice(s * BLK, (s + 1) * BLK), store_map[s, member] >= 0) for s in range(STORE_DEV)
    ] + [(slice(STORED, ROWS), True)]
    for s in range(STORE_DEV):
        entry = store_map[s, member]
        step = jnp.where(entry >= 0, (entry // SLOT_DEV) ^ member, -1)
        at = jnp.where(step == BACK[0], 0, jnp.where(step == BACK[1], 1, 2))
        at = pl.multiple_of(at * BLK, BLK)
        rows = slice(s * BLK, (s + 1) * BLK)
        mine = jnp.full((BLK, half), step, jnp.int32) == 0
        for k in range(2):
            context[k, rows, :] = jnp.where(
                mine, own[sides[k], :BLK, :], arrived[sides[k], pl.ds(at, BLK), :]
            )
    for k in range(2):
        context[k, STORED:, :] = own[sides[k], BLK:, :]

    tile = 512
    gains = gain[...]
    halves = (slice(0, 208), slice(208, ROWS))
    for rows in halves:
        for side in range(2):
            cols = slice(side * half, (side + 1) * half)
            got = jnp.dot(context[0, rows, :], w_out[:, cols], preferred_element_type=F32)
            got = got + jnp.dot(context[1, rows, :], w_out_other[:, cols], preferred_element_type=F32)
            after[rows, cols] = (got + stored[side, rows, :].astype(F32)).astype(BF16)
    for rows in halves:
        norm_into(
            after[rows, :half], after[rows, half:], gains, normed, rows.start, rows.stop - rows.start
        )
        for j in range(0, hidden, tile):
            got = jnp.dot(normed[rows, :], w_up[:, j : j + tile], preferred_element_type=F32)
            active[rows, j : j + tile] = jax.nn.gelu(got, approximate=True).astype(BF16)
    other = pl.multiple_of((1 - core) * half, half)
    got = jnp.dot(active[...], w_down[:, pl.ds(other, half)], preferred_element_type=F32)
    for rows, keep in kept:
        send[rows, :] = jnp.where(keep, got[rows], 0.0).astype(BF16)
    mine = pl.multiple_of(core * half, half)
    got = jnp.dot(active[...], w_down[:, pl.ds(mine, half)], preferred_element_type=F32)
    got = got + after[:, pl.ds(mine, half)].astype(F32)
    for rows, keep in kept:
        base[rows, :] = jnp.where(keep, got[rows], 0.0)


def finish_kernel(base, sums, mixed, merged):
    other = 1 - lax.axis_index("mp")
    for s in range(STORE_DEV):
        rows = slice(s * BLK, (s + 1) * BLK)
        mixed[s] = (base[rows, :] + sums[other, rows, :].astype(F32)).astype(BF16)
    got = base[STORED:, :] + sums[other, STORED:, :].astype(F32)
    merged[0] = got[:NB].astype(BF16)


def stay(x):
    return pltpu.with_memory_space_constraint(x, pltpu.HBM)


def ready(slots, clip_lengths, video_blocks, gain1, w_qkv, stored_all):
    model = w_qkv.shape[1]
    width = w_qkv.shape[2]
    pairs = width // BLK
    info = (1, 2 * GROUP)
    return pl.pallas_call(
        ready_kernel,
        name="ready",
        out_shape=(
            spec(w_qkv.shape),
            spec((BLK + PAD, width)),
            spec((BLK + PAD, width)),
            spec((pairs, BLK, BLK + PAD)),
            spec((1, model), F32),
            spec(info, jnp.int32),
        ),
        in_specs=[HBM] * 5 + [VMEM],
        out_specs=(VMEM,) * 6,
        scratch_shapes=[
            pltpu.VMEM((BLK + PAD, model), BF16),
            pltpu.SMEM(info, jnp.int32),
            pltpu.SMEM(slots.shape, jnp.int32),
            pltpu.SMEM(clip_lengths.shape, jnp.int32),
            pltpu.SMEM(video_blocks.shape, jnp.int32),
            DMA((8,)),
        ],
        compiler_params=pltpu.CompilerParams(vmem_limit_bytes=8 << 20),
        cost_estimate=pl.CostEstimate(flops=450000000, bytes_accessed=4000000, transcendentals=0),
    )(stay(slots), stay(clip_lengths), stay(video_blocks), stay(gain1), stay(w_qkv), stored_all)


def attend(facts, gain, arrived, weights, own_qkv):
    model = weights.shape[1]
    width = weights.shape[2]
    pairs = width // BLK
    rows = CLIP_ROWS + 2 * BLK
    block = spec((BLK, width))
    return pl.pallas_call(
        attend_kernel,
        name="attend",
        out_shape=(
            block,
            block,
            spec((rows, width)),
            spec((rows, width)),
            spec((pairs, BLK + PAD, rows)),
        ),
        in_specs=[VMEM] * 7,
        out_specs=(VMEM,) * 5,
        scratch_shapes=[
            pltpu.VMEM(((GROUP - 1) * BLK, model), BF16),
            pltpu.VMEM((2, BLK, width), BF16),
            pltpu.SMEM(facts.shape, jnp.int32),
            DMA((1,)),
        ],
        compiler_params=pltpu.CompilerParams(vmem_limit_bytes=16 << 20),
        cost_estimate=pl.CostEstimate(flops=1800000000, bytes_accessed=6000000, transcendentals=1500000),
    )(facts, gain, arrived, weights, *own_qkv)


def part(kernel, name, rows, query, keys, values, facts):
    width = query.shape[1]
    return pl.pallas_call(
        kernel,
        name=name,
        out_shape=spec((rows, width)),
        in_specs=[VMEM] * 4,
        out_specs=VMEM,
        scratch_shapes=[
            pltpu.VMEM((1, BLK, width), BF16),
            pltpu.SMEM(facts.shape, jnp.int32),
            DMA((1,)),
        ],
        compiler_params=pltpu.CompilerParams(vmem_limit_bytes=16 << 20),
        cost_estimate=pl.CostEstimate(flops=400000000, bytes_accessed=3000000, transcendentals=700000),
    )(query, keys, values, facts)


def feed(slots, stored_all, own_all, arrived, w_out, w_out_other, gain2, w_up, w_down):
    width = stored_all.shape[2]
    model = 2 * width
    hidden = w_up.shape[1]
    return pl.pallas_call(
        feed_kernel,
        name="feed",
        out_shape=(spec((ROWS, width), F32), spec((ROWS, width))),
        in_specs=[SMEM] + [VMEM] * 8,
        out_specs=(VMEM,) * 2,
        scratch_shapes=[
            pltpu.VMEM((2, ROWS, width), BF16),
            pltpu.VMEM((ROWS, model), BF16),
            pltpu.VMEM((ROWS, model), BF16),
            pltpu.VMEM((ROWS, hidden), BF16),
        ],
        compiler_params=pltpu.CompilerParams(vmem_limit_bytes=16 << 20),
        cost_estimate=pl.CostEstimate(flops=4100000000, bytes_accessed=14000000, transcendentals=820000),
    )(slots, stored_all, own_all, arrived, w_out, w_out_other, gain2, w_up, w_down)


def body(
    tokens,
    bottleneck,
    clip_lengths,
    video_blocks,
    store_map,
    norm1_gain,
    w_qkv,
    w_out,
    norm2_gain,
    w_up,
    w_down,
):
    width = tokens.shape[2]
    model = 2 * width
    gain1 = norm1_gain.reshape(1, model)
    gain2 = norm2_gain.reshape(1, model)
    block = spec((BLK, width))
    slots = store_map.T

    far, near, across, stored = pl.pallas_call(
        pack_kernel,
        name="pack",
        out_shape=(block, block, block, spec((ROWS, width))),
        in_specs=[HBM, HBM, HBM],
        out_specs=(VMEM,) * 4,
        scratch_shapes=[
            pltpu.SMEM(slots.shape, jnp.int32),
            pltpu.VMEM(tokens.shape, BF16),
            pltpu.VMEM(bottleneck.shape, BF16),
            DMA((3,)),
        ],
        compiler_params=pltpu.CompilerParams(vmem_limit_bytes=4 << 20),
    )(stay(slots), stay(tokens), stay(bottleneck))
    far = partner(far, 2)
    near = partner(near, 1)
    across = partner(across, 3)
    stored_all = lax.all_gather(stored, "mp", axis=0)
    stored_all, w_out_late = lax.optimization_barrier((stored_all, w_out))
    w_out_other = lax.ppermute(w_out_late, "mp", [(0, 1), (1, 0)])
    weights, *own_qkv, gain, facts = ready(
        slots, clip_lengths, video_blocks, gain1, w_qkv, stored_all
    )
    arrived = lax.all_gather(jnp.concatenate([far, near, across], axis=0), "mp", axis=0)

    far, across, query, keys, values = attend(facts, gain, arrived, weights, own_qkv)
    far = partner(far, 2)
    near = part(near_kernel, "near", BLK, query, keys, values, facts)
    across, near = lax.optimization_barrier((across, near))
    across = partner(across, 3)
    near = partner(near, 1)
    own = part(own_kernel, "own", BLK + PAD, query, keys, values, facts)
    own, far = lax.optimization_barrier((own, far))
    own_all = lax.all_gather(own, "mp", axis=0)
    arrived = lax.all_gather(jnp.concatenate([far, across, near], axis=0), "mp", axis=0)

    base, send = feed(
        slots, stored_all, own_all, arrived, w_out, w_out_other, gain2, w_up, w_down
    )
    sums = lax.all_gather(send, "mp", axis=0)

    mixed, merged = pl.pallas_call(
        finish_kernel,
        name="finish",
        out_shape=(spec(tokens.shape), spec(bottleneck.shape)),
        in_specs=[VMEM, VMEM],
        out_specs=(VMEM,) * 2,
        compiler_params=pltpu.CompilerParams(vmem_limit_bytes=8 << 20),
    )(base, sums)
    return mixed, merged


def solution(mesh):
    placed = (
        P("clip", None, "mp"),
        P("clip", None, "mp"),
        P(),
        P(),
        P(),
        P(),
        P(None, None, "mp"),
        P("mp", None),
        P(),
        P(None, "mp"),
        P("mp", None),
    )
    return jax.shard_map(
        body,
        mesh=mesh,
        in_specs=placed,
        out_specs=(P("clip", None, "mp"), P("clip", None, "mp")),
        check_vma=False,
    )
```
